32 devices in a mesh: groups: 2 (over y), seq: 4 (over z), tp: 2 (over x), dp: 2 (over core).
Axes of the slice: x: 2, y: 2, z: 4, core: 2. Of those that a mesh axis runs over, the one named last changes fastest.
Arguments:
- x_in: bfloat16 [2048, 8192], P(('groups', 'seq'), ('tp', 'dp')), parts along dimension 0, may hold values from -6 to 6
- z_gate: bfloat16 [2048, 8192], P(('groups', 'seq'), ('tp', 'dp')), parts along dimension 0, may hold values from -6 to 6
- b_in: bfloat16 [2048, 2048], P(('groups', 'seq'), 'tp'), parts along dimension 0, may hold values from -0.375 to 0.375
- c_in: bfloat16 [2048, 2048], P(('groups', 'seq'), 'tp'), parts along dimension 0, may hold values from -0.375 to 0.375
- dt_raw: float32 [2048, 128], P(('groups', 'seq'), ('tp', 'dp')), parts along dimension 0, may hold values from -3 to 3
- dt_bias: float32 [128], P(('tp', 'dp')), may hold values from -0.5 to 0.5
- a_log: float32 [128], P(('tp', 'dp')), may hold values from -20 to 0
- d_skip: float32 [128], P(('tp', 'dp')), may hold values from 0.5 to 2
- norm_weight: float32 [8192], P(('tp', 'dp')), may hold values from 0.5 to 1.5
- ssm_init: float32 [256, 64, 256], P(('groups', 'tp', 'dp')), parts along dimension 0, may hold values from -6 to 6
- queries: bfloat16 [2048, 8192], P(('groups', 'seq'), ('tp', 'dp')), parts along dimension 0, may hold values from -6 to 6
- keys: bfloat16 [2048, 1024], P(('groups', 'seq'), 'tp'), parts along dimension 0, may hold values from -6 to 6
- values: bfloat16 [2048, 1024], P(('groups', 'seq'), 'tp'), parts along dimension 0, may hold values from -6 to 6
- cache_keys: bfloat16 [8192, 1024], P(('groups', 'dp'), 'tp'), parts along dimension 0, may hold values from -6 to 6
- cache_values: bfloat16 [8192, 1024], P(('groups', 'dp'), 'tp'), parts along dimension 0, may hold values from -6 to 6
- window_start: int32 [2], P('groups'), parts along dimension 0, may hold values from 4096 to 1047551
- prefix_len: int32 [2], P('groups'), parts along dimension 0, may hold values from 1024 to 4096
Outputs:
- mamba_out: bfloat16 [2048, 8192], P(('groups', 'seq'), ('tp', 'dp')), parts along dimension 0
- attention_out: bfloat16 [2048, 8192], P(('groups', 'seq'), ('tp', 'dp')), parts along dimension 0
The draws below stay inside these ranges and needn't reach their ends.
There are 2 independent parts, one for each index of `groups`. The reference program is written for one: setup_inputs(seed, part) draws one part's arguments, and reference() takes and returns one part's arrays. A program takes and returns all parts, laid end to end along the dimension named above; an argument that names none is the same for every part. Nothing has to cross between parts.
Inputs may be any that keep to these rules, and one draw needn't show every extreme that they name: prefix_len <= window_start.
All inputs are finite; a program needn't handle non-finite values.
Results may differ from the reference program's by a relative error of at most 0.008.
Values may be sent and summed in bfloat16 or wider, within the bound.
No kernel may reach another device: no remote copies, remote signals or barrier semaphores. Data moves between devices by JAX's collectives and lax.ppermute only.
A program may use at most 128 MiB of HBM per device.

```python
import math
import jax
import jax.numpy as jnp
from jax import lax

MH = 128
MP = 64
N_STATE = 256
NG = 8
AH = 64
KVH = 8
HD = 128
BLOCK = 128
S = 1024
CACHE = 4096


def draw_a_log(key, part):
    key_order, key_level = jax.random.split(key)
    head_order = jax.random.permutation(key_order, MH)
    level_draw = jax.random.uniform(key_level, (MH,), jnp.float32)
    slow_count = MH // 2
    slow_heads = head_order < slow_count
    slow_low = math.log(1.0 / (40.0 * S))
    slow_high = math.log(1.0 / (3.0 * S))
    fast_low = math.log(1.0 / 50.0)
    fast_high = math.log(1.0 / 20.0)
    slow_value = slow_low + level_draw * (slow_high - slow_low)
    fast_value = fast_low + level_draw * (fast_high - fast_low)
    return jnp.where(slow_heads, slow_value, fast_value).astype(jnp.float32)


def key_draw(key):
    return jax.random.normal(jax.random.fold_in(key, 7), (S, KVH, HD), jnp.float32)


def draw_keys(key, part):
    drawn = key_draw(key)
    return jnp.clip(drawn, -6.0, 6.0).reshape(S, KVH * HD).astype(jnp.bfloat16)


def draw_queries(key, part):
    query_draw = jax.random.normal(jax.random.fold_in(key, 11), (S, AH, HD), jnp.float32)
    return jnp.clip(query_draw, -6.0, 6.0).reshape(S, AH * HD).astype(jnp.bfloat16)


def block_levels(stream_key, dims, cuts, least, largest):
    def one(axis_at, parts):
        draws = jax.random.uniform(jax.random.fold_in(jax.random.fold_in(stream_key, 6), axis_at), (parts,), jnp.float32, least / len(cuts), largest / len(cuts))
        return jnp.repeat(jnp.exp(draws), dims[axis_at] // parts).reshape((-1,) + (1,) * (len(dims) - axis_at - 1))

    factor_of = one(*cuts[0])
    for cut in cuts[1:]:
        factor_of = factor_of * one(*cut)
    return factor_of


def centred(own_key, shape, scale, limit, cuts=(), held_as=jnp.bfloat16):
    values = jax.random.normal(own_key, shape, jnp.float32) * scale
    if len(cuts) > 0:
        values = block_levels(own_key, shape, cuts, -0.22, 0.18) * values
    return jnp.clip(values, min=-limit, max=limit).astype(held_as)


def setup_inputs(seed: int = 0, part: int = 0) -> dict:
    arg_keys = jax.random.split(jax.random.key(seed), 18)
    part_splits = jax.random.split(jax.random.fold_in(arg_keys[17], part), 18)
    x_in = centred(part_splits[0], (S, MH * MP), 1.0, 6.0, ((0, 4), (1, 4)))
    z_gate = centred(part_splits[1], (S, MH * MP), 1.0, 6.0, ((0, 4), (1, 4)))
    b_in = centred(part_splits[2], (S, NG * N_STATE), N_STATE ** -0.5, 0.375, ((0, 4), (1, 2)))
    c_in = centred(part_splits[3], (S, NG * N_STATE), N_STATE ** -0.5, 0.375, ((0, 4), (1, 2)))
    dt_raw = centred(part_splits[4], (S, MH), 0.5, 3.0, ((0, 4), (1, 4)), jnp.float32)
    dt_bias = jnp.clip(jax.random.uniform(arg_keys[5], (MH,), jnp.float32, -0.5, 0.5) * block_levels(arg_keys[5], (MH,), ((0, 4),), -0.4, 0.0), -0.5, 0.5)
    a_log = draw_a_log(jax.random.fold_in(arg_keys[17], 71), part)
    d_skip = jnp.clip(0.5 + 1.5 * jax.random.uniform(arg_keys[7], (MH,), jnp.float32) ** block_levels(arg_keys[7], (MH,), ((0, 4),), -0.2, 0.2), 0.5, 2.0)
    norm_weight = jnp.clip(1.0 + 0.1 * jax.random.normal(arg_keys[8], (MH * MP,), jnp.float32), 0.5, 1.5)
    ssm_init = centred(part_splits[9], (MH, MP, N_STATE), 1.0, 6.0, ((0, 4),), jnp.float32)
    queries = draw_queries(jax.random.fold_in(jax.random.fold_in(arg_keys[17], part), 71), part)
    keys = draw_keys(jax.random.fold_in(jax.random.fold_in(arg_keys[17], part), 71), part)
    values = centred(part_splits[12], (S, KVH * HD), 1.0, 6.0, ((0, 4), (1, 2)))
    cache_keys = centred(part_splits[13], (CACHE, KVH * HD), 1.0, 6.0, ((0, 2), (1, 2)))
    cache_values = centred(part_splits[14], (CACHE, KVH * HD), 1.0, 6.0, ((0, 2), (1, 2)))
    window_start = jax.random.randint(part_splits[15], (1,), CACHE, 1048576 - S).astype(jnp.int32)
    prefix_len = jax.random.randint(part_splits[16], (1,), CACHE // 4, CACHE + 1).astype(jnp.int32)
    return {"x_in": x_in, "z_gate": z_gate, "b_in": b_in, "c_in": c_in, "dt_raw": dt_raw, "dt_bias": dt_bias, "a_log": a_log, "d_skip": d_skip, "norm_weight": norm_weight, "ssm_init": ssm_init, "queries": queries, "keys": keys, "values": values, "cache_keys": cache_keys, "cache_values": cache_values, "window_start": window_start, "prefix_len": prefix_len}


def lowered(value):
    return lax.optimization_barrier(value.astype(jnp.bfloat16)).astype(jnp.float32)

def ssd_block(ssm_state, inputs):
    x_block, b_block, c_block, dt_block, log_block = inputs
    highest = lax.Precision.HIGHEST
    cumulative = jnp.cumsum(log_block, axis=0)
    per_group = MH // NG
    b_heads = jnp.repeat(b_block, per_group, axis=1)
    c_heads = jnp.repeat(c_block, per_group, axis=1)
    products = jnp.einsum('thn,shn->hts', c_heads, b_heads, precision=highest)
    positions = jnp.arange(BLOCK)
    lower_part = positions[:, None] >= positions[None, :]
    spread_log = cumulative.T[:, :, None] - cumulative.T[:, None, :]
    kernel = jnp.where(lower_part[None], jnp.exp(jnp.where(lower_part[None], spread_log, 0.0)), 0.0)
    kernel = lowered(kernel * products * dt_block.T[:, None, :])
    inner_part = jnp.einsum('hts,shp->thp', kernel, x_block, precision=highest)
    state_low = lowered(ssm_state)
    carried = jnp.exp(cumulative)[:, :, None] * jnp.einsum('thn,hpn->thp', c_heads, state_low, precision=highest)
    weights_tail = jnp.exp(cumulative[-1][None, :] - cumulative) * dt_block
    weighted = lowered(weights_tail[:, :, None] * x_block)
    update = jnp.einsum('shp,shn->hpn', weighted, b_heads, precision=highest)
    new_state = jnp.exp(cumulative[-1])[:, None, None] * ssm_state + update
    return (new_state, inner_part + carried)

def reference(x_in, z_gate, b_in, c_in, dt_raw, dt_bias, a_log, d_skip, norm_weight, ssm_init, queries, keys, values, cache_keys, cache_values, window_start, prefix_len):
    dt_value = jax.nn.softplus(dt_raw + dt_bias[None, :])
    decay_log = -jnp.exp(a_log)[None, :] * dt_value
    x_heads = x_in.astype(jnp.float32).reshape(S, MH, MP)
    b_groups = b_in.astype(jnp.float32).reshape(S, NG, N_STATE)
    c_groups = c_in.astype(jnp.float32).reshape(S, NG, N_STATE)
    block_count = S // BLOCK

    def as_blocks(array):
        return array.reshape((block_count, BLOCK) + array.shape[1:])
    final_state, outputs = lax.scan(ssd_block, ssm_init, (as_blocks(x_heads), as_blocks(b_groups), as_blocks(c_groups), as_blocks(dt_value), as_blocks(decay_log)))
    ssd_out = outputs.reshape(S, MH, MP) + d_skip[None, :, None] * x_heads
    gated = ssd_out * jax.nn.silu(z_gate.astype(jnp.float32).reshape(S, MH, MP))
    scale = lax.rsqrt(lax.optimization_barrier(jnp.mean(gated * gated, axis=-1, keepdims=True)) + 1e-05)
    mamba_out = ((gated * scale).reshape(S, MH * MP) * norm_weight[None, :]).astype(jnp.bfloat16)
    slot_ids = jnp.arange(CACHE)
    cache_valid = jnp.mod(window_start[0] - 1 - slot_ids, CACHE) < prefix_len[0]
    tokens = jnp.arange(S)
    valid_mask = jnp.concatenate([jnp.broadcast_to(cache_valid[None, :], (S, CACHE)), tokens[:, None] >= tokens[None, :]], axis=1)
    all_keys = jnp.concatenate([cache_keys, keys], axis=0).reshape(CACHE + S, KVH, HD).transpose(1, 0, 2)
    all_values = jnp.concatenate([cache_values, values], axis=0).reshape(CACHE + S, KVH, HD).transpose(1, 0, 2)
    query_heads = queries.reshape(S, AH, HD).transpose(1, 0, 2)
    group_size = AH // KVH

    def one_head(head_id):
        kv_head = head_id // group_size
        scores = jnp.dot(query_heads[head_id], all_keys[kv_head].T, preferred_element_type=jnp.float32) * (1.0 / math.sqrt(HD))
        row_best = lax.optimization_barrier(jnp.max(jnp.where(valid_mask, scores, -1e+30), axis=1))
        weights = jnp.where(valid_mask, jnp.exp(scores - row_best[:, None]), 0.0)
        row_total = lax.optimization_barrier(jnp.sum(weights, axis=1))
        mixed = jnp.dot(weights.astype(jnp.bfloat16), all_values[kv_head], preferred_element_type=jnp.float32)
        return (mixed / row_total[:, None]).astype(jnp.bfloat16)
    head_outputs = lax.map(one_head, jnp.arange(AH))
    attention_out = head_outputs.transpose(1, 0, 2).reshape(S, AH * HD)
    return (mamba_out, attention_out)
```

```python
import functools
import math

import jax
import jax.numpy as jnp
from jax import lax
from jax.experimental import pallas as pl
from jax.experimental.pallas import tpu as pltpu
from jax.sharding import PartitionSpec as P

MH = 128
MP = 64
N_STATE = 256
NG = 8
AH = 64
KVH = 8
HD = 128
BLOCK = 128
KEY_BLOCK = 512
ROW_GROUP = 512
LOG2_SCALE = math.log2(math.e) / math.sqrt(HD)
NEG = -1e30
F32 = jnp.float32
BF16 = jnp.bfloat16
VMEM_LIMIT = 56 << 20


def mm(a, b):
    return jnp.dot(a, b, preferred_element_type=F32)


def mm_nt(a, b):
    return lax.dot_general(a, b, (((1,), (1,)), ((), ())), preferred_element_type=F32)


def pieces_of(value):
    first = value.astype(BF16)
    rest = value - first.astype(F32)
    second = rest.astype(BF16)
    third = (rest - second.astype(F32)).astype(BF16)
    return first, second, third


def one_hot_expand(value, width):
    count = value.shape[1]
    row = lax.broadcasted_iota(jnp.int32, (count, width), 0)
    lane = lax.broadcasted_iota(jnp.int32, (count, width), 1)
    table = jnp.where(lane // MP == row, 1.0, 0.0).astype(BF16)
    first, second, third = pieces_of(value)
    return mm(first, table) + mm(second, table) + mm(third, table)


def fold_lanes(value, op):
    parts = [value[:, k : k + 128] for k in range(0, value.shape[1], 128)]
    while len(parts) > 1:
        parts = [
            op(parts[k], parts[k + 1]) if k + 1 < len(parts) else parts[k]
            for k in range(0, len(parts), 2)
        ]
    return parts[0]


def ssm_states_kernel(
    scalars, x_ref, b_ref, dt_ref, bias_ref, alog_ref, dskip_ref, init_ref,
    state_ref, rows_ref, log_ref, logt_ref, dtt_ref, dt_all, log_all,
):
    chunk = pl.program_id(0)
    tok = x_ref.shape[0]
    width = x_ref.shape[1]
    heads = width // MP
    chunks = dt_ref.shape[1] // heads

    @pl.when(chunk == 0)
    def _():
        dt = jax.nn.softplus(dt_ref[...] + bias_ref[...])
        decay = -jnp.exp(alog_ref[...]) * dt
        row = lax.broadcasted_iota(jnp.int32, (BLOCK, BLOCK), 0)
        col = lax.broadcasted_iota(jnp.int32, (BLOCK, BLOCK), 1)
        lower = jnp.where(row >= col, 1.0, 0.0).astype(BF16)
        logs = []
        for blk in range(tok // BLOCK):
            first, second, third = pieces_of(decay[blk * BLOCK : (blk + 1) * BLOCK])
            logs.append(mm(lower, first) + mm(lower, second) + mm(lower, third))
        logs = jnp.concatenate(logs, axis=0)
        for k in range(chunks):
            dt_all[k] = dt[:, k * heads : (k + 1) * heads]
            log_all[k] = logs[:, k * heads : (k + 1) * heads]

    dt = dt_all[chunk]
    logs = log_all[chunk]
    log_ref[0] = logs
    logt_ref[0] = logs.T
    dtt_ref[0] = dt.T
    state = None
    total = jnp.zeros((1, heads), F32)
    for blk in range(tok // BLOCK):
        part = slice(blk * BLOCK, (blk + 1) * BLOCK)
        end = logs[(blk + 1) * BLOCK - 1 : (blk + 1) * BLOCK, :]
        tail = jnp.exp(end - logs[part]) * dt[part]
        weighted = (one_hot_expand(tail, width) * x_ref[part, :].astype(F32)).astype(BF16)
        update = mm(b_ref[part, :].T, weighted)
        if state is None:
            state = update
        else:
            state = one_hot_expand(jnp.exp(end), width) * state + update
        total = total + end
    decay_row = one_hot_expand(jnp.exp(total), width)
    state_ref[...] = state
    rows_ref[0:1, :] = decay_row
    rows_ref[1:2, :] = one_hot_expand(dskip_ref[0], width)

    @pl.when(scalars[0] == 0)
    def _():
        first = init_ref[...].reshape(width, N_STATE).T
        state_ref[...] = state_ref[...] + decay_row * first


def ssm_states(scalars, x_in, b_in, dt_raw, dt_bias, a_log, d_skip, ssm_init, width, group_of):
    tok, lanes = x_in.shape
    chunks = lanes // width
    heads = width // MP
    head_count = dt_raw.shape[1]
    const = lambda *zeros: (lambda c, s: zeros)
    return pl.pallas_call(
        ssm_states_kernel,
        grid_spec=pltpu.PrefetchScalarGridSpec(
            num_scalar_prefetch=1,
            grid=(chunks,),
            in_specs=[
                pl.BlockSpec((tok, width), lambda c, s: (0, c)),
                pl.BlockSpec((tok, N_STATE), lambda c, s: (0, group_of(c, s))),
                pl.BlockSpec((tok, head_count), const(0, 0)),
                pl.BlockSpec((1, head_count), const(0, 0)),
                pl.BlockSpec((1, head_count), const(0, 0)),
                pl.BlockSpec((1, 1, heads), lambda c, s: (c, 0, 0)),
                pl.BlockSpec((heads, MP, N_STATE), lambda c, s: (c, 0, 0)),
            ],
            out_specs=[
                pl.BlockSpec((N_STATE, width), lambda c, s: (0, c)),
                pl.BlockSpec((8, width), lambda c, s: (0, c)),
                pl.BlockSpec((1, tok, heads), lambda c, s: (c, 0, 0)),
                pl.BlockSpec((1, heads, tok), lambda c, s: (c, 0, 0)),
                pl.BlockSpec((1, heads, tok), lambda c, s: (c, 0, 0)),
            ],
            scratch_shapes=[pltpu.VMEM((chunks, tok, heads), F32)] * 2,
        ),
        out_shape=[
            jax.ShapeDtypeStruct((N_STATE, lanes), F32),
            jax.ShapeDtypeStruct((8, lanes), F32),
            jax.ShapeDtypeStruct((chunks, tok, heads), F32),
            jax.ShapeDtypeStruct((chunks, heads, tok), F32),
            jax.ShapeDtypeStruct((chunks, heads, tok), F32),
        ],
        compiler_params=pltpu.CompilerParams(vmem_limit_bytes=VMEM_LIMIT),
        cost_estimate=pl.CostEstimate(
            flops=2 * tok * lanes * N_STATE * 4, bytes_accessed=6 << 20, transcendentals=1 << 16
        ),
        name="ssm_states",
    )(
        scalars, x_in, b_in, dt_raw, dt_bias[None, :], a_log[None, :],
        d_skip.reshape(chunks, 1, heads), ssm_init,
    )


def hop_kernel(scalars, received_ref, state_ref, rows_ref, out_ref, *, step):
    place = scalars[0]

    @pl.when(step <= place)
    def _():
        out_ref[...] = received_ref[...]

    @pl.when((step > place) & (place == 0))
    def _():
        out_ref[...] = state_ref[...].astype(BF16)

    @pl.when((step > place) & (place > 0))
    def _():
        carried = rows_ref[0:1, :] * received_ref[...].astype(F32)
        out_ref[...] = (carried + state_ref[...]).astype(BF16)


def hop(scalars, received, state, rows, step):
    width = received.shape[1]
    chunks = state.shape[1] // width

    def chunk_of(k, s):
        return (0, jnp.clip(step - 1 - s[0], 0, chunks - 1))

    return pl.pallas_call(
        functools.partial(hop_kernel, step=step),
        grid_spec=pltpu.PrefetchScalarGridSpec(
            num_scalar_prefetch=1,
            grid=(1,),
            in_specs=[
                pl.BlockSpec(received.shape, lambda k, s: (0, 0)),
                pl.BlockSpec((N_STATE, width), chunk_of),
                pl.BlockSpec((8, width), chunk_of),
            ],
            out_specs=pl.BlockSpec(received.shape, lambda k, s: (0, 0)),
        ),
        out_shape=jax.ShapeDtypeStruct(received.shape, BF16),
        cost_estimate=pl.CostEstimate(flops=1 << 18, bytes_accessed=1 << 20, transcendentals=0),
        name="hop",
    )(scalars, received, state, rows)


def ssm_outputs_kernel(
    scalars, x_ref, z_ref, b_ref, c_ref, log_ref, logt_ref, dtt_ref, rows_ref, norm_ref, init_hbm,
    *rest, hops,
):
    received = rest[:hops]
    out_ref, carry, init_buf, sems, init_sem = rest[hops:]
    chunk = pl.program_id(0)
    chunks = pl.num_programs(0)
    place = scalars[0]
    tok, width = x_ref.shape
    heads = width // MP
    count = carry.shape[0]

    @pl.when(chunk == 0)
    def _():
        for k in range(count):
            for r in range(hops):
                @pl.when((place > 0) & (place + k == r))
                def _():
                    pltpu.make_async_copy(received[r], carry.at[k], sems.at[k]).start()

        @pl.when(place == 0)
        def _():
            whole = pltpu.make_async_copy(init_hbm, init_buf, init_sem)
            whole.start()
            whole.wait()
            for k in range(count):
                first = init_buf[k * heads : (k + 1) * heads].reshape(width, N_STATE)
                carry[k] = first.astype(BF16).T

    @pl.when(place > 0)
    def _():
        pltpu.make_async_copy(received[0], carry.at[chunk], sems.at[chunk]).wait()

    row = lax.broadcasted_iota(jnp.int32, (BLOCK, BLOCK), 0)
    col = lax.broadcasted_iota(jnp.int32, (BLOCK, BLOCK), 1)
    lower = row >= col
    low_half = col < MP
    mean_table = jnp.where(row // MP == col // MP, 1.0 / MP, 0.0).astype(BF16)
    logs = log_ref[0]
    logt = logt_ref[0]
    dtt = dtt_ref[0]
    dts = dtt.T
    skip = rows_ref[1:2, :]
    state = carry[chunk].astype(F32)
    for blk in range(tok // BLOCK):
        part = slice(blk * BLOCK, (blk + 1) * BLOCK)
        c_blk = c_ref[part, :]
        b_blk = b_ref[part, :]
        products = mm_nt(c_blk, b_blk)
        log_blk = logs[part]
        carried = one_hot_expand(jnp.exp(log_blk), width) * mm(c_blk, state.astype(BF16))
        x_blk = x_ref[part, :]
        if (blk + 1) * BLOCK < tok:
            end = log_blk[BLOCK - 1 : BLOCK, :]
            tail = jnp.exp(end - log_blk) * dts[part]
            weighted = (one_hot_expand(tail, width) * x_blk.astype(F32)).astype(BF16)
            state = one_hot_expand(jnp.exp(end), width) * state + mm(b_blk.T, weighted)
        for pair in range(heads // 2):
            lanes = slice(pair * 128, (pair + 1) * 128)
            kernels = []
            for h in (2 * pair, 2 * pair + 1):
                spread = log_blk[:, h : h + 1] - logt[h : h + 1, part]
                decay = jnp.exp(jnp.where(lower, spread, NEG))
                kernels.append((decay * products * dtt[h : h + 1, part]).astype(BF16))
            x_pair = x_blk[:, lanes]
            zero = jnp.zeros_like(x_pair)
            stacked = jnp.concatenate(
                [jnp.where(low_half, x_pair, zero), jnp.where(low_half, zero, x_pair)], axis=0
            )
            inner = mm(jnp.concatenate(kernels, axis=1), stacked)
            value = inner + carried[:, lanes] + skip[:, lanes] * x_pair.astype(F32)
            z_pair = z_ref[part, lanes].astype(F32)
            gated = value * (z_pair / (1.0 + jnp.exp(-z_pair)))
            square = gated * gated
            high = square.astype(BF16)
            low = (square - high.astype(F32)).astype(BF16)
            mean = mm(high, mean_table) + mm(low, mean_table)
            normed = gated * lax.rsqrt(mean + 1e-05) * norm_ref[:, lanes]
            out_ref[part, lanes] = normed.astype(BF16)


def ssm_outputs(scalars, x_in, z_gate, b_in, c_in, logs, logt, dtt, rows, norm_weight, ssm_init,
                received, width, group_of):
    tok, lanes = x_in.shape
    chunks = lanes // width
    heads = width // MP
    anywhere = pl.BlockSpec(memory_space=pl.ANY)
    per_chunk = pl.BlockSpec((tok, width), lambda c, s: (0, c))
    per_group = pl.BlockSpec((tok, N_STATE), lambda c, s: (0, group_of(c, s)))
    return pl.pallas_call(
        functools.partial(ssm_outputs_kernel, hops=len(received)),
        grid_spec=pltpu.PrefetchScalarGridSpec(
            num_scalar_prefetch=1,
            grid=(chunks,),
            in_specs=[
                per_chunk,
                per_chunk,
                per_group,
                per_group,
                pl.BlockSpec((1, tok, heads), lambda c, s: (c, 0, 0)),
                pl.BlockSpec((1, heads, tok), lambda c, s: (c, 0, 0)),
                pl.BlockSpec((1, heads, tok), lambda c, s: (c, 0, 0)),
                pl.BlockSpec((8, width), lambda c, s: (0, c)),
                pl.BlockSpec((1, width), lambda c, s: (0, c)),
            ]
            + [anywhere] * (1 + len(received)),
            out_specs=per_chunk,
            scratch_shapes=[
                pltpu.VMEM((chunks, N_STATE, width), BF16),
                pltpu.VMEM(ssm_init.shape, F32),
                pltpu.SemaphoreType.DMA((chunks,)),
                pltpu.SemaphoreType.DMA,
            ],
        ),
        out_shape=jax.ShapeDtypeStruct((tok, lanes), BF16),
        compiler_params=pltpu.CompilerParams(vmem_limit_bytes=VMEM_LIMIT),
        cost_estimate=pl.CostEstimate(
            flops=2 * tok * lanes * N_STATE * 8, bytes_accessed=6 << 20, transcendentals=1 << 21
        ),
        name="ssm_outputs",
    )(scalars, x_in, z_gate, b_in, c_in, logs, logt, dtt, rows, norm_weight[None, :], ssm_init,
      *received)


def attend_kernel(scalars, q_ref, *rest, kv_head, kv_count, heads, hops, use_cache, use_window,
                  carry_in, final, slots, alias):
    rest = list(rest)
    take = lambda n: [rest.pop(0) for _ in range(n)]
    keys_near, keys_far, values_near, values_far = take(4) if use_cache else [None] * 4
    window = take(hops + 1) if use_window else []
    acc_in, best_in, total_in = take(3) if carry_in else [None] * 3
    if alias:
        take(1)
    outs = take(1 if final else 3)
    k_buf, v_buf, s_even, s_odd, best_buf, total_buf, acc_buf, sems = rest
    place, dp, first_block, cache_blocks, newest, held = (scalars[k] for k in range(6))
    column = scalars[6]
    tok = q_ref.shape[0]
    half = slots // 2
    base = slots if use_cache else 0

    copies = []
    if use_cache:
        near = pl.multiple_of(dp * half, half)
        far = pl.multiple_of((1 - dp) * half, half)
        lanes = pl.ds(pl.multiple_of((column + kv_head) * HD, HD), HD)
        copies += [
            pltpu.make_async_copy(keys_near.at[:, lanes], k_buf.at[pl.ds(near, half)], sems.at[0]),
            pltpu.make_async_copy(keys_far.at[:, lanes], k_buf.at[pl.ds(far, half)], sems.at[1]),
            pltpu.make_async_copy(values_near.at[:, lanes], v_buf.at[pl.ds(near, half)], sems.at[2]),
            pltpu.make_async_copy(values_far.at[:, lanes], v_buf.at[pl.ds(far, half)], sems.at[3]),
        ]
    for k, ref in enumerate(window):
        rows = pl.ds(base + k * tok, tok)
        for which, buf in ((kv_head, k_buf), (kv_count + kv_head, v_buf)):
            copies.append(
                pltpu.make_async_copy(
                    ref.at[:, which * HD : (which + 1) * HD], buf.at[rows],
                    sems.at[len(copies) + (0 if use_cache else 4)],
                )
            )
    for copy in copies:
        copy.start()
    if use_window:
        loose = (hops + 1) * tok
        padded = -(-loose // KEY_BLOCK) * KEY_BLOCK
        if padded > loose:
            for buf in (k_buf, v_buf):
                buf[base + loose : base + padded, :] = jnp.zeros((padded - loose, HD), BF16)
    for copy in copies:
        copy.wait()

    group = min(ROW_GROUP, heads * tok)
    per_group = group // tok
    steps = heads // per_group
    all_blocks = cache_blocks if use_cache else 0
    extra = (place * tok + tok + KEY_BLOCK - 1) // KEY_BLOCK
    cache_total = slots // KEY_BLOCK
    near_window = (
        lax.broadcasted_iota(jnp.int32, (group, KEY_BLOCK), 0) % tok
        - lax.broadcasted_iota(jnp.int32, (group, KEY_BLOCK), 1)
    )
    lane = lax.broadcasted_iota(jnp.int32, (1, KEY_BLOCK), 1)

    def queries(step):
        return jnp.concatenate(
            [
                q_ref[:, (step * per_group + h) * HD : (step * per_group + h + 1) * HD]
                for h in range(per_group)
            ],
            axis=0,
        )

    buffers = (s_even, s_odd)
    row_best = None
    for step in range(steps + 1):
        first_pass = step < steps
        second_pass = step > 0
        into, out_of = buffers[step % 2], buffers[1 - step % 2]
        rows_now = slice(step * group, (step + 1) * group)
        rows_before = slice((step - 1) * group, step * group)
        if first_pass:
            if carry_in:
                best_buf[...] = best_in[rows_now, :]
            else:
                best_buf[...] = jnp.full_like(best_buf, NEG)
        if second_pass:
            if carry_in:
                factor = jnp.exp2((best_in[rows_before, :] - row_best) * LOG2_SCALE)
                acc_buf[...] = factor * acc_in[rows_before, :]
                lead = lax.broadcasted_iota(jnp.int32, (group, 128), 1) == 0
                total_buf[...] = jnp.where(lead, factor * total_in[rows_before, :], 0.0)
            else:
                acc_buf[...] = jnp.zeros_like(acc_buf)
                total_buf[...] = jnp.zeros_like(total_buf)
            scaled_best = row_best[:, 0:1] * LOG2_SCALE

        def visit(offset, bias, step=step, first_pass=first_pass, second_pass=second_pass,
                  into=into, out_of=out_of, scaled_best=scaled_best if second_pass else None):
            span = pl.ds(offset, KEY_BLOCK)
            if first_pass:
                scores = mm_nt(queries(step), k_buf[span, :]) + bias
                into[:, span] = scores
                best_buf[...] = jnp.maximum(best_buf[...], fold_lanes(scores, jnp.maximum))
            if second_pass:
                probs = jnp.exp2(out_of[:, span] * LOG2_SCALE - scaled_best)
                total_buf[...] += fold_lanes(probs, jnp.add)
                acc_buf[...] += mm(probs.astype(BF16), v_buf[span, :])

        if use_cache:
            def cache_step(j, unused):
                offset = pl.multiple_of(lax.rem(first_block + j, cache_total) * KEY_BLOCK, KEY_BLOCK)
                age = newest - (offset + lane)
                age = jnp.where(age < 0, age + slots, age)
                visit(offset, jnp.where(age < held, 0.0, NEG))
                return 0

            lax.fori_loop(0, all_blocks, cache_step, 0)
        if use_window:
            allowed = (near_window >= 0) | ((lane >= tok) & (lane < tok * (place + 1)))
            visit(base, jnp.where(allowed, 0.0, NEG))

            def window_step(j, unused):
                offset = pl.multiple_of(base + j * KEY_BLOCK, KEY_BLOCK)
                visit(offset, jnp.where(lane + j * KEY_BLOCK < tok * (place + 1), 0.0, NEG))
                return 0

            lax.fori_loop(1, extra, window_step, 0)
        if second_pass:
            total = jnp.sum(total_buf[...], axis=-1, keepdims=True)
            if final:
                result = (acc_buf[...] / total).astype(BF16)
                for h in range(per_group):
                    k = (step - 1) * per_group + h
                    outs[0][:, k * HD : (k + 1) * HD] = result[h * tok : (h + 1) * tok]
            else:
                outs[0][rows_before, :] = acc_buf[...]
                outs[1][rows_before, :] = row_best
                outs[2][rows_before, :] = jnp.broadcast_to(total, (group, 128))
        if first_pass:
            row_best = jnp.broadcast_to(
                jnp.max(best_buf[...], axis=-1, keepdims=True), (group, 128)
            )


def attend(scalars, queries, head, heads, kv_count, cache=None, window=None, carry=None, into=None,
           final=True):
    tok = queries.shape[0]
    kv_head = head // (AH // KVH)
    slots = 2 * cache[0].shape[0] if cache is not None else 0
    hops = len(window) - 1 if window is not None else 0
    rows = heads * tok
    depth = slots
    if window is not None:
        depth += -(-((hops + 1) * tok) // KEY_BLOCK) * KEY_BLOCK
    group = min(ROW_GROUP, rows)
    anywhere = pl.BlockSpec(memory_space=pl.ANY)
    whole = pl.BlockSpec((rows, 128), lambda k, s: (0, 0))
    part = pl.BlockSpec((tok, heads * HD), lambda k, s: (0, head // heads))
    operands = [scalars, queries]
    in_specs = [part]
    for group_of in (cache, window):
        if group_of is not None:
            operands += list(group_of)
            in_specs += [anywhere] * len(group_of)
    if carry is not None:
        operands += list(carry)
        in_specs += [whole] * 3
    aliases = {}
    if into is not None:
        aliases = {len(operands): 0}
        operands.append(into)
        in_specs.append(anywhere)
    if final:
        out_specs, out_shape = part, jax.ShapeDtypeStruct(queries.shape, BF16)
    else:
        out_specs, out_shape = [whole] * 3, [jax.ShapeDtypeStruct((rows, 128), F32)] * 3
    keys_read = slots + (hops + 1) * tok * (window is not None)
    return pl.pallas_call(
        functools.partial(
            attend_kernel, kv_head=kv_head, kv_count=kv_count, heads=heads, hops=hops,
            use_cache=cache is not None, use_window=window is not None, carry_in=carry is not None,
            final=final, slots=slots, alias=into is not None,
        ),
        grid_spec=pltpu.PrefetchScalarGridSpec(
            num_scalar_prefetch=1,
            grid=(1,),
            in_specs=in_specs,
            out_specs=out_specs,
            scratch_shapes=[
                pltpu.VMEM((depth, HD), BF16),
                pltpu.VMEM((depth, HD), BF16),
                pltpu.VMEM((group, depth), F32),
                pltpu.VMEM((group, depth), F32),
                pltpu.VMEM((group, 128), F32),
                pltpu.VMEM((group, 128), F32),
                pltpu.VMEM((group, 128), F32),
                pltpu.SemaphoreType.DMA((4 + 2 * (hops + 1),)),
            ],
        ),
        out_shape=out_shape,
        input_output_aliases=aliases,
        compiler_params=pltpu.CompilerParams(vmem_limit_bytes=VMEM_LIMIT),
        cost_estimate=pl.CostEstimate(
            flops=16 * rows * keys_read * HD, bytes_accessed=4 * keys_read * HD,
            transcendentals=rows * keys_read,
        ),
        name="attend",
    )(*operands)


def tie(*values):
    return lax.optimization_barrier(values)


def local(x_in, z_gate, b_in, c_in, dt_raw, dt_bias, a_log, d_skip, norm_weight, ssm_init, queries,
          keys, values, cache_keys, cache_values, window_start, prefix_len):
    tok, lanes = x_in.shape
    head_count = dt_raw.shape[1]
    per_group = MH // NG
    places = lax.axis_size("seq")
    place = lax.axis_index("seq")
    dp = lax.axis_index("dp")
    q_count = queries.shape[1] // HD
    kv_here = keys.shape[1] // HD
    kv_count = max(1, q_count * KVH // AH)
    width = 2 * kv_count * HD
    chunks = lanes // width
    heads_in_chunk = width // MP
    column = (dp * q_count) // (AH // KVH)
    slots = 2 * cache_keys.shape[0]

    ring = [(k, (k + 1) % places) for k in range(places)]
    swap = [(0, 1), (1, 0)]
    far_keys = lax.ppermute(cache_keys, "dp", swap)
    far_values = lax.ppermute(cache_values, "dp", swap)

    own_rows = jnp.concatenate(
        [
            lax.dynamic_slice_in_dim(array, column * HD, kv_count * HD, axis=1)
            for array in (keys, values)
        ],
        axis=1,
    )

    newest = jnp.mod(window_start[0] - 1, slots)
    held = prefix_len[0]
    oldest = jnp.mod(newest - held + 1, slots)
    first_block = oldest // KEY_BLOCK
    cache_blocks = jnp.minimum(
        slots // KEY_BLOCK, (oldest % KEY_BLOCK + held + KEY_BLOCK - 1) // KEY_BLOCK
    )
    first_head = dp * head_count
    scalars = jnp.stack(
        [place, dp, first_block, cache_blocks, newest, held, column, first_head]
    ).astype(jnp.int32)

    def group_of(c, s):
        return (s[7] + c * heads_in_chunk) // per_group

    received = []
    send = own_rows
    arrived = lax.ppermute(send, "seq", ring)
    x_tied, send = tie(x_in, send)
    states, rows, logs, logt, dtt = ssm_states(
        scalars, x_tied, b_in, dt_raw, dt_bias, a_log, d_skip, ssm_init, width, group_of
    )
    received.append(arrived)

    cache = (cache_keys, far_keys, cache_values, far_values)
    heads = min(4, q_count)
    parts = list(range(0, q_count, heads))
    last_step = places - 1 + chunks - 1
    window_ready = places - 1
    result = None
    partial = None
    jobs = []
    if len(parts) > 1:
        jobs.append(("open", parts[0]))
        jobs += [("full", head) for head in parts[1:]]
        jobs.append(("close", parts[0]))
    else:
        jobs.append(("full", parts[0]))

    def run(job, queries_now):
        nonlocal result, partial
        kind, head = job
        if kind == "open":
            partial = attend(scalars, queries_now, head, heads, kv_count, cache=cache, final=False)
            return partial[0]
        window = [own_rows] + received[: places - 1]
        if kind == "full":
            result = attend(
                scalars, queries_now, head, heads, kv_count, cache=cache, window=window, into=result
            )
        else:
            result = attend(
                scalars, queries_now, head, heads, kv_count, window=window, carry=partial,
                into=result,
            )
        return result

    done = states
    for step in range(1, last_step + 1):
        incoming, tied = tie(received[-1], done)
        if done is states:
            states = tied
        elif done is result:
            result = tied
        done = tied
        send = hop(scalars, incoming, states, rows, step)
        arrived = lax.ppermute(send, "seq", ring)
        queries_now, send = tie(queries, send)
        ready = jobs and (jobs[0][0] == "open" or step >= window_ready)
        if ready:
            done = run(jobs.pop(0), queries_now)
        received.append(arrived)
    for job in jobs:
        run(job, queries)
    mamba_out = ssm_outputs(
        scalars, x_in, z_gate, b_in, c_in, logs, logt, dtt, rows, norm_weight, ssm_init, received,
        width, group_of,
    )
    return (mamba_out, result)


def solution(mesh):
    rows = P(("groups", "seq"), ("tp", "dp"))
    shared = P(("groups", "seq"), "tp")
    heads = P(("tp", "dp"))
    cached = P(("groups", "dp"), "tp")
    return jax.shard_map(
        local,
        mesh=mesh,
        in_specs=(
            rows, rows, shared, shared, rows, heads, heads, heads, heads,
            P(("groups", "tp", "dp"), None, None), rows, shared, shared, cached, cached,
            P("groups"), P("groups"),
        ),
        out_specs=(rows, rows),
        check_vma=False,
    )
```

```python
import functools
import math

import jax
import jax.numpy as jnp
from jax import lax
from jax.experimental import pallas as pl
from jax.experimental.pallas import tpu as pltpu
from jax.sharding import PartitionSpec as P

MH = 128
MP = 64
N_STATE = 256
NG = 8
AH = 64
KVH = 8
HD = 128
BLOCK = 128
KEY_BLOCK = 512
LOG2_SCALE = math.log2(math.e) / math.sqrt(HD)
NEG = -1e30
F32 = jnp.float32
BF16 = jnp.bfloat16
VMEM_LIMIT = 56 << 20


def mm(a, b):
    return jnp.dot(a, b, preferred_element_type=F32)


def mm_nt(a, b):
    return lax.dot_general(a, b, (((1,), (1,)), ((), ())), preferred_element_type=F32)


def pieces_of(value):
    first = value.astype(BF16)
    rest = value - first.astype(F32)
    second = rest.astype(BF16)
    third = (rest - second.astype(F32)).astype(BF16)
    return first, second, third


def head_table(heads, width):
    row = lax.broadcasted_iota(jnp.int32, (heads, width), 0)
    lane = lax.broadcasted_iota(jnp.int32, (heads, width), 1)
    table = jnp.where(lane // MP == row, 1.0, 0.0).astype(BF16)
    return jnp.concatenate([table] * 3, axis=0)


def expand(value, table):
    stacked = jnp.concatenate(pieces_of(value), axis=0)
    return lax.dot_general(stacked, table, (((0,), (0,)), ((), ())), preferred_element_type=F32)


def fold_lanes(value, op):
    parts = [value[:, k : k + 128] for k in range(0, value.shape[1], 128)]
    while len(parts) > 1:
        parts = [
            op(parts[k], parts[k + 1]) if k + 1 < len(parts) else parts[k]
            for k in range(0, len(parts), 2)
        ]
    return parts[0]


def ssm_states_kernel(
    scalars, x_ref, b_ref, dt_ref, bias_ref, alog_ref, dskip_ref, init_ref,
    state_ref, rows_ref, logt_ref, dtt_ref, dt_all, log_all, skip_all,
):
    span = pl.program_id(0)
    tok, lanes = x_ref.shape
    heads = lanes // MP
    spans = dt_ref.shape[0] // heads
    parts = state_ref.shape[0]
    width = lanes // parts

    @pl.when(span == 0)
    def _():
        column = lambda ref: jnp.broadcast_to(ref[...], (8, ref.shape[1])).T[:, 0:1]
        dt = jax.nn.softplus(dt_ref[...] + column(bias_ref))
        decay = -jnp.exp(column(alog_ref)) * dt
        row = lax.broadcasted_iota(jnp.int32, (BLOCK, BLOCK), 0)
        col = lax.broadcasted_iota(jnp.int32, (BLOCK, BLOCK), 1)
        upper = jnp.where(row <= col, 1.0, 0.0).astype(BF16)
        logs = []
        for blk in range(tok // BLOCK):
            first, second, third = pieces_of(decay[:, blk * BLOCK : (blk + 1) * BLOCK])
            logs.append(mm(first, upper) + mm(second, upper) + mm(third, upper))
        logs = jnp.concatenate(logs, axis=1)
        skip = jnp.broadcast_to(column(dskip_ref), (dt_ref.shape[0], 128))
        for k in range(spans):
            dt_all[k] = dt[k * heads : (k + 1) * heads]
            log_all[k] = logs[k * heads : (k + 1) * heads]
            skip_all[k] = skip[k * heads : (k + 1) * heads]

    dt = dt_all[span]
    logs = log_all[span]
    few = heads // parts
    for k in range(parts):
        logt_ref[k] = logs[k * few : (k + 1) * few]
        dtt_ref[k] = dt[k * few : (k + 1) * few]
    table = head_table(heads, lanes)
    state = None
    total = jnp.zeros((heads, 1), F32)
    for blk in range(tok // BLOCK):
        part = slice(blk * BLOCK, (blk + 1) * BLOCK)
        end = logs[:, (blk + 1) * BLOCK - 1 : (blk + 1) * BLOCK]
        tail = jnp.exp(end - logs[:, part]) * dt[:, part]
        weighted = (expand(tail, table) * x_ref[part, :].astype(F32)).astype(BF16)
        update = mm(b_ref[part, :].T, weighted)
        if state is None:
            state = update
        else:
            state = expand(jnp.broadcast_to(jnp.exp(end), (heads, 8)), table)[0:1] * state + update
        total = total + end
    place = scalars[0]
    lane = lax.broadcasted_iota(jnp.int32, (heads, 8), 1)
    rows = expand(jnp.where(lane == 0, jnp.exp(total), skip_all[span][:, 0:8]), table)
    for k in range(parts):
        state_ref[k] = state[:, k * width : (k + 1) * width]
        rows_ref[k] = rows[:, k * width : (k + 1) * width]

    @pl.when(place == 0)
    def _():
        for k in range(parts):
            first = init_ref[k * few : (k + 1) * few].reshape(width, N_STATE).T
            state_ref[k] = state_ref[k] + rows_ref[k, 0:1, :] * first
            rows_ref[k, 0:1, :] = jnp.zeros((1, width), F32)


def ssm_states(scalars, x_in, b_in, dt_raw, dt_bias, a_log, d_skip, ssm_init, width, span):
    tok, lanes = x_in.shape
    chunks = lanes // width
    head_count = dt_raw.shape[1]
    heads = span // MP
    few = width // MP
    parts = span // width
    per_group = MH // NG
    flat = lambda c, s: (0, 0)
    major = lambda c, s: (c, 0, 0)
    return pl.pallas_call(
        ssm_states_kernel,
        grid_spec=pltpu.PrefetchScalarGridSpec(
            num_scalar_prefetch=1,
            grid=(lanes // span,),
            in_specs=[
                pl.BlockSpec((tok, span), lambda c, s: (0, c)),
                pl.BlockSpec((tok, N_STATE), lambda c, s: (0, (s[7] + c * heads) // per_group)),
                pl.BlockSpec((head_count, tok), flat),
                pl.BlockSpec((1, head_count), flat),
                pl.BlockSpec((1, head_count), flat),
                pl.BlockSpec((1, head_count), flat),
                pl.BlockSpec((heads, MP, N_STATE), major),
            ],
            out_specs=[
                pl.BlockSpec((parts, N_STATE, width), major),
                pl.BlockSpec((parts, 8, width), major),
                pl.BlockSpec((parts, few, tok), major),
                pl.BlockSpec((parts, few, tok), major),
            ],
            scratch_shapes=[
                pltpu.VMEM((lanes // span, heads, tok), F32),
                pltpu.VMEM((lanes // span, heads, tok), F32),
                pltpu.VMEM((lanes // span, heads, 128), F32),
            ],
        ),
        out_shape=[
            jax.ShapeDtypeStruct((chunks, N_STATE, width), F32),
            jax.ShapeDtypeStruct((chunks, 8, width), F32),
            jax.ShapeDtypeStruct((chunks, few, tok), F32),
            jax.ShapeDtypeStruct((chunks, few, tok), F32),
        ],
        compiler_params=pltpu.CompilerParams(vmem_limit_bytes=VMEM_LIMIT),
        cost_estimate=pl.CostEstimate(
            flops=2 * tok * lanes * N_STATE * 4, bytes_accessed=6 << 20, transcendentals=1 << 16
        ),
        name="ssm_states",
    )(
        scalars, x_in, b_in, dt_raw.T, dt_bias[None, :], a_log[None, :], d_skip[None, :], ssm_init
    )


def hop(place, received, states, rows, step):
    chunks = states.shape[0]
    chunk = jnp.clip(step - 1 - place, 0, chunks - 1)
    state = lax.dynamic_index_in_dim(states, chunk, 0, keepdims=False)
    decay = lax.dynamic_index_in_dim(rows, chunk, 0, keepdims=False)[0:1, :]
    combined = (decay * received.astype(F32) + state).astype(BF16)
    return jnp.where(step <= place, received, combined)


def ssm_outputs_kernel(
    scalars, x_ref, z_ref, b_ref, c_ref, logt_ref, dtt_ref, rows_ref, norm_ref, init_hbm,
    *rest, hops,
):
    received = rest[:hops]
    out_ref, carry, init_buf, sems, init_sem = rest[hops:]
    chunk = pl.program_id(0)
    place = scalars[0]
    tok, width = x_ref.shape
    heads = width // MP
    count = carry.shape[0]

    @pl.when(chunk == 0)
    def _():
        for k in range(count):
            for r in range(hops):
                @pl.when((place > 0) & (place + k == r))
                def _():
                    pltpu.make_async_copy(received[r], carry.at[k], sems.at[k]).start()

        @pl.when(place == 0)
        def _():
            whole = pltpu.make_async_copy(init_hbm, init_buf, init_sem)
            whole.start()
            whole.wait()
            for k in range(count):
                first = init_buf[k * heads : (k + 1) * heads].reshape(width, N_STATE)
                carry[k] = first.astype(BF16).T

    @pl.when(place > 0)
    def _():
        pltpu.make_async_copy(received[0], carry.at[chunk], sems.at[chunk]).wait()

    row = lax.broadcasted_iota(jnp.int32, (BLOCK, BLOCK), 0)
    col = lax.broadcasted_iota(jnp.int32, (BLOCK, BLOCK), 1)
    lower = row >= col
    low_half = col < MP
    mean_table = jnp.where(row // MP == col // MP, 1.0 / MP, 0.0).astype(BF16)
    mean_table = jnp.concatenate([mean_table, mean_table], axis=0)
    table = head_table(heads, width)
    logt = logt_ref[0]
    dtt = dtt_ref[0]
    logs = logt.T
    skip = rows_ref[0, 1:2, :]
    low_state = carry[chunk]
    pairs = heads // 2
    for blk in range(tok // BLOCK):
        part = slice(blk * BLOCK, (blk + 1) * BLOCK)
        c_blk = c_ref[part, :]
        b_blk = b_ref[part, :]
        x_blk = x_ref[part, :]
        products = mm_nt(c_blk, b_blk)
        log_blk = logs[part]
        kernels = []
        for h in range(heads):
            spread = log_blk[:, h : h + 1] - logt[h : h + 1, part]
            decay = jnp.exp(jnp.where(lower, spread, NEG))
            kernels.append((decay * products * dtt[h : h + 1, part]).astype(BF16))
        carried = expand(jnp.exp(logt[:, part]), table) * mm(c_blk, low_state)
        if (blk + 1) * BLOCK < tok:
            end = logt[:, (blk + 1) * BLOCK - 1 : (blk + 1) * BLOCK]
            tail = jnp.exp(end - logt[:, part]) * dtt[:, part]
            weighted = (expand(tail, table) * x_blk.astype(F32)).astype(BF16)
            factor = expand(jnp.broadcast_to(jnp.exp(end), (heads, 8)), table)[0:1]
            low_state = (factor * low_state.astype(F32) + mm(b_blk.T, weighted)).astype(BF16)
        lanes = [slice(pair * 128, (pair + 1) * 128) for pair in range(pairs)]
        inner = []
        for pair in range(pairs):
            x_pair = x_blk[:, lanes[pair]]
            zero = jnp.zeros_like(x_pair)
            stacked = jnp.concatenate(
                [jnp.where(low_half, x_pair, zero), jnp.where(low_half, zero, x_pair)], axis=0
            )
            inner.append(mm(jnp.concatenate(kernels[2 * pair : 2 * pair + 2], axis=1), stacked))
        gated = []
        for pair in range(pairs):
            value = (
                inner[pair]
                + carried[:, lanes[pair]]
                + skip[:, lanes[pair]] * x_blk[:, lanes[pair]].astype(F32)
            )
            z_pair = z_ref[part, lanes[pair]].astype(F32)
            gated.append(value * (z_pair / (1.0 + jnp.exp(-z_pair))))
        means = []
        for pair in range(pairs):
            square = gated[pair] * gated[pair]
            high = square.astype(BF16)
            low = (square - high.astype(F32)).astype(BF16)
            means.append(mm(jnp.concatenate([high, low], axis=1), mean_table))
        for pair in range(pairs):
            normed = gated[pair] * lax.rsqrt(means[pair] + 1e-05) * norm_ref[:, lanes[pair]]
            out_ref[part, lanes[pair]] = normed.astype(BF16)


def ssm_outputs(scalars, x_in, z_gate, b_in, c_in, logt, dtt, rows, norm_weight, ssm_init,
                received, width):
    tok, lanes = x_in.shape
    chunks = lanes // width
    heads = width // MP
    per_group = MH // NG
    anywhere = pl.BlockSpec(memory_space=pl.ANY)
    per_chunk = pl.BlockSpec((tok, width), lambda c, s: (0, c))
    grouped = pl.BlockSpec((tok, N_STATE), lambda c, s: (0, (s[7] + c * heads) // per_group))
    return pl.pallas_call(
        functools.partial(ssm_outputs_kernel, hops=len(received)),
        grid_spec=pltpu.PrefetchScalarGridSpec(
            num_scalar_prefetch=1,
            grid=(chunks,),
            in_specs=[
                per_chunk,
                per_chunk,
                grouped,
                grouped,
                pl.BlockSpec((1, heads, tok), lambda c, s: (c, 0, 0)),
                pl.BlockSpec((1, heads, tok), lambda c, s: (c, 0, 0)),
                pl.BlockSpec((1, 8, width), lambda c, s: (c, 0, 0)),
                pl.BlockSpec((1, width), lambda c, s: (0, c)),
            ]
            + [anywhere] * (1 + len(received)),
            out_specs=per_chunk,
            scratch_shapes=[
                pltpu.VMEM((chunks, N_STATE, width), BF16),
                pltpu.VMEM(ssm_init.shape, F32),
                pltpu.SemaphoreType.DMA((chunks,)),
                pltpu.SemaphoreType.DMA,
            ],
        ),
        out_shape=jax.ShapeDtypeStruct((tok, lanes), BF16),
        compiler_params=pltpu.CompilerParams(vmem_limit_bytes=VMEM_LIMIT),
        cost_estimate=pl.CostEstimate(
            flops=2 * tok * lanes * N_STATE * 8, bytes_accessed=6 << 20, transcendentals=1 << 21
        ),
        name="ssm_outputs",
    )(scalars, x_in, z_gate, b_in, c_in, logt, dtt, rows, norm_weight[None, :], ssm_init,
      *received)


def attend_kernel(scalars, q_ref, *rest, kv_head, kv_count, heads, hops, use_cache, use_window,
                  carry_in, final, slots, alias):
    rest = list(rest)
    take = lambda n: [rest.pop(0) for _ in range(n)]
    keys_near, keys_far, values_near, values_far = take(4) if use_cache else [None] * 4
    window = take(hops + 1) if use_window else []
    acc_in, best_in, total_in = take(3) if carry_in else [None] * 3
    if alias:
        take(1)
    outs = take(1 if final else 3)
    k_buf, v_buf, s_buf, best_buf, total_buf, acc_buf, sems = rest
    place, dp, first_block, cache_blocks, newest, held = (scalars[k] for k in range(6))
    column = scalars[6]
    tok = q_ref.shape[0]
    half = slots // 2
    base = slots if use_cache else 0
    double = 2 * KEY_BLOCK

    key_copies, value_copies = [], []

    def add(group, source, target):
        sem = sems.at[len(key_copies) + len(value_copies)]
        group.append(pltpu.make_async_copy(source, target, sem))

    if use_cache:
        near = pl.ds(pl.multiple_of(dp * half, half), half)
        far = pl.ds(pl.multiple_of((1 - dp) * half, half), half)
        lanes = pl.ds(pl.multiple_of((column + kv_head) * HD, HD), HD)
        add(key_copies, keys_near.at[:, lanes], k_buf.at[near])
        add(key_copies, keys_far.at[:, lanes], k_buf.at[far])
        add(value_copies, values_near.at[:, lanes], v_buf.at[near])
        add(value_copies, values_far.at[:, lanes], v_buf.at[far])
    for k, ref in enumerate(window):
        rows = pl.ds(base + k * tok, tok)
        at = kv_head * HD
        add(key_copies, ref.at[:, at : at + HD], k_buf.at[rows])
        at = (kv_count + kv_head) * HD
        add(value_copies, ref.at[:, at : at + HD], v_buf.at[rows])
    for copy in key_copies + value_copies:
        copy.start()
    if use_window:
        loose = (hops + 1) * tok
        padded = -(-loose // double) * double
        if padded > loose:
            for buf in (k_buf, v_buf):
                buf[base + loose : base + padded, :] = jnp.zeros((padded - loose, HD), BF16)
    cache_total = slots // KEY_BLOCK
    window_pairs = (place * tok + tok + double - 1) // double
    lane = lax.broadcasted_iota(jnp.int32, (1, KEY_BLOCK), 1)

    def cache_offset(j):
        return pl.multiple_of(lax.rem(first_block + j, cache_total) * KEY_BLOCK, KEY_BLOCK)

    def cache_bias(offset):
        age = newest - (offset + lane)
        age = jnp.where(age < 0, age + slots, age)
        return jnp.where(age < held, 0.0, NEG)

    def score(offset, bias_of):
        span = pl.ds(offset, KEY_BLOCK)
        for h in range(heads):
            rows = slice(h * tok, (h + 1) * tok)
            scores = mm_nt(q_ref[:, h * HD : (h + 1) * HD], k_buf[span, :])
            scores = scores * LOG2_SCALE + bias_of
            s_buf[rows, span] = scores
            best_buf[rows, :] = jnp.maximum(best_buf[rows, :], fold_lanes(scores, jnp.maximum))

    def mix(offset):
        span = pl.ds(offset, KEY_BLOCK)
        for h in range(heads):
            rows = slice(h * tok, (h + 1) * tok)
            best = best_buf[rows, :]
            probs = jnp.concatenate(
                [
                    jnp.exp2(s_buf[rows, pl.ds(offset + k, 128)] - best)
                    for k in range(0, KEY_BLOCK, 128)
                ],
                axis=1,
            )
            total_buf[rows, :] += fold_lanes(probs, jnp.add)
            acc_buf[rows, :] += mm(probs.astype(BF16), v_buf[span, :])

    def sweep(cache_visit, window_visit):
        if use_cache:
            def both(j, unused):
                cache_visit(2 * j)
                cache_visit(2 * j + 1)
                return 0

            lax.fori_loop(0, cache_blocks // 2, both, 0)

            @pl.when(cache_blocks % 2 == 1)
            def _():
                cache_visit(cache_blocks - 1)
        if use_window:
            window_visit(base, 0)
            window_visit(base + KEY_BLOCK, 1)

            def more(j, unused):
                for k in range(2):
                    at = 2 * j + k
                    window_visit(pl.multiple_of(base + at * KEY_BLOCK, KEY_BLOCK), at)
                return 0

            lax.fori_loop(1, window_pairs, more, 0)

    def cache_score(j):
        offset = cache_offset(j)
        score(offset, cache_bias(offset))

    def window_score(offset, at):
        if isinstance(at, int) and at * KEY_BLOCK < tok:
            later = (
                lax.broadcasted_iota(jnp.int32, (tok, KEY_BLOCK), 0)
                - lax.broadcasted_iota(jnp.int32, (tok, KEY_BLOCK), 1)
            )
            allowed = (later >= 0) | ((lane >= tok) & (lane < tok * (place + 1)))
        else:
            allowed = lane + at * KEY_BLOCK < tok * (place + 1)
        score(offset, jnp.where(allowed, 0.0, NEG))

    best_buf[...] = best_in[...] if carry_in else jnp.full_like(best_buf, NEG)
    for copy in key_copies:
        copy.wait()
    sweep(cache_score, window_score)
    best = jnp.broadcast_to(jnp.max(best_buf[...], axis=-1, keepdims=True), best_buf.shape)
    best_buf[...] = best
    if carry_in:
        factor = jnp.exp2(best_in[...] - best)
        acc_buf[...] = factor * acc_in[...]
        total_buf[...] = factor * total_in[...]
    else:
        acc_buf[...] = jnp.zeros_like(acc_buf)
        total_buf[...] = jnp.zeros_like(total_buf)
    for copy in value_copies:
        copy.wait()
    sweep(lambda j: mix(cache_offset(j)), lambda offset, at: mix(offset))
    if final:
        for h in range(heads):
            rows = slice(h * tok, (h + 1) * tok)
            total = jnp.sum(total_buf[rows, :], axis=-1, keepdims=True)
            outs[0][:, h * HD : (h + 1) * HD] = (acc_buf[rows, :] / total).astype(BF16)
    else:
        outs[0][...] = acc_buf[...]
        outs[1][...] = best_buf[...]
        outs[2][...] = total_buf[...]


def attend(scalars, queries, head, heads, kv_count, cache=None, window=None, carry=None, into=None,
           final=True):
    tok = queries.shape[0]
    kv_head = head // (AH // KVH)
    slots = 2 * cache[0].shape[0] if cache is not None else 0
    hops = len(window) - 1 if window is not None else 0
    rows = heads * tok
    depth = slots
    if window is not None:
        depth += -(-((hops + 1) * tok) // (2 * KEY_BLOCK)) * (2 * KEY_BLOCK)
    anywhere = pl.BlockSpec(memory_space=pl.ANY)
    whole = pl.BlockSpec((rows, 128), lambda k, s: (0, 0))
    part = pl.BlockSpec((tok, heads * HD), lambda k, s: (0, head // heads))
    operands = [scalars, queries]
    in_specs = [part]
    for group in (cache, window):
        if group is not None:
            operands += list(group)
            in_specs += [anywhere] * len(group)
    if carry is not None:
        operands += list(carry)
        in_specs += [whole] * 3
    aliases = {}
    if into is not None:
        aliases = {len(operands): 0}
        operands.append(into)
        in_specs.append(anywhere)
    if final:
        out_specs, out_shape = part, jax.ShapeDtypeStruct(queries.shape, BF16)
    else:
        out_specs, out_shape = [whole] * 3, [jax.ShapeDtypeStruct((rows, 128), F32)] * 3
    keys_read = slots + (hops + 1) * tok * (window is not None)
    return pl.pallas_call(
        functools.partial(
            attend_kernel, kv_head=kv_head, kv_count=kv_count, heads=heads, hops=hops,
            use_cache=cache is not None, use_window=window is not None, carry_in=carry is not None,
            final=final, slots=slots, alias=into is not None,
        ),
        grid_spec=pltpu.PrefetchScalarGridSpec(
            num_scalar_prefetch=1,
            grid=(1,),
            in_specs=in_specs,
            out_specs=out_specs,
            scratch_shapes=[
                pltpu.VMEM((depth, HD), BF16),
                pltpu.VMEM((depth, HD), BF16),
                pltpu.VMEM((rows, depth), F32),
                pltpu.VMEM((rows, 128), F32),
                pltpu.VMEM((rows, 128), F32),
                pltpu.VMEM((rows, 128), F32),
                pltpu.SemaphoreType.DMA((4 + 2 * (hops + 1),)),
            ],
        ),
        out_shape=out_shape,
        input_output_aliases=aliases,
        compiler_params=pltpu.CompilerParams(vmem_limit_bytes=VMEM_LIMIT),
        cost_estimate=pl.CostEstimate(
            flops=16 * rows * keys_read * HD, bytes_accessed=4 * keys_read * HD,
            transcendentals=rows * keys_read,
        ),
        name="attend",
    )(*operands)


def tie(*values):
    return lax.optimization_barrier(values)


def local(x_in, z_gate, b_in, c_in, dt_raw, dt_bias, a_log, d_skip, norm_weight, ssm_init, queries,
          keys, values, cache_keys, cache_values, window_start, prefix_len):
    tok, lanes = x_in.shape
    head_count = dt_raw.shape[1]
    per_group = MH // NG
    places = lax.axis_size("seq")
    place = lax.axis_index("seq")
    dp = lax.axis_index("dp")
    q_count = queries.shape[1] // HD
    kv_here = keys.shape[1] // HD
    kv_count = max(1, q_count * KVH // AH)
    width = 2 * kv_count * HD
    chunks = lanes // width
    column = (dp * q_count) // (AH // KVH)
    slots = 2 * cache_keys.shape[0]

    ring = [(k, (k + 1) % places) for k in range(places)]
    swap = [(0, 1), (1, 0)]
    far_keys = lax.ppermute(cache_keys, "dp", swap)
    far_values = lax.ppermute(cache_values, "dp", swap)

    own_rows = jnp.concatenate(
        [
            lax.dynamic_slice_in_dim(array, column * HD, kv_count * HD, axis=1)
            for array in (keys, values)
        ],
        axis=1,
    )

    newest = jnp.mod(window_start[0] - 1, slots)
    held = prefix_len[0]
    oldest = jnp.mod(newest - held + 1, slots)
    first_block = oldest // KEY_BLOCK
    cache_blocks = jnp.minimum(
        slots // KEY_BLOCK, (oldest % KEY_BLOCK + held + KEY_BLOCK - 1) // KEY_BLOCK
    )
    first_head = dp * head_count
    scalars = jnp.stack(
        [place, dp, first_block, cache_blocks, newest, held, column, first_head]
    ).astype(jnp.int32)

    received = []
    send = own_rows
    arrived = lax.ppermute(send, "seq", ring)
    x_tied, send = tie(x_in, send)
    span = max(width, min(lanes, per_group * MP))
    states, rows, logt, dtt = ssm_states(
        scalars, x_tied, b_in, dt_raw, dt_bias, a_log, d_skip, ssm_init, width, span
    )
    received.append(arrived)

    cache = (cache_keys, far_keys, cache_values, far_values)
    heads = min(4, q_count)
    parts = list(range(0, q_count, heads))
    last_step = places - 1 + chunks - 1
    window_ready = places - 1
    result = None
    partial = None
    jobs = []
    if len(parts) > 1:
        jobs.append(("open", parts[0]))
        jobs += [("full", head) for head in parts[1:]]
        jobs.append(("close", parts[0]))
    else:
        jobs.append(("full", parts[0]))

    def run(job, queries_now):
        nonlocal result, partial
        kind, head = job
        if kind == "open":
            partial = attend(scalars, queries_now, head, heads, kv_count, cache=cache, final=False)
            return partial[0]
        window = [own_rows] + received[: places - 1]
        if kind == "full":
            result = attend(
                scalars, queries_now, head, heads, kv_count, cache=cache, window=window, into=result
            )
        else:
            result = attend(
                scalars, queries_now, head, heads, kv_count, window=window, carry=partial,
                into=result,
            )
        return result

    done = states
    for step in range(1, last_step + 1):
        incoming, tied = tie(received[-1], done)
        if done is states:
            states = tied
        elif done is result:
            result = tied
        done = tied
        send = hop(place, incoming, states, rows, step)
        arrived = lax.ppermute(send, "seq", ring)
        queries_now, send = tie(queries, send)
        ready = jobs and (jobs[0][0] == "open" or step >= window_ready)
        if ready:
            done = run(jobs.pop(0), queries_now)
        received.append(arrived)
    for job in jobs:
        run(job, queries)
    mamba_out = ssm_outputs(
        scalars, x_in, z_gate, b_in, c_in, logt, dtt, rows, norm_weight, ssm_init, received, width,
    )
    return (mamba_out, result)


def solution(mesh):
    rows = P(("groups", "seq"), ("tp", "dp"))
    shared = P(("groups", "seq"), "tp")
    heads = P(("tp", "dp"))
    cached = P(("groups", "dp"), "tp")
    return jax.shard_map(
        local,
        mesh=mesh,
        in_specs=(
            rows, rows, shared, shared, rows, heads, heads, heads, heads,
            P(("groups", "tp", "dp"), None, None), rows, shared, shared, cached, cached,
            P("groups"), P("groups"),
        ),
        out_specs=(rows, rows),
        check_vma=False,
    )
```

```python
import functools
import math

import jax
import jax.numpy as jnp
from jax import lax
from jax.experimental import pallas as pl
from jax.experimental.pallas import tpu as pltpu
from jax.sharding import PartitionSpec as P

MH = 128
MP = 64
N_STATE = 256
NG = 8
AH = 64
KVH = 8
HD = 128
BLOCK = 128
KEY_BLOCK = 512
LOG2_SCALE = math.log2(math.e) / math.sqrt(HD)
NEG = -1e30
F32 = jnp.float32
BF16 = jnp.bfloat16
VMEM_LIMIT = 56 << 20


def mm(a, b):
    return jnp.dot(a, b, preferred_element_type=F32)


def mm_nt(a, b):
    return lax.dot_general(a, b, (((1,), (1,)), ((), ())), preferred_element_type=F32)


def pieces_of(value):
    first = value.astype(BF16)
    rest = value - first.astype(F32)
    second = rest.astype(BF16)
    third = (rest - second.astype(F32)).astype(BF16)
    return first, second, third


def head_table(heads, width):
    row = lax.broadcasted_iota(jnp.int32, (heads, width), 0)
    lane = lax.broadcasted_iota(jnp.int32, (heads, width), 1)
    table = jnp.where(lane // MP == row, 1.0, 0.0).astype(BF16)
    return jnp.concatenate([table] * 3, axis=0)


def expand(value, table):
    stacked = jnp.concatenate(pieces_of(value), axis=0)
    return lax.dot_general(stacked, table, (((0,), (0,)), ((), ())), preferred_element_type=F32)


def fold_lanes(value, op):
    parts = [value[:, k : k + 128] for k in range(0, value.shape[1], 128)]
    while len(parts) > 1:
        parts = [
            op(parts[k], parts[k + 1]) if k + 1 < len(parts) else parts[k]
            for k in range(0, len(parts), 2)
        ]
    return parts[0]


def ssm_states_kernel(
    scalars, x_ref, b_ref, dt_ref, bias_ref, alog_ref, dskip_ref, init_ref,
    state_ref, rows_ref, logt_ref, dtt_ref, dt_all, log_all, skip_all,
):
    span = pl.program_id(0)
    tok, lanes = x_ref.shape
    heads = lanes // MP
    spans = dt_ref.shape[0] // heads
    parts = state_ref.shape[0]
    width = lanes // parts

    @pl.when(span == 0)
    def _():
        column = lambda ref: jnp.broadcast_to(ref[...], (8, ref.shape[1])).T[:, 0:1]
        dt = jax.nn.softplus(dt_ref[...] + column(bias_ref))
        decay = -jnp.exp(column(alog_ref)) * dt
        row = lax.broadcasted_iota(jnp.int32, (BLOCK, BLOCK), 0)
        col = lax.broadcasted_iota(jnp.int32, (BLOCK, BLOCK), 1)
        upper = jnp.where(row <= col, 1.0, 0.0).astype(BF16)
        logs = []
        for blk in range(tok // BLOCK):
            first, second, third = pieces_of(decay[:, blk * BLOCK : (blk + 1) * BLOCK])
            logs.append(mm(first, upper) + mm(second, upper) + mm(third, upper))
        logs = jnp.concatenate(logs, axis=1)
        skip = jnp.broadcast_to(column(dskip_ref), (dt_ref.shape[0], 128))
        for k in range(spans):
            dt_all[k] = dt[k * heads : (k + 1) * heads]
            log_all[k] = logs[k * heads : (k + 1) * heads]
            skip_all[k] = skip[k * heads : (k + 1) * heads]

    dt = dt_all[span]
    logs = log_all[span]
    few = heads // parts
    for k in range(parts):
        logt_ref[k] = logs[k * few : (k + 1) * few]
        dtt_ref[k] = dt[k * few : (k + 1) * few]
    table = head_table(heads, lanes)
    state = None
    total = jnp.zeros((heads, 1), F32)
    for blk in range(tok // BLOCK):
        part = slice(blk * BLOCK, (blk + 1) * BLOCK)
        end = logs[:, (blk + 1) * BLOCK - 1 : (blk + 1) * BLOCK]
        tail = jnp.exp(end - logs[:, part]) * dt[:, part]
        weighted = (expand(tail, table) * x_ref[part, :].astype(F32)).astype(BF16)
        update = mm(b_ref[part, :].T, weighted)
        if state is None:
            state = update
        else:
            state = expand(jnp.broadcast_to(jnp.exp(end), (heads, 8)), table)[0:1] * state + update
        total = total + end
    place = scalars[0]
    lane = lax.broadcasted_iota(jnp.int32, (heads, 8), 1)
    rows = expand(jnp.where(lane == 0, jnp.exp(total), skip_all[span][:, 0:8]), table)
    for k in range(parts):
        state_ref[k] = state[:, k * width : (k + 1) * width]
        rows_ref[k] = rows[:, k * width : (k + 1) * width]

    @pl.when(place == 0)
    def _():
        for k in range(parts):
            first = init_ref[k * few : (k + 1) * few].reshape(width, N_STATE).T
            state_ref[k] = state_ref[k] + rows_ref[k, 0:1, :] * first
            rows_ref[k, 0:1, :] = jnp.zeros((1, width), F32)


def ssm_states(scalars, x_in, b_in, dt_raw, dt_bias, a_log, d_skip, ssm_init, width, span):
    tok, lanes = x_in.shape
    chunks = lanes // width
    head_count = dt_raw.shape[1]
    heads = span // MP
    few = width // MP
    parts = span // width
    per_group = MH // NG
    flat = lambda c, s: (0, 0)
    major = lambda c, s: (c, 0, 0)
    return pl.pallas_call(
        ssm_states_kernel,
        grid_spec=pltpu.PrefetchScalarGridSpec(
            num_scalar_prefetch=1,
            grid=(lanes // span,),
            in_specs=[
                pl.BlockSpec((tok, span), lambda c, s: (0, c)),
                pl.BlockSpec((tok, N_STATE), lambda c, s: (0, (s[7] + c * heads) // per_group)),
                pl.BlockSpec((head_count, tok), flat),
                pl.BlockSpec((1, head_count), flat),
                pl.BlockSpec((1, head_count), flat),
                pl.BlockSpec((1, head_count), flat),
                pl.BlockSpec((heads, MP, N_STATE), major),
            ],
            out_specs=[
                pl.BlockSpec((parts, N_STATE, width), major),
                pl.BlockSpec((parts, 8, width), major),
                pl.BlockSpec((parts, few, tok), major),
                pl.BlockSpec((parts, few, tok), major),
            ],
            scratch_shapes=[
                pltpu.VMEM((lanes // span, heads, tok), F32),
                pltpu.VMEM((lanes // span, heads, tok), F32),
                pltpu.VMEM((lanes // span, heads, 128), F32),
            ],
        ),
        out_shape=[
            jax.ShapeDtypeStruct((chunks, N_STATE, width), F32),
            jax.ShapeDtypeStruct((chunks, 8, width), F32),
            jax.ShapeDtypeStruct((chunks, few, tok), F32),
            jax.ShapeDtypeStruct((chunks, few, tok), F32),
        ],
        compiler_params=pltpu.CompilerParams(vmem_limit_bytes=VMEM_LIMIT),
        cost_estimate=pl.CostEstimate(
            flops=2 * tok * lanes * N_STATE * 4, bytes_accessed=6 << 20, transcendentals=1 << 16
        ),
        name="ssm_states",
    )(
        scalars, x_in, b_in, dt_raw.T, dt_bias[None, :], a_log[None, :], d_skip[None, :], ssm_init
    )


def hop(place, received, states, rows, step):
    chunks = states.shape[0]
    chunk = jnp.clip(step - 1 - place, 0, chunks - 1)
    state = lax.dynamic_index_in_dim(states, chunk, 0, keepdims=False)
    decay = lax.dynamic_index_in_dim(rows, chunk, 0, keepdims=False)[0:1, :]
    combined = (decay * received.astype(F32) + state).astype(BF16)
    return jnp.where(step <= place, received, combined)


def ssm_inner_kernel(scalars, x_ref, b_ref, c_ref, logt_ref, dtt_ref, rows_ref, out_ref):
    tok, width = x_ref.shape
    heads = width // MP
    row = lax.broadcasted_iota(jnp.int32, (BLOCK, BLOCK), 0)
    col = lax.broadcasted_iota(jnp.int32, (BLOCK, BLOCK), 1)
    lower = row >= col
    low_half = col < MP
    table = head_table(heads, width)
    logt = logt_ref[0]
    dtt = dtt_ref[0]
    logs = logt.T
    skip = rows_ref[0, 1:2, :]
    state = None
    pairs = heads // 2
    for blk in range(tok // BLOCK):
        part = slice(blk * BLOCK, (blk + 1) * BLOCK)
        c_blk = c_ref[part, :]
        b_blk = b_ref[part, :]
        x_blk = x_ref[part, :]
        products = mm_nt(c_blk, b_blk)
        log_blk = logs[part]
        kernels = []
        for h in range(heads):
            spread = log_blk[:, h : h + 1] - logt[h : h + 1, part]
            decay = jnp.exp(jnp.where(lower, spread, NEG))
            kernels.append((decay * products * dtt[h : h + 1, part]).astype(BF16))
        carried = None
        if state is not None:
            carried = expand(jnp.exp(logt[:, part]), table) * mm(c_blk, state.astype(BF16))
        if (blk + 1) * BLOCK < tok:
            end = logt[:, (blk + 1) * BLOCK - 1 : (blk + 1) * BLOCK]
            tail = jnp.exp(end - logt[:, part]) * dtt[:, part]
            weighted = (expand(tail, table) * x_blk.astype(F32)).astype(BF16)
            update = mm(b_blk.T, weighted)
            if state is None:
                state = update
            else:
                factor = expand(jnp.broadcast_to(jnp.exp(end), (heads, 8)), table)[0:1]
                state = factor * state + update
        for pair in range(pairs):
            lanes = slice(pair * 128, (pair + 1) * 128)
            x_pair = x_blk[:, lanes]
            zero = jnp.zeros_like(x_pair)
            stacked = jnp.concatenate(
                [jnp.where(low_half, x_pair, zero), jnp.where(low_half, zero, x_pair)], axis=0
            )
            inner = mm(jnp.concatenate(kernels[2 * pair : 2 * pair + 2], axis=1), stacked)
            value = inner + skip[:, lanes] * x_pair.astype(F32)
            if carried is not None:
                value = value + carried[:, lanes]
            out_ref[part, lanes] = value


def ssm_inner(scalars, x_in, b_in, c_in, logt, dtt, rows, width):
    tok, lanes = x_in.shape
    chunks = lanes // width
    heads = width // MP
    per_group = MH // NG
    per_chunk = pl.BlockSpec((tok, width), lambda c, s: (0, c))
    grouped = pl.BlockSpec((tok, N_STATE), lambda c, s: (0, (s[7] + c * heads) // per_group))
    major = lambda c, s: (c, 0, 0)
    return pl.pallas_call(
        ssm_inner_kernel,
        grid_spec=pltpu.PrefetchScalarGridSpec(
            num_scalar_prefetch=1,
            grid=(chunks,),
            in_specs=[
                per_chunk,
                grouped,
                grouped,
                pl.BlockSpec((1, heads, tok), major),
                pl.BlockSpec((1, heads, tok), major),
                pl.BlockSpec((1, 8, width), major),
            ],
            out_specs=per_chunk,
        ),
        out_shape=jax.ShapeDtypeStruct((tok, lanes), F32),
        compiler_params=pltpu.CompilerParams(vmem_limit_bytes=VMEM_LIMIT),
        cost_estimate=pl.CostEstimate(
            flops=2 * tok * lanes * N_STATE * 8, bytes_accessed=6 << 20, transcendentals=1 << 21
        ),
        name="ssm_inner",
    )(scalars, x_in, b_in, c_in, logt, dtt, rows)


def ssm_outputs_kernel(
    scalars, inner_ref, z_ref, c_ref, logt_ref, norm_ref, init_hbm, *rest, hops,
):
    received = rest[:hops]
    out_ref, carry, init_buf, sems, init_sem = rest[hops:]
    chunk = pl.program_id(0)
    place = scalars[0]
    tok, width = inner_ref.shape
    heads = width // MP
    count = carry.shape[0]

    @pl.when(chunk == 0)
    def _():
        for k in range(count):
            for r in range(hops):
                @pl.when((place > 0) & (place + k == r))
                def _():
                    pltpu.make_async_copy(received[r], carry.at[k], sems.at[k]).start()

        @pl.when(place == 0)
        def _():
            whole = pltpu.make_async_copy(init_hbm, init_buf, init_sem)
            whole.start()
            whole.wait()
            for k in range(count):
                first = init_buf[k * heads : (k + 1) * heads].reshape(width, N_STATE)
                carry[k] = first.astype(BF16).T

    @pl.when(place > 0)
    def _():
        pltpu.make_async_copy(received[0], carry.at[chunk], sems.at[chunk]).wait()

    row = lax.broadcasted_iota(jnp.int32, (BLOCK, BLOCK), 0)
    col = lax.broadcasted_iota(jnp.int32, (BLOCK, BLOCK), 1)
    mean_table = jnp.where(row // MP == col // MP, 1.0 / MP, 0.0).astype(BF16)
    mean_table = jnp.concatenate([mean_table, mean_table], axis=0)
    table = head_table(heads, width)
    logt = logt_ref[0]
    whole_logs = []
    before = jnp.zeros((heads, 1), F32)
    for blk in range(tok // BLOCK):
        part = slice(blk * BLOCK, (blk + 1) * BLOCK)
        whole_logs.append(jnp.exp(logt[:, part] + before))
        before = before + logt[:, (blk + 1) * BLOCK - 1 : (blk + 1) * BLOCK]
    carried = expand(jnp.concatenate(whole_logs, axis=1), table) * mm(c_ref[...], carry[chunk])
    z = z_ref[...].astype(F32)
    gated = (inner_ref[...] + carried) * (z / (1.0 + jnp.exp(-z)))
    square = gated * gated
    high = square.astype(BF16)
    low = (square - high.astype(F32)).astype(BF16)
    for at in range(0, width, 128):
        lanes = slice(at, at + 128)
        mean = mm(jnp.concatenate([high[:, lanes], low[:, lanes]], axis=1), mean_table)
        normed = gated[:, lanes] * lax.rsqrt(mean + 1e-05) * norm_ref[:, lanes]
        out_ref[:, lanes] = normed.astype(BF16)


def ssm_outputs(scalars, inner, z_gate, c_in, logt, norm_weight, ssm_init, received, width):
    tok, lanes = inner.shape
    chunks = lanes // width
    heads = width // MP
    per_group = MH // NG
    anywhere = pl.BlockSpec(memory_space=pl.ANY)
    per_chunk = pl.BlockSpec((tok, width), lambda c, s: (0, c))
    grouped = pl.BlockSpec((tok, N_STATE), lambda c, s: (0, (s[7] + c * heads) // per_group))
    return pl.pallas_call(
        functools.partial(ssm_outputs_kernel, hops=len(received)),
        grid_spec=pltpu.PrefetchScalarGridSpec(
            num_scalar_prefetch=1,
            grid=(chunks,),
            in_specs=[
                per_chunk,
                per_chunk,
                grouped,
                pl.BlockSpec((1, heads, tok), lambda c, s: (c, 0, 0)),
                pl.BlockSpec((1, width), lambda c, s: (0, c)),
            ]
            + [anywhere] * (1 + len(received)),
            out_specs=per_chunk,
            scratch_shapes=[
                pltpu.VMEM((chunks, N_STATE, width), BF16),
                pltpu.VMEM(ssm_init.shape, F32),
                pltpu.SemaphoreType.DMA((chunks,)),
                pltpu.SemaphoreType.DMA,
            ],
        ),
        out_shape=jax.ShapeDtypeStruct((tok, lanes), BF16),
        compiler_params=pltpu.CompilerParams(vmem_limit_bytes=VMEM_LIMIT),
        cost_estimate=pl.CostEstimate(
            flops=2 * tok * lanes * N_STATE * 2, bytes_accessed=6 << 20, transcendentals=1 << 20
        ),
        name="ssm_outputs",
    )(scalars, inner, z_gate, c_in, logt, norm_weight[None, :], ssm_init, *received)


def attend_kernel(scalars, q_ref, *rest, kv_head, kv_count, heads, hops, use_cache, use_window,
                  carry_in, final, slots, alias):
    rest = list(rest)
    take = lambda n: [rest.pop(0) for _ in range(n)]
    keys_near, keys_far, values_near, values_far = take(4) if use_cache else [None] * 4
    window = take(hops + 1) if use_window else []
    acc_in, best_in, total_in = take(3) if carry_in else [None] * 3
    if alias:
        take(1)
    outs = take(1 if final else 3)
    k_buf, v_buf, s_buf, best_buf, total_buf, acc_buf, sems = rest
    place, dp, first_block, cache_blocks, newest, held = (scalars[k] for k in range(6))
    column = scalars[6]
    tok = q_ref.shape[0]
    half = slots // 2
    base = slots if use_cache else 0
    double = 2 * KEY_BLOCK

    key_copies, value_copies = [], []

    def add(group, source, target):
        sem = sems.at[len(key_copies) + len(value_copies)]
        group.append(pltpu.make_async_copy(source, target, sem))

    if use_cache:
        near = pl.ds(pl.multiple_of(dp * half, half), half)
        far = pl.ds(pl.multiple_of((1 - dp) * half, half), half)
        lanes = pl.ds(pl.multiple_of((column + kv_head) * HD, HD), HD)
        add(key_copies, keys_near.at[:, lanes], k_buf.at[near])
        add(key_copies, keys_far.at[:, lanes], k_buf.at[far])
        add(value_copies, values_near.at[:, lanes], v_buf.at[near])
        add(value_copies, values_far.at[:, lanes], v_buf.at[far])
    for k, ref in enumerate(window):
        rows = pl.ds(base + k * tok, tok)
        at = kv_head * HD
        add(key_copies, ref.at[:, at : at + HD], k_buf.at[rows])
        at = (kv_count + kv_head) * HD
        add(value_copies, ref.at[:, at : at + HD], v_buf.at[rows])
    for copy in key_copies + value_copies:
        copy.start()
    if use_window:
        loose = (hops + 1) * tok
        padded = -(-loose // double) * double
        if padded > loose:
            for buf in (k_buf, v_buf):
                buf[base + loose : base + padded, :] = jnp.zeros((padded - loose, HD), BF16)
    cache_total = slots // KEY_BLOCK
    window_pairs = (place * tok + tok + double - 1) // double
    lane = lax.broadcasted_iota(jnp.int32, (1, KEY_BLOCK), 1)

    def cache_offset(j):
        return pl.multiple_of(lax.rem(first_block + j, cache_total) * KEY_BLOCK, KEY_BLOCK)

    def cache_bias(offset):
        age = newest - (offset + lane)
        age = jnp.where(age < 0, age + slots, age)
        return jnp.where(age < held, 0.0, NEG)

    def score(offset, bias_of):
        span = pl.ds(offset, KEY_BLOCK)
        for h in range(heads):
            rows = slice(h * tok, (h + 1) * tok)
            scores = mm_nt(q_ref[:, h * HD : (h + 1) * HD], k_buf[span, :])
            scores = scores * LOG2_SCALE + bias_of
            s_buf[rows, span] = scores
            best_buf[rows, :] = jnp.maximum(best_buf[rows, :], fold_lanes(scores, jnp.maximum))

    def mix(offset):
        span = pl.ds(offset, KEY_BLOCK)
        for h in range(heads):
            rows = slice(h * tok, (h + 1) * tok)
            best = best_buf[rows, :]
            probs = jnp.concatenate(
                [
                    jnp.exp2(s_buf[rows, pl.ds(offset + k, 128)] - best)
                    for k in range(0, KEY_BLOCK, 128)
                ],
                axis=1,
            )
            total_buf[rows, :] += fold_lanes(probs, jnp.add)
            acc_buf[rows, :] += mm(probs.astype(BF16), v_buf[span, :])

    def sweep(cache_visit, window_visit):
        if use_cache:
            def both(j, unused):
                cache_visit(2 * j)
                cache_visit(2 * j + 1)
                return 0

            lax.fori_loop(0, cache_blocks // 2, both, 0)

            @pl.when(cache_blocks % 2 == 1)
            def _():
                cache_visit(cache_blocks - 1)
        if use_window:
            window_visit(base, 0)
            window_visit(base + KEY_BLOCK, 1)

            def more(j, unused):
                for k in range(2):
                    at = 2 * j + k
                    window_visit(pl.multiple_of(base + at * KEY_BLOCK, KEY_BLOCK), at)
                return 0

            lax.fori_loop(1, window_pairs, more, 0)

    def cache_score(j):
        offset = cache_offset(j)
        score(offset, cache_bias(offset))

    def window_score(offset, at):
        if isinstance(at, int) and at * KEY_BLOCK < tok:
            later = (
                lax.broadcasted_iota(jnp.int32, (tok, KEY_BLOCK), 0)
                - lax.broadcasted_iota(jnp.int32, (tok, KEY_BLOCK), 1)
            )
            allowed = (later >= 0) | ((lane >= tok) & (lane < tok * (place + 1)))
        else:
            allowed = lane + at * KEY_BLOCK < tok * (place + 1)
        score(offset, jnp.where(allowed, 0.0, NEG))

    best_buf[...] = best_in[...] if carry_in else jnp.full_like(best_buf, NEG)
    for copy in key_copies:
        copy.wait()
    sweep(cache_score, window_score)
    best = jnp.broadcast_to(jnp.max(best_buf[...], axis=-1, keepdims=True), best_buf.shape)
    best_buf[...] = best
    if carry_in:
        factor = jnp.exp2(best_in[...] - best)
        acc_buf[...] = factor * acc_in[...]
        total_buf[...] = factor * total_in[...]
    else:
        acc_buf[...] = jnp.zeros_like(acc_buf)
        total_buf[...] = jnp.zeros_like(total_buf)
    for copy in value_copies:
        copy.wait()
    sweep(lambda j: mix(cache_offset(j)), lambda offset, at: mix(offset))
    if final:
        for h in range(heads):
            rows = slice(h * tok, (h + 1) * tok)
            total = jnp.sum(total_buf[rows, :], axis=-1, keepdims=True)
            outs[0][:, h * HD : (h + 1) * HD] = (acc_buf[rows, :] / total).astype(BF16)
    else:
        outs[0][...] = acc_buf[...]
        outs[1][...] = best_buf[...]
        outs[2][...] = total_buf[...]


def attend(scalars, queries, head, heads, kv_count, cache=None, window=None, carry=None, into=None,
           final=True):
    tok = queries.shape[0]
    kv_head = head // (AH // KVH)
    slots = 2 * cache[0].shape[0] if cache is not None else 0
    hops = len(window) - 1 if window is not None else 0
    rows = heads * tok
    depth = slots
    if window is not None:
        depth += -(-((hops + 1) * tok) // (2 * KEY_BLOCK)) * (2 * KEY_BLOCK)
    anywhere = pl.BlockSpec(memory_space=pl.ANY)
    whole = pl.BlockSpec((rows, 128), lambda k, s: (0, 0))
    part = pl.BlockSpec((tok, heads * HD), lambda k, s: (0, head // heads))
    operands = [scalars, queries]
    in_specs = [part]
    for group in (cache, window):
        if group is not None:
            operands += list(group)
            in_specs += [anywhere] * len(group)
    if carry is not None:
        operands += list(carry)
        in_specs += [whole] * 3
    aliases = {}
    if into is not None:
        aliases = {len(operands): 0}
        operands.append(into)
        in_specs.append(anywhere)
    if final:
        out_specs, out_shape = part, jax.ShapeDtypeStruct(queries.shape, BF16)
    else:
        out_specs, out_shape = [whole] * 3, [jax.ShapeDtypeStruct((rows, 128), F32)] * 3
    keys_read = slots + (hops + 1) * tok * (window is not None)
    return pl.pallas_call(
        functools.partial(
            attend_kernel, kv_head=kv_head, kv_count=kv_count, heads=heads, hops=hops,
            use_cache=cache is not None, use_window=window is not None, carry_in=carry is not None,
            final=final, slots=slots, alias=into is not None,
        ),
        grid_spec=pltpu.PrefetchScalarGridSpec(
            num_scalar_prefetch=1,
            grid=(1,),
            in_specs=in_specs,
            out_specs=out_specs,
            scratch_shapes=[
                pltpu.VMEM((depth, HD), BF16),
                pltpu.VMEM((depth, HD), BF16),
                pltpu.VMEM((rows, depth), F32),
                pltpu.VMEM((rows, 128), F32),
                pltpu.VMEM((rows, 128), F32),
                pltpu.VMEM((rows, 128), F32),
                pltpu.SemaphoreType.DMA((4 + 2 * (hops + 1),)),
            ],
        ),
        out_shape=out_shape,
        input_output_aliases=aliases,
        compiler_params=pltpu.CompilerParams(vmem_limit_bytes=VMEM_LIMIT),
        cost_estimate=pl.CostEstimate(
            flops=16 * rows * keys_read * HD, bytes_accessed=4 * keys_read * HD,
            transcendentals=rows * keys_read,
        ),
        name="attend",
    )(*operands)


def tie(*values):
    return lax.optimization_barrier(values)


def local(x_in, z_gate, b_in, c_in, dt_raw, dt_bias, a_log, d_skip, norm_weight, ssm_init, queries,
          keys, values, cache_keys, cache_values, window_start, prefix_len):
    tok, lanes = x_in.shape
    head_count = dt_raw.shape[1]
    per_group = MH // NG
    places = lax.axis_size("seq")
    place = lax.axis_index("seq")
    dp = lax.axis_index("dp")
    q_count = queries.shape[1] // HD
    kv_here = keys.shape[1] // HD
    kv_count = max(1, q_count * KVH // AH)
    width = 2 * kv_count * HD
    chunks = lanes // width
    column = (dp * q_count) // (AH // KVH)
    slots = 2 * cache_keys.shape[0]

    ring = [(k, (k + 1) % places) for k in range(places)]
    swap = [(0, 1), (1, 0)]
    far_keys = lax.ppermute(cache_keys, "dp", swap)
    far_values = lax.ppermute(cache_values, "dp", swap)

    own_rows = jnp.concatenate(
        [
            lax.dynamic_slice_in_dim(array, column * HD, kv_count * HD, axis=1)
            for array in (keys, values)
        ],
        axis=1,
    )

    newest = jnp.mod(window_start[0] - 1, slots)
    held = prefix_len[0]
    oldest = jnp.mod(newest - held + 1, slots)
    first_block = oldest // KEY_BLOCK
    cache_blocks = jnp.minimum(
        slots // KEY_BLOCK, (oldest % KEY_BLOCK + held + KEY_BLOCK - 1) // KEY_BLOCK
    )
    first_head = dp * head_count
    scalars = jnp.stack(
        [place, dp, first_block, cache_blocks, newest, held, column, first_head]
    ).astype(jnp.int32)

    received = []
    send = own_rows
    arrived = lax.ppermute(send, "seq", ring)
    x_tied, send = tie(x_in, send)
    span = max(width, min(lanes, per_group * MP))
    states, rows, logt, dtt = ssm_states(
        scalars, x_tied, b_in, dt_raw, dt_bias, a_log, d_skip, ssm_init, width, span
    )
    received.append(arrived)

    cache = (cache_keys, far_keys, cache_values, far_values)
    heads = min(4, q_count)
    parts = list(range(0, q_count, heads))
    last_step = places - 1 + chunks - 1
    window_ready = places - 1
    result = None
    partial = None
    inner = None
    jobs = [("inner", 0)]
    if len(parts) > 1:
        jobs.append(("open", parts[0]))
        jobs += [("full", head) for head in parts[1:]]
        jobs.append(("close", parts[0]))
    else:
        jobs.append(("full", parts[0]))

    def run(job, queries_now):
        nonlocal result, partial, inner
        kind, head = job
        if kind == "inner":
            inner = ssm_inner(scalars, queries_now, b_in, c_in, logt, dtt, rows, width)
            return inner
        if kind == "open":
            partial = attend(scalars, queries_now, head, heads, kv_count, cache=cache, final=False)
            return partial[0]
        window = [own_rows] + received[: places - 1]
        if kind == "full":
            result = attend(
                scalars, queries_now, head, heads, kv_count, cache=cache, window=window, into=result
            )
        else:
            result = attend(
                scalars, queries_now, head, heads, kv_count, window=window, carry=partial,
                into=result,
            )
        return result

    done = states
    for step in range(1, last_step + 1):
        incoming, tied = tie(received[-1], done)
        if done is states:
            states = tied
        elif done is result:
            result = tied
        elif done is inner:
            inner = tied
        done = tied
        send = hop(place, incoming, states, rows, step)
        arrived = lax.ppermute(send, "seq", ring)
        ready = jobs and (jobs[0][0] in ("inner", "open") or step >= window_ready)
        if ready:
            job = jobs.pop(0)
            tied, send = tie(x_in if job[0] == "inner" else queries, send)
            done = run(job, tied)
        received.append(arrived)
    for job in jobs:
        run(job, queries)
    mamba_out = ssm_outputs(
        scalars, inner, z_gate, c_in, logt, norm_weight, ssm_init, received, width
    )
    return (mamba_out, result)


def solution(mesh):
    rows = P(("groups", "seq"), ("tp", "dp"))
    shared = P(("groups", "seq"), "tp")
    heads = P(("tp", "dp"))
    cached = P(("groups", "dp"), "tp")
    return jax.shard_map(
        local,
        mesh=mesh,
        in_specs=(
            rows, rows, shared, shared, rows, heads, heads, heads, heads,
            P(("groups", "tp", "dp"), None, None), rows, shared, shared, cached, cached,
            P("groups"), P("groups"),
        ),
        out_specs=(rows, rows),
        check_vma=False,
    )
```

```python
import functools
import math

import jax
import jax.numpy as jnp
from jax import lax
from jax.experimental import pallas as pl
from jax.experimental.pallas import tpu as pltpu
from jax.sharding import PartitionSpec as P

MH = 128
MP = 64
N_STATE = 256
NG = 8
AH = 64
KVH = 8
HD = 128
BLOCK = 128
KEY_BLOCK = 512
GROUPS = (4, 2, 1)
LOG2_SCALE = math.log2(math.e) / math.sqrt(HD)
NEG = -1e30
F32 = jnp.float32
BF16 = jnp.bfloat16
VMEM_LIMIT = 56 << 20


def mm(a, b):
    return jnp.dot(a, b, preferred_element_type=F32)


def mm_nt(a, b):
    return lax.dot_general(a, b, (((1,), (1,)), ((), ())), preferred_element_type=F32)


def pieces_of(value):
    first = value.astype(BF16)
    rest = value - first.astype(F32)
    second = rest.astype(BF16)
    third = (rest - second.astype(F32)).astype(BF16)
    return first, second, third


def head_table(heads, width):
    row = lax.broadcasted_iota(jnp.int32, (heads, width), 0)
    lane = lax.broadcasted_iota(jnp.int32, (heads, width), 1)
    table = jnp.where(lane // MP == row, 1.0, 0.0).astype(BF16)
    return jnp.concatenate([table] * 3, axis=0)


def expand(value, table):
    stacked = jnp.concatenate(pieces_of(value), axis=0)
    return lax.dot_general(stacked, table, (((0,), (0,)), ((), ())), preferred_element_type=F32)


def fold_lanes(value, op):
    parts = [value[:, k : k + 128] for k in range(0, value.shape[1], 128)]
    while len(parts) > 1:
        parts = [
            op(parts[k], parts[k + 1]) if k + 1 < len(parts) else parts[k]
            for k in range(0, len(parts), 2)
        ]
    return parts[0]


def ssm_states_kernel(
    scalars, x_ref, b_ref, dt_ref, bias_ref, alog_ref, dskip_ref, init_ref,
    state_ref, rows_ref, logt_ref, dtt_ref, dt_all, log_all, skip_all,
):
    span = pl.program_id(0)
    tok, lanes = x_ref.shape
    heads = lanes // MP
    spans = dt_ref.shape[0] // heads
    parts = state_ref.shape[0]
    width = lanes // parts

    @pl.when(span == 0)
    def _():
        column = lambda ref: jnp.broadcast_to(ref[...], (8, ref.shape[1])).T[:, 0:1]
        dt = jax.nn.softplus(dt_ref[...] + column(bias_ref))
        decay = -jnp.exp(column(alog_ref)) * dt
        row = lax.broadcasted_iota(jnp.int32, (BLOCK, BLOCK), 0)
        col = lax.broadcasted_iota(jnp.int32, (BLOCK, BLOCK), 1)
        upper = jnp.where(row <= col, 1.0, 0.0).astype(BF16)
        logs = []
        for blk in range(tok // BLOCK):
            first, second, third = pieces_of(decay[:, blk * BLOCK : (blk + 1) * BLOCK])
            logs.append(mm(first, upper) + mm(second, upper) + mm(third, upper))
        logs = jnp.concatenate(logs, axis=1)
        skip = jnp.broadcast_to(column(dskip_ref), (dt_ref.shape[0], 128))
        for k in range(spans):
            dt_all[k] = dt[k * heads : (k + 1) * heads]
            log_all[k] = logs[k * heads : (k + 1) * heads]
            skip_all[k] = skip[k * heads : (k + 1) * heads]

    dt = dt_all[span]
    logs = log_all[span]
    few = heads // parts
    for k in range(parts):
        logt_ref[k] = logs[k * few : (k + 1) * few]
        dtt_ref[k] = dt[k * few : (k + 1) * few]
    table = head_table(heads, lanes)
    state = None
    total = jnp.zeros((heads, 1), F32)
    for blk in range(tok // BLOCK):
        part = slice(blk * BLOCK, (blk + 1) * BLOCK)
        end = logs[:, (blk + 1) * BLOCK - 1 : (blk + 1) * BLOCK]
        tail = jnp.exp(end - logs[:, part]) * dt[:, part]
        weighted = (expand(tail, table) * x_ref[part, :].astype(F32)).astype(BF16)
        update = mm(b_ref[part, :].T, weighted)
        if state is None:
            state = update
        else:
            state = expand(jnp.broadcast_to(jnp.exp(end), (heads, 8)), table)[0:1] * state + update
        total = total + end
    place = scalars[0]
    lane = lax.broadcasted_iota(jnp.int32, (heads, 8), 1)
    rows = expand(jnp.where(lane == 0, jnp.exp(total), skip_all[span][:, 0:8]), table)
    for k in range(parts):
        state_ref[k] = state[:, k * width : (k + 1) * width]
        rows_ref[k] = rows[:, k * width : (k + 1) * width]

    @pl.when(place == 0)
    def _():
        for k in range(parts):
            first = init_ref[k * few : (k + 1) * few].reshape(width, N_STATE).T
            state_ref[k] = state_ref[k] + rows_ref[k, 0:1, :] * first
            rows_ref[k, 0:1, :] = jnp.zeros((1, width), F32)


def ssm_states(scalars, x_in, b_in, dt_raw, dt_bias, a_log, d_skip, ssm_init, width, span):
    tok, lanes = x_in.shape
    chunks = lanes // width
    head_count = dt_raw.shape[1]
    heads = span // MP
    few = width // MP
    parts = span // width
    per_group = MH // NG
    flat = lambda c, s: (0, 0)
    major = lambda c, s: (c, 0, 0)
    return pl.pallas_call(
        ssm_states_kernel,
        grid_spec=pltpu.PrefetchScalarGridSpec(
            num_scalar_prefetch=1,
            grid=(lanes // span,),
            in_specs=[
                pl.BlockSpec((tok, span), lambda c, s: (0, c)),
                pl.BlockSpec((tok, N_STATE), lambda c, s: (0, (s[7] + c * heads) // per_group)),
                pl.BlockSpec((head_count, tok), flat),
                pl.BlockSpec((1, head_count), flat),
                pl.BlockSpec((1, head_count), flat),
                pl.BlockSpec((1, head_count), flat),
                pl.BlockSpec((heads, MP, N_STATE), major),
            ],
            out_specs=[
                pl.BlockSpec((parts, N_STATE, width), major),
                pl.BlockSpec((parts, 8, width), major),
                pl.BlockSpec((parts, few, tok), major),
                pl.BlockSpec((parts, few, tok), major),
            ],
            scratch_shapes=[
                pltpu.VMEM((lanes // span, heads, tok), F32),
                pltpu.VMEM((lanes // span, heads, tok), F32),
                pltpu.VMEM((lanes // span, heads, 128), F32),
            ],
        ),
        out_shape=[
            jax.ShapeDtypeStruct((chunks, N_STATE, width), F32),
            jax.ShapeDtypeStruct((chunks, 8, width), F32),
            jax.ShapeDtypeStruct((chunks, few, tok), F32),
            jax.ShapeDtypeStruct((chunks, few, tok), F32),
        ],
        compiler_params=pltpu.CompilerParams(vmem_limit_bytes=VMEM_LIMIT),
        cost_estimate=pl.CostEstimate(
            flops=2 * tok * lanes * N_STATE * 4, bytes_accessed=6 << 20, transcendentals=1 << 16
        ),
        name="ssm_states",
    )(
        scalars, x_in, b_in, dt_raw.T, dt_bias[None, :], a_log[None, :], d_skip[None, :], ssm_init
    )


def hop(place, received, states, rows, step):
    chunks = states.shape[0]
    chunk = jnp.clip(step - 1 - place, 0, chunks - 1)
    state = lax.dynamic_index_in_dim(states, chunk, 0, keepdims=False)
    decay = lax.dynamic_index_in_dim(rows, chunk, 0, keepdims=False)[0:1, :]
    combined = (decay * received.astype(F32) + state).astype(BF16)
    return jnp.where(step <= place, received, combined)


def ssm_inner_kernel(scalars, x_ref, b_ref, c_ref, logt_ref, dtt_ref, rows_ref, out_ref):
    tok, width = x_ref.shape
    heads = width // MP
    row = lax.broadcasted_iota(jnp.int32, (BLOCK, BLOCK), 0)
    col = lax.broadcasted_iota(jnp.int32, (BLOCK, BLOCK), 1)
    lower = row >= col
    low_half = col < MP
    table = head_table(heads, width)
    logt = logt_ref[0]
    dtt = dtt_ref[0]
    logs = logt.T
    skip = rows_ref[0, 1:2, :]
    state = None
    pairs = heads // 2
    for blk in range(tok // BLOCK):
        part = slice(blk * BLOCK, (blk + 1) * BLOCK)
        c_blk = c_ref[part, :]
        b_blk = b_ref[part, :]
        x_blk = x_ref[part, :]
        products = mm_nt(c_blk, b_blk)
        log_blk = logs[part]
        kernels = []
        for h in range(heads):
            spread = log_blk[:, h : h + 1] - logt[h : h + 1, part]
            decay = jnp.exp(jnp.where(lower, spread, NEG))
            kernels.append((decay * products * dtt[h : h + 1, part]).astype(BF16))
        carried = None
        if state is not None:
            carried = expand(jnp.exp(logt[:, part]), table) * mm(c_blk, state.astype(BF16))
        if (blk + 1) * BLOCK < tok:
            end = logt[:, (blk + 1) * BLOCK - 1 : (blk + 1) * BLOCK]
            tail = jnp.exp(end - logt[:, part]) * dtt[:, part]
            weighted = (expand(tail, table) * x_blk.astype(F32)).astype(BF16)
            update = mm(b_blk.T, weighted)
            if state is None:
                state = update
            else:
                factor = expand(jnp.broadcast_to(jnp.exp(end), (heads, 8)), table)[0:1]
                state = factor * state + update
        for pair in range(pairs):
            lanes = slice(pair * 128, (pair + 1) * 128)
            x_pair = x_blk[:, lanes]
            zero = jnp.zeros_like(x_pair)
            stacked = jnp.concatenate(
                [jnp.where(low_half, x_pair, zero), jnp.where(low_half, zero, x_pair)], axis=0
            )
            inner = mm(jnp.concatenate(kernels[2 * pair : 2 * pair + 2], axis=1), stacked)
            value = inner + skip[:, lanes] * x_pair.astype(F32)
            if carried is not None:
                value = value + carried[:, lanes]
            out_ref[part, lanes] = value


def ssm_inner(scalars, x_in, b_in, c_in, logt, dtt, rows, width):
    tok, lanes = x_in.shape
    chunks = lanes // width
    heads = width // MP
    per_group = MH // NG
    per_chunk = pl.BlockSpec((tok, width), lambda c, s: (0, c))
    grouped = pl.BlockSpec((tok, N_STATE), lambda c, s: (0, (s[7] + c * heads) // per_group))
    major = lambda c, s: (c, 0, 0)
    return pl.pallas_call(
        ssm_inner_kernel,
        grid_spec=pltpu.PrefetchScalarGridSpec(
            num_scalar_prefetch=1,
            grid=(chunks,),
            in_specs=[
                per_chunk,
                grouped,
                grouped,
                pl.BlockSpec((1, heads, tok), major),
                pl.BlockSpec((1, heads, tok), major),
                pl.BlockSpec((1, 8, width), major),
            ],
            out_specs=per_chunk,
        ),
        out_shape=jax.ShapeDtypeStruct((tok, lanes), F32),
        compiler_params=pltpu.CompilerParams(vmem_limit_bytes=VMEM_LIMIT),
        cost_estimate=pl.CostEstimate(
            flops=2 * tok * lanes * N_STATE * 8, bytes_accessed=6 << 20, transcendentals=1 << 21
        ),
        name="ssm_inner",
    )(scalars, x_in, b_in, c_in, logt, dtt, rows)


def ssm_outputs_kernel(
    scalars, inner_ref, z_ref, c_ref, logt_ref, norm_ref, init_hbm, *rest, hops, chunk, alias,
):
    received = rest[:hops]
    out_ref, carry, init_buf, sem = rest[hops + alias :]
    place = scalars[0]
    tok, width = inner_ref.shape
    heads = width // MP

    for r in range(hops):
        @pl.when(place == r + 1)
        def _():
            pltpu.make_async_copy(received[r], carry, sem).start()

    @pl.when(place == 0)
    def _():
        piece = pltpu.make_async_copy(
            init_hbm.at[chunk * heads : (chunk + 1) * heads], init_buf, sem
        )
        piece.start()
        piece.wait()
        carry[...] = init_buf[...].reshape(width, N_STATE).astype(BF16).T

    row = lax.broadcasted_iota(jnp.int32, (BLOCK, BLOCK), 0)
    col = lax.broadcasted_iota(jnp.int32, (BLOCK, BLOCK), 1)
    mean_table = jnp.where(row // MP == col // MP, 1.0 / MP, 0.0).astype(BF16)
    mean_table = jnp.concatenate([mean_table, mean_table], axis=0)
    table = head_table(heads, width)
    logt = logt_ref[0]
    whole_logs = []
    before = jnp.zeros((heads, 1), F32)
    for blk in range(tok // BLOCK):
        part = slice(blk * BLOCK, (blk + 1) * BLOCK)
        whole_logs.append(jnp.exp(logt[:, part] + before))
        before = before + logt[:, (blk + 1) * BLOCK - 1 : (blk + 1) * BLOCK]
    spread = expand(jnp.concatenate(whole_logs, axis=1), table)
    z = z_ref[...].astype(F32)
    gate = z / (1.0 + jnp.exp(-z))

    @pl.when(place > 0)
    def _():
        pltpu.make_async_copy(received[0], carry, sem).wait()

    gated = (inner_ref[...] + spread * mm(c_ref[...], carry[...])) * gate
    square = gated * gated
    high = square.astype(BF16)
    low = (square - high.astype(F32)).astype(BF16)
    for at in range(0, width, 128):
        lanes = slice(at, at + 128)
        mean = mm(jnp.concatenate([high[:, lanes], low[:, lanes]], axis=1), mean_table)
        normed = gated[:, lanes] * lax.rsqrt(mean + 1e-05) * norm_ref[:, lanes]
        out_ref[:, lanes] = normed.astype(BF16)


def ssm_outputs(scalars, inner, z_gate, c_in, logt, norm_weight, ssm_init, received, width, chunk,
                into):
    tok, lanes = inner.shape
    heads = width // MP
    per_group = MH // NG
    anywhere = pl.BlockSpec(memory_space=pl.ANY)
    per_chunk = pl.BlockSpec((tok, width), lambda k, s: (0, chunk))
    operands = [scalars, inner, z_gate, c_in, logt, norm_weight[None, :], ssm_init, *received]
    in_specs = [
        per_chunk,
        per_chunk,
        pl.BlockSpec((tok, N_STATE), lambda k, s: (0, (s[7] + chunk * heads) // per_group)),
        pl.BlockSpec((1, heads, tok), lambda k, s: (chunk, 0, 0)),
        pl.BlockSpec((1, width), lambda k, s: (0, chunk)),
    ] + [anywhere] * (1 + len(received))
    aliases = {}
    if into is not None:
        aliases = {len(operands): 0}
        operands.append(into)
        in_specs.append(anywhere)
    return pl.pallas_call(
        functools.partial(
            ssm_outputs_kernel, hops=len(received), chunk=chunk, alias=len(aliases)
        ),
        grid_spec=pltpu.PrefetchScalarGridSpec(
            num_scalar_prefetch=1,
            grid=(1,),
            in_specs=in_specs,
            out_specs=per_chunk,
            scratch_shapes=[
                pltpu.VMEM((N_STATE, width), BF16),
                pltpu.VMEM((heads, MP, N_STATE), F32),
                pltpu.SemaphoreType.DMA,
            ],
        ),
        out_shape=jax.ShapeDtypeStruct((tok, lanes), BF16),
        input_output_aliases=aliases,
        compiler_params=pltpu.CompilerParams(vmem_limit_bytes=VMEM_LIMIT),
        cost_estimate=pl.CostEstimate(
            flops=2 * tok * width * N_STATE * 2, bytes_accessed=2 << 20, transcendentals=1 << 18
        ),
        name="ssm_outputs",
    )(*operands)


def attend_kernel(scalars, q_ref, keys_near, keys_far, values_near, values_far, *rest, kv_head,
                  kv_count, heads, hops, alias):
    window = rest[: hops + 1]
    out_ref, k_buf, v_buf, s_buf, best_buf, total_buf, acc_buf, sems, window_sems = rest[
        hops + 1 + alias :
    ]
    place, dp, first_block, cache_blocks, newest, held = (scalars[k] for k in range(6))
    column = scalars[6]
    tok = q_ref.shape[0]
    half = keys_near.shape[0]
    slots = 2 * half
    cache_total = slots // KEY_BLOCK
    lanes = pl.ds(pl.multiple_of((column + kv_head) * HD, HD), HD)
    lane = lax.broadcasted_iota(jnp.int32, (1, KEY_BLOCK), 1)

    def block_of(j):
        return lax.rem(first_block + j, cache_total)

    def block_copy(which, source, block):
        rows = pl.ds(pl.multiple_of(lax.rem(block * KEY_BLOCK, half), KEY_BLOCK), KEY_BLOCK)
        into = pl.ds(pl.multiple_of(block * KEY_BLOCK, KEY_BLOCK), KEY_BLOCK)
        buf = (k_buf, v_buf)[which]
        return pltpu.make_async_copy(source.at[rows, lanes], buf.at[into], sems.at[which, block])

    for which, near, far in ((0, keys_near, keys_far), (1, values_near, values_far)):
        def start(j, unused, which=which, near=near, far=far):
            block = block_of(j)
            mine = block // (half // KEY_BLOCK) == dp

            @pl.when(mine)
            def _():
                block_copy(which, near, block).start()

            @pl.when(jnp.logical_not(mine))
            def _():
                block_copy(which, far, block).start()

            return 0

        lax.fori_loop(0, cache_blocks, start, 0)

    window_copies = []
    for which, buf, at in ((0, k_buf, kv_head), (1, v_buf, kv_count + kv_head)):
        for k, ref in enumerate(window):
            window_copies.append(
                pltpu.make_async_copy(
                    ref.at[:, at * HD : (at + 1) * HD],
                    buf.at[slots + k * tok : slots + (k + 1) * tok],
                    window_sems.at[which, k],
                )
            )
    for copy in window_copies:
        copy.start()
    depth = k_buf.shape[0]
    loose = slots + (hops + 1) * tok
    if depth > loose:
        for buf in (k_buf, v_buf):
            buf[loose:depth, :] = jnp.zeros((depth - loose, HD), BF16)

    def score(offsets, biases):
        for h in range(heads):
            rows = slice(h * tok, (h + 1) * tok)
            best = best_buf[rows, :]
            for offset, bias in zip(offsets, biases):
                span = pl.ds(offset, KEY_BLOCK)
                scores = mm_nt(q_ref[:, h * HD : (h + 1) * HD], k_buf[span, :])
                scores = scores * LOG2_SCALE + bias
                s_buf[rows, span] = scores
                best = jnp.maximum(best, fold_lanes(scores, jnp.maximum))
            best_buf[rows, :] = best

    def mix(offsets):
        for h in range(heads):
            rows = slice(h * tok, (h + 1) * tok)
            best = best_buf[rows, :]
            total = total_buf[rows, :]
            acc = acc_buf[rows, :]
            for offset in offsets:
                probs = jnp.concatenate(
                    [
                        jnp.exp2(s_buf[rows, pl.ds(offset + k, 128)] - best)
                        for k in range(0, KEY_BLOCK, 128)
                    ],
                    axis=1,
                )
                total = total + fold_lanes(probs, jnp.add)
                acc = acc + mm(probs.astype(BF16), v_buf[pl.ds(offset, KEY_BLOCK), :])
            total_buf[rows, :] = total
            acc_buf[rows, :] = acc

    def sweep(visit):
        done = 0
        for size in GROUPS:
            if size > cache_total:
                continue
            count = (cache_blocks - done) // size

            def some(j, unused, size=size, done=done):
                visit([block_of(done + j * size + k) for k in range(size)])
                return 0

            lax.fori_loop(0, count, some, 0)
            done = done + count * size

    def place_of(block):
        return pl.multiple_of(block * KEY_BLOCK, KEY_BLOCK)

    def cache_score(blocks):
        offsets, biases = [], []
        for block in blocks:
            block_copy(0, keys_near, block).wait()
            offset = place_of(block)
            age = newest - (offset + lane)
            age = jnp.where(age < 0, age + slots, age)
            offsets.append(offset)
            biases.append(jnp.where(age < held, 0.0, NEG))
        score(offsets, biases)

    def cache_mix(blocks):
        for block in blocks:
            block_copy(1, values_near, block).wait()
        mix([place_of(block) for block in blocks])

    double = 2 * KEY_BLOCK
    window_pairs = (place * tok + tok + double - 1) // double

    def window_bias(at):
        if isinstance(at, int) and at * KEY_BLOCK < tok:
            later = (
                lax.broadcasted_iota(jnp.int32, (tok, KEY_BLOCK), 0)
                - lax.broadcasted_iota(jnp.int32, (tok, KEY_BLOCK), 1)
            )
            allowed = (later >= 0) | ((lane >= tok) & (lane < tok * (place + 1)))
        else:
            allowed = lane + at * KEY_BLOCK < tok * (place + 1)
        return jnp.where(allowed, 0.0, NEG)

    def window_offsets(j):
        return [pl.multiple_of(slots + (2 * j + k) * KEY_BLOCK, KEY_BLOCK) for k in range(2)]

    best_buf[...] = jnp.full_like(best_buf, NEG)
    acc_buf[...] = jnp.zeros_like(acc_buf)
    total_buf[...] = jnp.zeros_like(total_buf)
    sweep(cache_score)
    for copy in window_copies[: hops + 1]:
        copy.wait()
    score([slots, slots + KEY_BLOCK], [window_bias(0), window_bias(1)])

    def more_scores(j, unused):
        score(window_offsets(j), [window_bias(2 * j), window_bias(2 * j + 1)])
        return 0

    if depth > slots + double:
        lax.fori_loop(1, window_pairs, more_scores, 0)
    best_buf[...] = jnp.broadcast_to(
        jnp.max(best_buf[...], axis=-1, keepdims=True), best_buf.shape
    )
    sweep(cache_mix)
    for copy in window_copies[hops + 1 :]:
        copy.wait()
    mix([slots, slots + KEY_BLOCK])

    def more_mix(j, unused):
        mix(window_offsets(j))
        return 0

    if depth > slots + double:
        lax.fori_loop(1, window_pairs, more_mix, 0)
    for h in range(heads):
        rows = slice(h * tok, (h + 1) * tok)
        total = jnp.sum(total_buf[rows, :], axis=-1, keepdims=True)
        out_ref[:, h * HD : (h + 1) * HD] = (acc_buf[rows, :] / total).astype(BF16)


def attend(scalars, queries, head, heads, kv_count, cache, window, into=None):
    tok = queries.shape[0]
    kv_head = head // (AH // KVH)
    slots = 2 * cache[0].shape[0]
    hops = len(window) - 1
    rows = heads * tok
    depth = slots + -(-((hops + 1) * tok) // (2 * KEY_BLOCK)) * (2 * KEY_BLOCK)
    anywhere = pl.BlockSpec(memory_space=pl.ANY)
    part = pl.BlockSpec((tok, heads * HD), lambda k, s: (0, head // heads))
    operands = [scalars, queries, *cache, *window]
    in_specs = [part] + [anywhere] * (4 + len(window))
    aliases = {}
    if into is not None:
        aliases = {len(operands): 0}
        operands.append(into)
        in_specs.append(anywhere)
    keys_read = slots + (hops + 1) * tok
    return pl.pallas_call(
        functools.partial(
            attend_kernel, kv_head=kv_head, kv_count=kv_count, heads=heads, hops=hops,
            alias=len(aliases),
        ),
        grid_spec=pltpu.PrefetchScalarGridSpec(
            num_scalar_prefetch=1,
            grid=(1,),
            in_specs=in_specs,
            out_specs=part,
            scratch_shapes=[
                pltpu.VMEM((depth, HD), BF16),
                pltpu.VMEM((depth, HD), BF16),
                pltpu.VMEM((rows, depth), F32),
                pltpu.VMEM((rows, 128), F32),
                pltpu.VMEM((rows, 128), F32),
                pltpu.VMEM((rows, 128), F32),
                pltpu.SemaphoreType.DMA((2, slots // KEY_BLOCK)),
                pltpu.SemaphoreType.DMA((2, hops + 1)),
            ],
        ),
        out_shape=jax.ShapeDtypeStruct(queries.shape, BF16),
        input_output_aliases=aliases,
        compiler_params=pltpu.CompilerParams(vmem_limit_bytes=VMEM_LIMIT),
        cost_estimate=pl.CostEstimate(
            flops=16 * rows * keys_read * HD, bytes_accessed=4 * keys_read * HD,
            transcendentals=rows * keys_read,
        ),
        name="attend",
    )(*operands)


def tie(*values):
    return lax.optimization_barrier(values)


def local(x_in, z_gate, b_in, c_in, dt_raw, dt_bias, a_log, d_skip, norm_weight, ssm_init, queries,
          keys, values, cache_keys, cache_values, window_start, prefix_len):
    tok, lanes = x_in.shape
    head_count = dt_raw.shape[1]
    per_group = MH // NG
    places = lax.axis_size("seq")
    place = lax.axis_index("seq")
    dp = lax.axis_index("dp")
    q_count = queries.shape[1] // HD
    kv_here = keys.shape[1] // HD
    kv_count = max(1, q_count * KVH // AH)
    width = 2 * kv_count * HD
    chunks = lanes // width
    column = (dp * q_count) // (AH // KVH)
    slots = 2 * cache_keys.shape[0]

    ring = [(k, (k + 1) % places) for k in range(places)]
    swap = [(0, 1), (1, 0)]
    far_keys = lax.ppermute(cache_keys, "dp", swap)
    far_values = lax.ppermute(cache_values, "dp", swap)

    own_rows = jnp.concatenate(
        [
            lax.dynamic_slice_in_dim(array, column * HD, kv_count * HD, axis=1)
            for array in (keys, values)
        ],
        axis=1,
    )

    newest = jnp.mod(window_start[0] - 1, slots)
    held = prefix_len[0]
    oldest = jnp.mod(newest - held + 1, slots)
    first_block = oldest // KEY_BLOCK
    cache_blocks = jnp.minimum(
        slots // KEY_BLOCK, (oldest % KEY_BLOCK + held + KEY_BLOCK - 1) // KEY_BLOCK
    )
    first_head = dp * head_count
    scalars = jnp.stack(
        [place, dp, first_block, cache_blocks, newest, held, column, first_head]
    ).astype(jnp.int32)

    received = []
    send = own_rows
    arrived = lax.ppermute(send, "seq", ring)
    x_tied, send = tie(x_in, send)
    span = max(width, min(lanes, per_group * MP))
    states, rows, logt, dtt = ssm_states(
        scalars, x_tied, b_in, dt_raw, dt_bias, a_log, d_skip, ssm_init, width, span
    )
    received.append(arrived)

    cache = (cache_keys, far_keys, cache_values, far_values)
    heads = min(4, q_count)
    parts = list(range(0, q_count, heads))
    last_step = places - 1 + chunks - 1
    result = inner = mamba_out = None
    outputs_done = 0

    def outputs(chunk, into):
        candidates = received[chunk + 1 : chunk + places]
        return ssm_outputs(
            scalars, inner, z_gate, c_in, logt, norm_weight, ssm_init, candidates, width, chunk,
            into,
        )

    for step in range(1, last_step + 1):
        incoming = received[-1]
        if step == 1:
            incoming, states = tie(incoming, states)
        elif step == 2:
            incoming, inner = tie(incoming, inner)
        elif result is not None and mamba_out is not None:
            incoming, result, mamba_out = tie(incoming, result, mamba_out)
        elif result is not None:
            incoming, result = tie(incoming, result)
        send = hop(place, incoming, states, rows, step)
        arrived = lax.ppermute(send, "seq", ring)
        if step == 1:
            x_tied, send = tie(x_in, send)
            inner = ssm_inner(scalars, x_tied, b_in, c_in, logt, dtt, rows, width)
        elif step >= places - 1:
            queries_now, z_tied, send = tie(queries, z_gate, send)
            if parts:
                window = [own_rows] + received[: places - 1]
                result = attend(
                    scalars, queries_now, parts.pop(0), heads, kv_count, cache, window, result
                )
            if step >= places:
                mamba_out = outputs(outputs_done, mamba_out)
                outputs_done += 1
        received.append(arrived)
    for head in parts:
        window = [own_rows] + received[: places - 1]
        result = attend(scalars, queries, head, heads, kv_count, cache, window, result)
    while outputs_done < chunks:
        mamba_out = outputs(outputs_done, mamba_out)
        outputs_done += 1
    return (mamba_out, result)


def solution(mesh):
    rows = P(("groups", "seq"), ("tp", "dp"))
    shared = P(("groups", "seq"), "tp")
    heads = P(("tp", "dp"))
    cached = P(("groups", "dp"), "tp")
    return jax.shard_map(
        local,
        mesh=mesh,
        in_specs=(
            rows, rows, shared, shared, rows, heads, heads, heads, heads,
            P(("groups", "tp", "dp"), None, None), rows, shared, shared, cached, cached,
            P("groups"), P("groups"),
        ),
        out_specs=(rows, rows),
        check_vma=False,
    )
```

```python
import functools
import math

import jax
import jax.numpy as jnp
from jax import lax
from jax.experimental import pallas as pl
from jax.experimental.pallas import tpu as pltpu
from jax.sharding import PartitionSpec as P

MH = 128
MP = 64
N_STATE = 256
NG = 8
AH = 64
KVH = 8
HD = 128
BLOCK = 128
KEY_BLOCK = 512
GROUPS = (2, 1)
STATE_WIDTH = 4
HEADS_IN_CALL = 8
LOG2_SCALE = math.log2(math.e) / math.sqrt(HD)
NEG = -1e30
F32 = jnp.float32
BF16 = jnp.bfloat16
VMEM_LIMIT = 56 << 20


def mm(a, b):
    return jnp.dot(a, b, preferred_element_type=F32)


def mm_nt(a, b):
    return lax.dot_general(a, b, (((1,), (1,)), ((), ())), preferred_element_type=F32)


def pieces_of(value):
    first = value.astype(BF16)
    rest = value - first.astype(F32)
    second = rest.astype(BF16)
    third = (rest - second.astype(F32)).astype(BF16)
    return first, second, third


def head_table(heads, width):
    row = lax.broadcasted_iota(jnp.int32, (heads, width), 0)
    lane = lax.broadcasted_iota(jnp.int32, (heads, width), 1)
    table = jnp.where(lane // MP == row, 1.0, 0.0).astype(BF16)
    return jnp.concatenate([table] * 3, axis=0)


def expand(value, table):
    stacked = jnp.concatenate(pieces_of(value), axis=0)
    return lax.dot_general(stacked, table, (((0,), (0,)), ((), ())), preferred_element_type=F32)


def fold_lanes(value, op):
    parts = [value[:, k : k + 128] for k in range(0, value.shape[1], 128)]
    while len(parts) > 1:
        parts = [
            op(parts[k], parts[k + 1]) if k + 1 < len(parts) else parts[k]
            for k in range(0, len(parts), 2)
        ]
    return parts[0]


def ssm_states_kernel(
    scalars, x_ref, b_ref, dt_ref, bias_ref, alog_ref, dskip_ref, init_ref,
    state_ref, rows_ref, logt_ref, dtt_ref, dt_all, log_all, skip_all,
):
    span = pl.program_id(0)
    tok, lanes = x_ref.shape
    heads = lanes // MP
    spans = dt_ref.shape[0] // heads
    parts = state_ref.shape[0]
    width = lanes // parts

    @pl.when(span == 0)
    def _():
        column = lambda ref: jnp.broadcast_to(ref[...], (8, ref.shape[1])).T[:, 0:1]
        dt = jax.nn.softplus(dt_ref[...] + column(bias_ref))
        decay = -jnp.exp(column(alog_ref)) * dt
        row = lax.broadcasted_iota(jnp.int32, (BLOCK, BLOCK), 0)
        col = lax.broadcasted_iota(jnp.int32, (BLOCK, BLOCK), 1)
        upper = jnp.where(row <= col, 1.0, 0.0).astype(BF16)
        logs = []
        for blk in range(tok // BLOCK):
            first, second, third = pieces_of(decay[:, blk * BLOCK : (blk + 1) * BLOCK])
            logs.append(mm(first, upper) + mm(second, upper) + mm(third, upper))
        logs = jnp.concatenate(logs, axis=1)
        skip = jnp.broadcast_to(column(dskip_ref), (dt_ref.shape[0], 128))
        for k in range(spans):
            dt_all[k] = dt[k * heads : (k + 1) * heads]
            log_all[k] = logs[k * heads : (k + 1) * heads]
            skip_all[k] = skip[k * heads : (k + 1) * heads]

    dt = dt_all[span]
    logs = log_all[span]
    few = heads // parts
    for k in range(parts):
        logt_ref[k] = logs[k * few : (k + 1) * few]
        dtt_ref[k] = dt[k * few : (k + 1) * few]
    table = head_table(heads, lanes)
    state = None
    total = jnp.zeros((heads, 1), F32)
    for blk in range(tok // BLOCK):
        part = slice(blk * BLOCK, (blk + 1) * BLOCK)
        end = logs[:, (blk + 1) * BLOCK - 1 : (blk + 1) * BLOCK]
        tail = jnp.exp(end - logs[:, part]) * dt[:, part]
        weighted = (expand(tail, table) * x_ref[part, :].astype(F32)).astype(BF16)
        update = mm(b_ref[part, :].T, weighted)
        if state is None:
            state = update
        else:
            state = expand(jnp.broadcast_to(jnp.exp(end), (heads, 8)), table)[0:1] * state + update
        total = total + end
    place = scalars[0]
    lane = lax.broadcasted_iota(jnp.int32, (heads, 8), 1)
    rows = expand(jnp.where(lane == 0, jnp.exp(total), skip_all[span][:, 0:8]), table)
    for k in range(parts):
        state_ref[k] = state[:, k * width : (k + 1) * width]
        rows_ref[k] = rows[:, k * width : (k + 1) * width]

    @pl.when(place == 0)
    def _():
        for k in range(parts):
            first = init_ref[k * few : (k + 1) * few].reshape(width, N_STATE).T
            state_ref[k] = state_ref[k] + rows_ref[k, 0:1, :] * first
            rows_ref[k, 0:1, :] = jnp.zeros((1, width), F32)


def ssm_states(scalars, x_in, b_in, dt_raw, dt_bias, a_log, d_skip, ssm_init, width, span):
    tok, lanes = x_in.shape
    chunks = lanes // width
    head_count = dt_raw.shape[1]
    heads = span // MP
    few = width // MP
    parts = span // width
    per_group = MH // NG
    flat = lambda c, s: (0, 0)
    major = lambda c, s: (c, 0, 0)
    return pl.pallas_call(
        ssm_states_kernel,
        grid_spec=pltpu.PrefetchScalarGridSpec(
            num_scalar_prefetch=1,
            grid=(lanes // span,),
            in_specs=[
                pl.BlockSpec((tok, span), lambda c, s: (0, c)),
                pl.BlockSpec((tok, N_STATE), lambda c, s: (0, (s[7] + c * heads) // per_group)),
                pl.BlockSpec((head_count, tok), flat),
                pl.BlockSpec((1, head_count), flat),
                pl.BlockSpec((1, head_count), flat),
                pl.BlockSpec((1, head_count), flat),
                pl.BlockSpec((heads, MP, N_STATE), major),
            ],
            out_specs=[
                pl.BlockSpec((parts, N_STATE, width), major),
                pl.BlockSpec((parts, 8, width), major),
                pl.BlockSpec((parts, few, tok), major),
                pl.BlockSpec((parts, few, tok), major),
            ],
            scratch_shapes=[
                pltpu.VMEM((lanes // span, heads, tok), F32),
                pltpu.VMEM((lanes // span, heads, tok), F32),
                pltpu.VMEM((lanes // span, heads, 128), F32),
            ],
        ),
        out_shape=[
            jax.ShapeDtypeStruct((chunks, N_STATE, width), F32),
            jax.ShapeDtypeStruct((chunks, 8, width), F32),
            jax.ShapeDtypeStruct((chunks, few, tok), F32),
            jax.ShapeDtypeStruct((chunks, few, tok), F32),
        ],
        compiler_params=pltpu.CompilerParams(vmem_limit_bytes=VMEM_LIMIT),
        cost_estimate=pl.CostEstimate(
            flops=2 * tok * lanes * N_STATE * 4, bytes_accessed=6 << 20, transcendentals=1 << 16
        ),
        name="ssm_states",
    )(
        scalars, x_in, b_in, dt_raw.T, dt_bias[None, :], a_log[None, :], d_skip[None, :], ssm_init
    )


def hop(place, received, states, rows, step):
    chunks, unused, width = states.shape
    if received.shape[1] < width:
        received = jnp.pad(received, ((0, 0), (0, width - received.shape[1])))
    chunk = jnp.clip(step - 1 - place, 0, chunks - 1)
    state = lax.dynamic_index_in_dim(states, chunk, 0, keepdims=False)
    decay = lax.dynamic_index_in_dim(rows, chunk, 0, keepdims=False)[0:1, :]
    combined = (decay * received.astype(F32) + state).astype(BF16)
    return jnp.where(step <= place, received, combined)


def ssm_inner_kernel(scalars, x_ref, b_ref, c_ref, logt_ref, dtt_ref, rows_ref, out_ref):
    tok, width = x_ref.shape
    heads = width // MP
    row = lax.broadcasted_iota(jnp.int32, (BLOCK, BLOCK), 0)
    col = lax.broadcasted_iota(jnp.int32, (BLOCK, BLOCK), 1)
    lower = row >= col
    low_half = col < MP
    table = head_table(heads, width)
    logt = logt_ref[0]
    dtt = dtt_ref[0]
    logs = logt.T
    skip = rows_ref[0, 1:2, :]
    state = None
    pairs = heads // 2
    for blk in range(tok // BLOCK):
        part = slice(blk * BLOCK, (blk + 1) * BLOCK)
        c_blk = c_ref[part, :]
        b_blk = b_ref[part, :]
        x_blk = x_ref[part, :]
        products = mm_nt(c_blk, b_blk)
        log_blk = logs[part]
        kernels = []
        for h in range(heads):
            spread = log_blk[:, h : h + 1] - logt[h : h + 1, part]
            decay = jnp.exp(jnp.where(lower, spread, NEG))
            kernels.append((decay * products * dtt[h : h + 1, part]).astype(BF16))
        carried = None
        if state is not None:
            carried = expand(jnp.exp(logt[:, part]), table) * mm(c_blk, state.astype(BF16))
        if (blk + 1) * BLOCK < tok:
            end = logt[:, (blk + 1) * BLOCK - 1 : (blk + 1) * BLOCK]
            tail = jnp.exp(end - logt[:, part]) * dtt[:, part]
            weighted = (expand(tail, table) * x_blk.astype(F32)).astype(BF16)
            update = mm(b_blk.T, weighted)
            if state is None:
                state = update
            else:
                factor = expand(jnp.broadcast_to(jnp.exp(end), (heads, 8)), table)[0:1]
                state = factor * state + update
        for pair in range(pairs):
            lanes = slice(pair * 128, (pair + 1) * 128)
            x_pair = x_blk[:, lanes]
            zero = jnp.zeros_like(x_pair)
            stacked = jnp.concatenate(
                [jnp.where(low_half, x_pair, zero), jnp.where(low_half, zero, x_pair)], axis=0
            )
            inner = mm(jnp.concatenate(kernels[2 * pair : 2 * pair + 2], axis=1), stacked)
            value = inner + skip[:, lanes] * x_pair.astype(F32)
            if carried is not None:
                value = value + carried[:, lanes]
            out_ref[part, lanes] = value


def ssm_inner(scalars, x_in, b_in, c_in, logt, dtt, rows, width):
    tok, lanes = x_in.shape
    chunks = lanes // width
    heads = width // MP
    per_group = MH // NG
    per_chunk = pl.BlockSpec((tok, width), lambda c, s: (0, c))
    grouped = pl.BlockSpec((tok, N_STATE), lambda c, s: (0, (s[7] + c * heads) // per_group))
    major = lambda c, s: (c, 0, 0)
    return pl.pallas_call(
        ssm_inner_kernel,
        grid_spec=pltpu.PrefetchScalarGridSpec(
            num_scalar_prefetch=1,
            grid=(chunks,),
            in_specs=[
                per_chunk,
                grouped,
                grouped,
                pl.BlockSpec((1, heads, tok), major),
                pl.BlockSpec((1, heads, tok), major),
                pl.BlockSpec((1, 8, width), major),
            ],
            out_specs=per_chunk,
        ),
        out_shape=jax.ShapeDtypeStruct((tok, lanes), F32),
        compiler_params=pltpu.CompilerParams(vmem_limit_bytes=VMEM_LIMIT),
        cost_estimate=pl.CostEstimate(
            flops=2 * tok * lanes * N_STATE * 8, bytes_accessed=6 << 20, transcendentals=1 << 21
        ),
        name="ssm_inner",
    )(scalars, x_in, b_in, c_in, logt, dtt, rows)


def ssm_outputs_kernel(
    scalars, inner_ref, z_ref, c_ref, logt_ref, norm_ref, init_hbm, *rest, hops,
):
    received = rest[:hops]
    out_ref, carry, init_buf, sems, init_sem = rest[hops:]
    chunk = pl.program_id(0)
    place = scalars[0]
    tok, width = inner_ref.shape
    heads = width // MP
    count = carry.shape[0]

    @pl.when(chunk == 0)
    def _():
        for k in range(count):
            for r in range(hops):
                @pl.when((place > 0) & (place + k == r + 1))
                def _():
                    pltpu.make_async_copy(received[r], carry.at[k], sems.at[k]).start()

        @pl.when(place == 0)
        def _():
            whole = pltpu.make_async_copy(init_hbm, init_buf, init_sem)
            whole.start()
            whole.wait()
            for k in range(count):
                first = init_buf[k * heads : (k + 1) * heads].reshape(width, N_STATE)
                carry[k] = first.astype(BF16).T

    @pl.when(place > 0)
    def _():
        pltpu.make_async_copy(received[0], carry.at[chunk], sems.at[chunk]).wait()

    row = lax.broadcasted_iota(jnp.int32, (BLOCK, BLOCK), 0)
    col = lax.broadcasted_iota(jnp.int32, (BLOCK, BLOCK), 1)
    mean_table = jnp.where(row // MP == col // MP, 1.0 / MP, 0.0).astype(BF16)
    mean_table = jnp.concatenate([mean_table, mean_table], axis=0)
    table = head_table(heads, width)
    logt = logt_ref[0]
    whole_logs = []
    before = jnp.zeros((heads, 1), F32)
    for blk in range(tok // BLOCK):
        part = slice(blk * BLOCK, (blk + 1) * BLOCK)
        whole_logs.append(jnp.exp(logt[:, part] + before))
        before = before + logt[:, (blk + 1) * BLOCK - 1 : (blk + 1) * BLOCK]
    carried = expand(jnp.concatenate(whole_logs, axis=1), table) * mm(c_ref[...], carry[chunk])
    z = z_ref[...].astype(F32)
    gated = (inner_ref[...] + carried) * (z / (1.0 + jnp.exp(-z)))
    square = gated * gated
    high = square.astype(BF16)
    low = (square - high.astype(F32)).astype(BF16)
    for at in range(0, width, 128):
        lanes = slice(at, at + 128)
        mean = mm(jnp.concatenate([high[:, lanes], low[:, lanes]], axis=1), mean_table)
        normed = gated[:, lanes] * lax.rsqrt(mean + 1e-05) * norm_ref[:, lanes]
        out_ref[:, lanes] = normed.astype(BF16)


def ssm_outputs(scalars, inner, z_gate, c_in, logt, norm_weight, ssm_init, received, width):
    tok, lanes = inner.shape
    chunks = lanes // width
    heads = width // MP
    per_group = MH // NG
    anywhere = pl.BlockSpec(memory_space=pl.ANY)
    per_chunk = pl.BlockSpec((tok, width), lambda c, s: (0, c))
    grouped = pl.BlockSpec((tok, N_STATE), lambda c, s: (0, (s[7] + c * heads) // per_group))
    return pl.pallas_call(
        functools.partial(ssm_outputs_kernel, hops=len(received)),
        grid_spec=pltpu.PrefetchScalarGridSpec(
            num_scalar_prefetch=1,
            grid=(chunks,),
            in_specs=[
                per_chunk,
                per_chunk,
                grouped,
                pl.BlockSpec((1, heads, tok), lambda c, s: (c, 0, 0)),
                pl.BlockSpec((1, width), lambda c, s: (0, c)),
            ]
            + [anywhere] * (1 + len(received)),
            out_specs=per_chunk,
            scratch_shapes=[
                pltpu.VMEM((chunks, N_STATE, width), BF16),
                pltpu.VMEM(ssm_init.shape, F32),
                pltpu.SemaphoreType.DMA((chunks,)),
                pltpu.SemaphoreType.DMA,
            ],
        ),
        out_shape=jax.ShapeDtypeStruct((tok, lanes), BF16),
        compiler_params=pltpu.CompilerParams(vmem_limit_bytes=VMEM_LIMIT),
        cost_estimate=pl.CostEstimate(
            flops=2 * tok * lanes * N_STATE * 2, bytes_accessed=6 << 20, transcendentals=1 << 20
        ),
        name="ssm_outputs",
    )(scalars, inner, z_gate, c_in, logt, norm_weight[None, :], ssm_init, *received)


def attend_kernel(scalars, q_ref, keys_near, keys_far, values_near, values_far, *rest, kv_head,
                  kv_count, heads, hops, alias):
    window = rest[: hops + 1]
    out_ref, k_buf, v_buf, s_buf, best_buf, total_buf, acc_buf, sems, window_sems = rest[
        hops + 1 + alias :
    ]
    place, dp, first_block, cache_blocks, newest, held = (scalars[k] for k in range(6))
    column = scalars[6]
    tok = q_ref.shape[0]
    half = keys_near.shape[0]
    slots = 2 * half
    cache_total = slots // KEY_BLOCK
    lanes = pl.ds(pl.multiple_of((column + kv_head) * HD, HD), HD)
    lane = lax.broadcasted_iota(jnp.int32, (1, KEY_BLOCK), 1)

    def block_of(j):
        return lax.rem(first_block + j, cache_total)

    def block_copy(which, source, block):
        rows = pl.ds(pl.multiple_of(lax.rem(block * KEY_BLOCK, half), KEY_BLOCK), KEY_BLOCK)
        into = pl.ds(pl.multiple_of(block * KEY_BLOCK, KEY_BLOCK), KEY_BLOCK)
        buf = (k_buf, v_buf)[which]
        return pltpu.make_async_copy(source.at[rows, lanes], buf.at[into], sems.at[which, block])

    for which, near, far in ((0, keys_near, keys_far), (1, values_near, values_far)):
        def start(j, unused, which=which, near=near, far=far):
            block = block_of(j)
            mine = block // (half // KEY_BLOCK) == dp

            @pl.when(mine)
            def _():
                block_copy(which, near, block).start()

            @pl.when(jnp.logical_not(mine))
            def _():
                block_copy(which, far, block).start()

            return 0

        lax.fori_loop(0, cache_blocks, start, 0)

    window_copies = []
    for which, buf, at in ((0, k_buf, kv_head), (1, v_buf, kv_count + kv_head)):
        for k, ref in enumerate(window):
            window_copies.append(
                pltpu.make_async_copy(
                    ref.at[:, at * HD : (at + 1) * HD],
                    buf.at[slots + k * tok : slots + (k + 1) * tok],
                    window_sems.at[which, k],
                )
            )
    for copy in window_copies:
        copy.start()
    depth = k_buf.shape[0]
    loose = slots + (hops + 1) * tok
    if depth > loose:
        for buf in (k_buf, v_buf):
            buf[loose:depth, :] = jnp.zeros((depth - loose, HD), BF16)

    def score(offsets, biases):
        for h in range(heads):
            rows = slice(h * tok, (h + 1) * tok)
            best = best_buf[rows, :]
            for offset, bias in zip(offsets, biases):
                span = pl.ds(offset, KEY_BLOCK)
                scores = mm_nt(q_ref[:, h * HD : (h + 1) * HD], k_buf[span, :])
                scores = scores * LOG2_SCALE + bias
                s_buf[rows, span] = scores
                best = jnp.maximum(best, fold_lanes(scores, jnp.maximum))
            best_buf[rows, :] = best

    def mix(offsets):
        for h in range(heads):
            rows = slice(h * tok, (h + 1) * tok)
            best = best_buf[rows, :]
            total = total_buf[rows, :]
            acc = acc_buf[rows, :]
            for offset in offsets:
                probs = jnp.concatenate(
                    [
                        jnp.exp2(s_buf[rows, pl.ds(offset + k, 128)] - best)
                        for k in range(0, KEY_BLOCK, 128)
                    ],
                    axis=1,
                )
                total = total + fold_lanes(probs, jnp.add)
                acc = acc + mm(probs.astype(BF16), v_buf[pl.ds(offset, KEY_BLOCK), :])
            total_buf[rows, :] = total
            acc_buf[rows, :] = acc

    def sweep(visit):
        done = 0
        for size in GROUPS:
            if size > cache_total:
                continue
            count = (cache_blocks - done) // size

            def some(j, unused, size=size, done=done):
                visit([block_of(done + j * size + k) for k in range(size)])
                return 0

            lax.fori_loop(0, count, some, 0)
            done = done + count * size

    def place_of(block):
        return pl.multiple_of(block * KEY_BLOCK, KEY_BLOCK)

    def cache_score(blocks):
        offsets, biases = [], []
        for block in blocks:
            block_copy(0, keys_near, block).wait()
            offset = place_of(block)
            age = newest - (offset + lane)
            age = jnp.where(age < 0, age + slots, age)
            offsets.append(offset)
            biases.append(jnp.where(age < held, 0.0, NEG))
        score(offsets, biases)

    def cache_mix(blocks):
        for block in blocks:
            block_copy(1, values_near, block).wait()
        mix([place_of(block) for block in blocks])

    double = 2 * KEY_BLOCK
    window_pairs = (place * tok + tok + double - 1) // double

    def window_bias(at):
        if isinstance(at, int) and at * KEY_BLOCK < tok:
            later = (
                lax.broadcasted_iota(jnp.int32, (tok, KEY_BLOCK), 0)
                - lax.broadcasted_iota(jnp.int32, (tok, KEY_BLOCK), 1)
            )
            allowed = (later >= 0) | ((lane >= tok) & (lane < tok * (place + 1)))
        else:
            allowed = lane + at * KEY_BLOCK < tok * (place + 1)
        return jnp.where(allowed, 0.0, NEG)

    def window_offsets(j):
        return [pl.multiple_of(slots + (2 * j + k) * KEY_BLOCK, KEY_BLOCK) for k in range(2)]

    best_buf[...] = jnp.full_like(best_buf, NEG)
    acc_buf[...] = jnp.zeros_like(acc_buf)
    total_buf[...] = jnp.zeros_like(total_buf)
    sweep(cache_score)
    for copy in window_copies[: hops + 1]:
        copy.wait()
    score([slots, slots + KEY_BLOCK], [window_bias(0), window_bias(1)])

    def more_scores(j, unused):
        score(window_offsets(j), [window_bias(2 * j), window_bias(2 * j + 1)])
        return 0

    if depth > slots + double:
        lax.fori_loop(1, window_pairs, more_scores, 0)
    best_buf[...] = jnp.broadcast_to(
        jnp.max(best_buf[...], axis=-1, keepdims=True), best_buf.shape
    )
    sweep(cache_mix)
    for copy in window_copies[hops + 1 :]:
        copy.wait()
    mix([slots, slots + KEY_BLOCK])

    def more_mix(j, unused):
        mix(window_offsets(j))
        return 0

    if depth > slots + double:
        lax.fori_loop(1, window_pairs, more_mix, 0)
    for h in range(heads):
        rows = slice(h * tok, (h + 1) * tok)
        total = jnp.sum(total_buf[rows, :], axis=-1, keepdims=True)
        out_ref[:, h * HD : (h + 1) * HD] = (acc_buf[rows, :] / total).astype(BF16)


def attend(scalars, queries, head, heads, kv_count, cache, window, into=None):
    tok = queries.shape[0]
    kv_head = head // (AH // KVH)
    slots = 2 * cache[0].shape[0]
    hops = len(window) - 1
    rows = heads * tok
    depth = slots + -(-((hops + 1) * tok) // (2 * KEY_BLOCK)) * (2 * KEY_BLOCK)
    anywhere = pl.BlockSpec(memory_space=pl.ANY)
    part = pl.BlockSpec((tok, heads * HD), lambda k, s: (0, head // heads))
    operands = [scalars, queries, *cache, *window]
    in_specs = [part] + [anywhere] * (4 + len(window))
    aliases = {}
    if into is not None:
        aliases = {len(operands): 0}
        operands.append(into)
        in_specs.append(anywhere)
    keys_read = slots + (hops + 1) * tok
    return pl.pallas_call(
        functools.partial(
            attend_kernel, kv_head=kv_head, kv_count=kv_count, heads=heads, hops=hops,
            alias=len(aliases),
        ),
        grid_spec=pltpu.PrefetchScalarGridSpec(
            num_scalar_prefetch=1,
            grid=(1,),
            in_specs=in_specs,
            out_specs=part,
            scratch_shapes=[
                pltpu.VMEM((depth, HD), BF16),
                pltpu.VMEM((depth, HD), BF16),
                pltpu.VMEM((rows, depth), F32),
                pltpu.VMEM((rows, 128), F32),
                pltpu.VMEM((rows, 128), F32),
                pltpu.VMEM((rows, 128), F32),
                pltpu.SemaphoreType.DMA((2, slots // KEY_BLOCK)),
                pltpu.SemaphoreType.DMA((2, hops + 1)),
            ],
        ),
        out_shape=jax.ShapeDtypeStruct(queries.shape, BF16),
        input_output_aliases=aliases,
        compiler_params=pltpu.CompilerParams(vmem_limit_bytes=VMEM_LIMIT),
        cost_estimate=pl.CostEstimate(
            flops=16 * rows * keys_read * HD, bytes_accessed=4 * keys_read * HD,
            transcendentals=rows * keys_read,
        ),
        name="attend",
    )(*operands)


def tie(*values):
    return lax.optimization_barrier(values)


def local(x_in, z_gate, b_in, c_in, dt_raw, dt_bias, a_log, d_skip, norm_weight, ssm_init, queries,
          keys, values, cache_keys, cache_values, window_start, prefix_len):
    tok, lanes = x_in.shape
    head_count = dt_raw.shape[1]
    per_group = MH // NG
    places = lax.axis_size("seq")
    place = lax.axis_index("seq")
    dp = lax.axis_index("dp")
    q_count = queries.shape[1] // HD
    kv_here = keys.shape[1] // HD
    kv_count = max(1, q_count * KVH // AH)
    width = min(lanes, STATE_WIDTH * kv_count * HD)
    chunks = lanes // width
    column = (dp * q_count) // (AH // KVH)
    slots = 2 * cache_keys.shape[0]

    ring = [(k, (k + 1) % places) for k in range(places)]
    swap = [(0, 1), (1, 0)]
    far_keys = lax.ppermute(cache_keys, "dp", swap)
    far_values = lax.ppermute(cache_values, "dp", swap)

    own_rows = jnp.concatenate(
        [
            lax.dynamic_slice_in_dim(array, column * HD, kv_count * HD, axis=1)
            for array in (keys, values)
        ],
        axis=1,
    )

    newest = jnp.mod(window_start[0] - 1, slots)
    held = prefix_len[0]
    oldest = jnp.mod(newest - held + 1, slots)
    first_block = oldest // KEY_BLOCK
    cache_blocks = jnp.minimum(
        slots // KEY_BLOCK, (oldest % KEY_BLOCK + held + KEY_BLOCK - 1) // KEY_BLOCK
    )
    first_head = dp * head_count
    scalars = jnp.stack(
        [place, dp, first_block, cache_blocks, newest, held, column, first_head]
    ).astype(jnp.int32)

    received = []
    send = own_rows
    arrived = lax.ppermute(send, "seq", ring)
    x_tied, send = tie(x_in, send)
    span = max(width, min(lanes, per_group * MP))
    states, rows, logt, dtt = ssm_states(
        scalars, x_tied, b_in, dt_raw, dt_bias, a_log, d_skip, ssm_init, width, span
    )
    received.append(arrived)

    cache = (cache_keys, far_keys, cache_values, far_values)
    heads = min(HEADS_IN_CALL, q_count)
    parts = list(range(0, q_count, heads))
    last_step = places - 1 + chunks - 1
    result = inner = None

    def attend_next(queries_now, into):
        window = [own_rows] + received[: places - 1]
        return attend(
            scalars, queries_now, parts.pop(0), heads, kv_count, cache, window, into
        )

    for step in range(1, last_step + 1):
        incoming = received[-1]
        if step == 1:
            incoming, states = tie(incoming, states)
        elif result is not None:
            incoming, result = tie(incoming, result)
        else:
            incoming, inner = tie(incoming, inner)
        send = hop(place, incoming, states, rows, step)
        arrived = lax.ppermute(send, "seq", ring)
        if step == 1:
            x_tied, send = tie(x_in, send)
            inner = ssm_inner(scalars, x_tied, b_in, c_in, logt, dtt, rows, width)
        elif step >= places - 1 and parts:
            queries_now, send = tie(queries, send)
            result = attend_next(queries_now, result)
        received.append(arrived)
    while parts:
        result = attend_next(queries, result)
    mamba_out = ssm_outputs(
        scalars, inner, z_gate, c_in, logt, norm_weight, ssm_init, received[1:], width
    )
    return (mamba_out, result)


def solution(mesh):
    rows = P(("groups", "seq"), ("tp", "dp"))
    shared = P(("groups", "seq"), "tp")
    heads = P(("tp", "dp"))
    cached = P(("groups", "dp"), "tp")
    return jax.shard_map(
        local,
        mesh=mesh,
        in_specs=(
            rows, rows, shared, shared, rows, heads, heads, heads, heads,
            P(("groups", "tp", "dp"), None, None), rows, shared, shared, cached, cached,
            P("groups"), P("groups"),
        ),
        out_specs=(rows, rows),
        check_vma=False,
    )
```

```python
import functools
import math

import jax
import jax.numpy as jnp
from jax import lax
from jax.experimental import pallas as pl
from jax.experimental.pallas import tpu as pltpu
from jax.sharding import PartitionSpec as P

MH = 128
MP = 64
N_STATE = 256
NG = 8
AH = 64
KVH = 8
HD = 128
BLOCK = 128
KEY_BLOCK = 512
GROUPS = (2, 1)
STATE_WIDTH = 4
HEADS_IN_CALL = 8
OPEN_STEP = 2
LOG2_SCALE = math.log2(math.e) / math.sqrt(HD)
NEG = -1e30
F32 = jnp.float32
BF16 = jnp.bfloat16
VMEM_LIMIT = 56 << 20


def mm(a, b):
    return jnp.dot(a, b, preferred_element_type=F32)


def mm_nt(a, b):
    return lax.dot_general(a, b, (((1,), (1,)), ((), ())), preferred_element_type=F32)


def pieces_of(value):
    first = value.astype(BF16)
    rest = value - first.astype(F32)
    second = rest.astype(BF16)
    third = (rest - second.astype(F32)).astype(BF16)
    return first, second, third


def head_table(heads, width):
    row = lax.broadcasted_iota(jnp.int32, (heads, width), 0)
    lane = lax.broadcasted_iota(jnp.int32, (heads, width), 1)
    table = jnp.where(lane // MP == row, 1.0, 0.0).astype(BF16)
    return jnp.concatenate([table] * 3, axis=0)


def expand(value, table):
    stacked = jnp.concatenate(pieces_of(value), axis=0)
    return lax.dot_general(stacked, table, (((0,), (0,)), ((), ())), preferred_element_type=F32)


def fold_lanes(value, op):
    parts = [value[:, k : k + 128] for k in range(0, value.shape[1], 128)]
    while len(parts) > 1:
        parts = [
            op(parts[k], parts[k + 1]) if k + 1 < len(parts) else parts[k]
            for k in range(0, len(parts), 2)
        ]
    return parts[0]


def ssm_states_kernel(
    scalars, x_ref, b_ref, dt_ref, bias_ref, alog_ref, dskip_ref, init_ref,
    state_ref, rows_ref, logt_ref, dtt_ref, dt_all, log_all, skip_all,
):
    span = pl.program_id(0)
    tok, lanes = x_ref.shape
    heads = lanes // MP
    spans = dt_ref.shape[0] // heads
    parts = state_ref.shape[0]
    width = lanes // parts

    @pl.when(span == 0)
    def _():
        column = lambda ref: jnp.broadcast_to(ref[...], (8, ref.shape[1])).T[:, 0:1]
        dt = jax.nn.softplus(dt_ref[...] + column(bias_ref))
        decay = -jnp.exp(column(alog_ref)) * dt
        row = lax.broadcasted_iota(jnp.int32, (BLOCK, BLOCK), 0)
        col = lax.broadcasted_iota(jnp.int32, (BLOCK, BLOCK), 1)
        upper = jnp.where(row <= col, 1.0, 0.0).astype(BF16)
        logs = []
        for blk in range(tok // BLOCK):
            first, second, third = pieces_of(decay[:, blk * BLOCK : (blk + 1) * BLOCK])
            logs.append(mm(first, upper) + mm(second, upper) + mm(third, upper))
        logs = jnp.concatenate(logs, axis=1)
        skip = jnp.broadcast_to(column(dskip_ref), (dt_ref.shape[0], 128))
        for k in range(spans):
            dt_all[k] = dt[k * heads : (k + 1) * heads]
            log_all[k] = logs[k * heads : (k + 1) * heads]
            skip_all[k] = skip[k * heads : (k + 1) * heads]

    dt = dt_all[span]
    logs = log_all[span]
    few = heads // parts
    for k in range(parts):
        logt_ref[k] = logs[k * few : (k + 1) * few]
        dtt_ref[k] = dt[k * few : (k + 1) * few]
    table = head_table(heads, lanes)
    state = None
    total = jnp.zeros((heads, 1), F32)
    for blk in range(tok // BLOCK):
        part = slice(blk * BLOCK, (blk + 1) * BLOCK)
        end = logs[:, (blk + 1) * BLOCK - 1 : (blk + 1) * BLOCK]
        tail = jnp.exp(end - logs[:, part]) * dt[:, part]
        weighted = (expand(tail, table) * x_ref[part, :].astype(F32)).astype(BF16)
        update = mm(b_ref[part, :].T, weighted)
        if state is None:
            state = update
        else:
            state = expand(jnp.broadcast_to(jnp.exp(end), (heads, 8)), table)[0:1] * state + update
        total = total + end
    place = scalars[0]
    lane = lax.broadcasted_iota(jnp.int32, (heads, 8), 1)
    rows = expand(jnp.where(lane == 0, jnp.exp(total), skip_all[span][:, 0:8]), table)
    for k in range(parts):
        state_ref[k] = state[:, k * width : (k + 1) * width]
        rows_ref[k] = rows[:, k * width : (k + 1) * width]

    @pl.when(place == 0)
    def _():
        for k in range(parts):
            first = init_ref[k * few : (k + 1) * few].reshape(width, N_STATE).T
            state_ref[k] = state_ref[k] + rows_ref[k, 0:1, :] * first
            rows_ref[k, 0:1, :] = jnp.zeros((1, width), F32)


def ssm_states(scalars, x_in, b_in, dt_raw, dt_bias, a_log, d_skip, ssm_init, width, span):
    tok, lanes = x_in.shape
    chunks = lanes // width
    head_count = dt_raw.shape[1]
    heads = span // MP
    few = width // MP
    parts = span // width
    per_group = MH // NG
    flat = lambda c, s: (0, 0)
    major = lambda c, s: (c, 0, 0)
    return pl.pallas_call(
        ssm_states_kernel,
        grid_spec=pltpu.PrefetchScalarGridSpec(
            num_scalar_prefetch=1,
            grid=(lanes // span,),
            in_specs=[
                pl.BlockSpec((tok, span), lambda c, s: (0, c)),
                pl.BlockSpec((tok, N_STATE), lambda c, s: (0, (s[7] + c * heads) // per_group)),
                pl.BlockSpec((head_count, tok), flat),
                pl.BlockSpec((1, head_count), flat),
                pl.BlockSpec((1, head_count), flat),
                pl.BlockSpec((1, head_count), flat),
                pl.BlockSpec((heads, MP, N_STATE), major),
            ],
            out_specs=[
                pl.BlockSpec((parts, N_STATE, width), major),
                pl.BlockSpec((parts, 8, width), major),
                pl.BlockSpec((parts, few, tok), major),
                pl.BlockSpec((parts, few, tok), major),
            ],
            scratch_shapes=[
                pltpu.VMEM((lanes // span, heads, tok), F32),
                pltpu.VMEM((lanes // span, heads, tok), F32),
                pltpu.VMEM((lanes // span, heads, 128), F32),
            ],
        ),
        out_shape=[
            jax.ShapeDtypeStruct((chunks, N_STATE, width), F32),
            jax.ShapeDtypeStruct((chunks, 8, width), F32),
            jax.ShapeDtypeStruct((chunks, few, tok), F32),
            jax.ShapeDtypeStruct((chunks, few, tok), F32),
        ],
        compiler_params=pltpu.CompilerParams(vmem_limit_bytes=VMEM_LIMIT),
        cost_estimate=pl.CostEstimate(
            flops=2 * tok * lanes * N_STATE * 4, bytes_accessed=6 << 20, transcendentals=1 << 16
        ),
        name="ssm_states",
    )(
        scalars, x_in, b_in, dt_raw.T, dt_bias[None, :], a_log[None, :], d_skip[None, :], ssm_init
    )


def hop(place, received, states, rows, step):
    chunks, unused, width = states.shape
    if received.shape[1] < width:
        received = jnp.pad(received, ((0, 0), (0, width - received.shape[1])))
    chunk = jnp.clip(step - 1 - place, 0, chunks - 1)
    state = lax.dynamic_index_in_dim(states, chunk, 0, keepdims=False)
    decay = lax.dynamic_index_in_dim(rows, chunk, 0, keepdims=False)[0:1, :]
    combined = (decay * received.astype(F32) + state).astype(BF16)
    return jnp.where(step <= place, received, combined)


def ssm_inner_kernel(scalars, x_ref, b_ref, c_ref, logt_ref, dtt_ref, rows_ref, out_ref):
    tok, width = x_ref.shape
    heads = width // MP
    row = lax.broadcasted_iota(jnp.int32, (BLOCK, BLOCK), 0)
    col = lax.broadcasted_iota(jnp.int32, (BLOCK, BLOCK), 1)
    lower = row >= col
    low_half = col < MP
    table = head_table(heads, width)
    logt = logt_ref[0]
    dtt = dtt_ref[0]
    logs = logt.T
    skip = rows_ref[0, 1:2, :]
    state = None
    pairs = heads // 2
    for blk in range(tok // BLOCK):
        part = slice(blk * BLOCK, (blk + 1) * BLOCK)
        c_blk = c_ref[part, :]
        b_blk = b_ref[part, :]
        x_blk = x_ref[part, :]
        products = mm_nt(c_blk, b_blk)
        log_blk = logs[part]
        kernels = []
        for h in range(heads):
            spread = log_blk[:, h : h + 1] - logt[h : h + 1, part]
            decay = jnp.exp(jnp.where(lower, spread, NEG))
            kernels.append((decay * products * dtt[h : h + 1, part]).astype(BF16))
        carried = None
        if state is not None:
            carried = expand(jnp.exp(logt[:, part]), table) * mm(c_blk, state.astype(BF16))
        if (blk + 1) * BLOCK < tok:
            end = logt[:, (blk + 1) * BLOCK - 1 : (blk + 1) * BLOCK]
            tail = jnp.exp(end - logt[:, part]) * dtt[:, part]
            weighted = (expand(tail, table) * x_blk.astype(F32)).astype(BF16)
            update = mm(b_blk.T, weighted)
            if state is None:
                state = update
            else:
                factor = expand(jnp.broadcast_to(jnp.exp(end), (heads, 8)), table)[0:1]
                state = factor * state + update
        for pair in range(pairs):
            lanes = slice(pair * 128, (pair + 1) * 128)
            x_pair = x_blk[:, lanes]
            zero = jnp.zeros_like(x_pair)
            stacked = jnp.concatenate(
                [jnp.where(low_half, x_pair, zero), jnp.where(low_half, zero, x_pair)], axis=0
            )
            inner = mm(jnp.concatenate(kernels[2 * pair : 2 * pair + 2], axis=1), stacked)
            value = inner + skip[:, lanes] * x_pair.astype(F32)
            if carried is not None:
                value = value + carried[:, lanes]
            out_ref[part, lanes] = value


def ssm_inner(scalars, x_in, b_in, c_in, logt, dtt, rows, width):
    tok, lanes = x_in.shape
    chunks = lanes // width
    heads = width // MP
    per_group = MH // NG
    per_chunk = pl.BlockSpec((tok, width), lambda c, s: (0, c))
    grouped = pl.BlockSpec((tok, N_STATE), lambda c, s: (0, (s[7] + c * heads) // per_group))
    major = lambda c, s: (c, 0, 0)
    return pl.pallas_call(
        ssm_inner_kernel,
        grid_spec=pltpu.PrefetchScalarGridSpec(
            num_scalar_prefetch=1,
            grid=(chunks,),
            in_specs=[
                per_chunk,
                grouped,
                grouped,
                pl.BlockSpec((1, heads, tok), major),
                pl.BlockSpec((1, heads, tok), major),
                pl.BlockSpec((1, 8, width), major),
            ],
            out_specs=per_chunk,
        ),
        out_shape=jax.ShapeDtypeStruct((tok, lanes), F32),
        compiler_params=pltpu.CompilerParams(vmem_limit_bytes=VMEM_LIMIT),
        cost_estimate=pl.CostEstimate(
            flops=2 * tok * lanes * N_STATE * 8, bytes_accessed=6 << 20, transcendentals=1 << 21
        ),
        name="ssm_inner",
    )(scalars, x_in, b_in, c_in, logt, dtt, rows)


def ssm_outputs_kernel(
    scalars, inner_ref, z_ref, c_ref, logt_ref, norm_ref, init_hbm, *rest, hops,
):
    received = rest[:hops]
    out_ref, carry, init_buf, sems, init_sem = rest[hops:]
    chunk = pl.program_id(0)
    place = scalars[0]
    tok, width = inner_ref.shape
    heads = width // MP
    count = carry.shape[0]

    @pl.when(chunk == 0)
    def _():
        for k in range(count):
            for r in range(hops):
                @pl.when((place > 0) & (place + k == r + 1))
                def _():
                    pltpu.make_async_copy(received[r], carry.at[k], sems.at[k]).start()

        @pl.when(place == 0)
        def _():
            whole = pltpu.make_async_copy(init_hbm, init_buf, init_sem)
            whole.start()
            whole.wait()
            for k in range(count):
                first = init_buf[k * heads : (k + 1) * heads].reshape(width, N_STATE)
                carry[k] = first.astype(BF16).T

    @pl.when(place > 0)
    def _():
        pltpu.make_async_copy(received[0], carry.at[chunk], sems.at[chunk]).wait()

    row = lax.broadcasted_iota(jnp.int32, (BLOCK, BLOCK), 0)
    col = lax.broadcasted_iota(jnp.int32, (BLOCK, BLOCK), 1)
    mean_table = jnp.where(row // MP == col // MP, 1.0 / MP, 0.0).astype(BF16)
    mean_table = jnp.concatenate([mean_table, mean_table], axis=0)
    table = head_table(heads, width)
    logt = logt_ref[0]
    whole_logs = []
    before = jnp.zeros((heads, 1), F32)
    for blk in range(tok // BLOCK):
        part = slice(blk * BLOCK, (blk + 1) * BLOCK)
        whole_logs.append(jnp.exp(logt[:, part] + before))
        before = before + logt[:, (blk + 1) * BLOCK - 1 : (blk + 1) * BLOCK]
    carried = expand(jnp.concatenate(whole_logs, axis=1), table) * mm(c_ref[...], carry[chunk])
    z = z_ref[...].astype(F32)
    gated = (inner_ref[...] + carried) * (z / (1.0 + jnp.exp(-z)))
    square = gated * gated
    high = square.astype(BF16)
    low = (square - high.astype(F32)).astype(BF16)
    for at in range(0, width, 128):
        lanes = slice(at, at + 128)
        mean = mm(jnp.concatenate([high[:, lanes], low[:, lanes]], axis=1), mean_table)
        normed = gated[:, lanes] * lax.rsqrt(mean + 1e-05) * norm_ref[:, lanes]
        out_ref[:, lanes] = normed.astype(BF16)


def ssm_outputs(scalars, inner, z_gate, c_in, logt, norm_weight, ssm_init, received, width):
    tok, lanes = inner.shape
    chunks = lanes // width
    heads = width // MP
    per_group = MH // NG
    anywhere = pl.BlockSpec(memory_space=pl.ANY)
    per_chunk = pl.BlockSpec((tok, width), lambda c, s: (0, c))
    grouped = pl.BlockSpec((tok, N_STATE), lambda c, s: (0, (s[7] + c * heads) // per_group))
    return pl.pallas_call(
        functools.partial(ssm_outputs_kernel, hops=len(received)),
        grid_spec=pltpu.PrefetchScalarGridSpec(
            num_scalar_prefetch=1,
            grid=(chunks,),
            in_specs=[
                per_chunk,
                per_chunk,
                grouped,
                pl.BlockSpec((1, heads, tok), lambda c, s: (c, 0, 0)),
                pl.BlockSpec((1, width), lambda c, s: (0, c)),
            ]
            + [anywhere] * (1 + len(received)),
            out_specs=per_chunk,
            scratch_shapes=[
                pltpu.VMEM((chunks, N_STATE, width), BF16),
                pltpu.VMEM(ssm_init.shape, F32),
                pltpu.SemaphoreType.DMA((chunks,)),
                pltpu.SemaphoreType.DMA,
            ],
        ),
        out_shape=jax.ShapeDtypeStruct((tok, lanes), BF16),
        compiler_params=pltpu.CompilerParams(vmem_limit_bytes=VMEM_LIMIT),
        cost_estimate=pl.CostEstimate(
            flops=2 * tok * lanes * N_STATE * 2, bytes_accessed=6 << 20, transcendentals=1 << 20
        ),
        name="ssm_outputs",
    )(scalars, inner, z_gate, c_in, logt, norm_weight[None, :], ssm_init, *received)


def attend_kernel(scalars, q_ref, *rest, kv_head, kv_count, heads, hops, slots, use_cache,
                  use_window, carry_in, final, alias):
    rest = list(rest)
    take = lambda count: [rest.pop(0) for _ in range(count)]
    keys_near, keys_far, values_near, values_far = take(4) if use_cache else [None] * 4
    window = take(hops + 1) if use_window else []
    acc_in, state_in = take(2) if carry_in else (None, None)
    take(alias)
    outs = take(1 if final else 2)
    k_buf, v_buf, s_buf, best_buf, total_buf, acc_buf, sems, window_sems = rest
    place, dp, first_block, cache_blocks, newest, held = (scalars[k] for k in range(6))
    column = scalars[6]
    tok = q_ref.shape[0]
    half = slots // 2
    cache_total = slots // KEY_BLOCK
    base = slots if use_cache else 0
    lanes = pl.ds(pl.multiple_of((column + kv_head) * HD, HD), HD)
    lane = lax.broadcasted_iota(jnp.int32, (1, KEY_BLOCK), 1)

    def block_of(j):
        return lax.rem(first_block + j, cache_total)

    def block_copy(which, source, block):
        rows = pl.ds(pl.multiple_of(lax.rem(block * KEY_BLOCK, half), KEY_BLOCK), KEY_BLOCK)
        into = pl.ds(pl.multiple_of(block * KEY_BLOCK, KEY_BLOCK), KEY_BLOCK)
        buf = (k_buf, v_buf)[which]
        return pltpu.make_async_copy(source.at[rows, lanes], buf.at[into], sems.at[which, block])

    for which, near, far in ((0, keys_near, keys_far), (1, values_near, values_far)):
        def start(j, unused, which=which, near=near, far=far):
            block = block_of(j)
            mine = block // (half // KEY_BLOCK) == dp

            @pl.when(mine)
            def _():
                block_copy(which, near, block).start()

            @pl.when(jnp.logical_not(mine))
            def _():
                block_copy(which, far, block).start()

            return 0

        if use_cache:
            lax.fori_loop(0, cache_blocks, start, 0)

    window_copies = []
    for which, buf, at in ((0, k_buf, kv_head), (1, v_buf, kv_count + kv_head)):
        for k, ref in enumerate(window):
            window_copies.append(
                pltpu.make_async_copy(
                    ref.at[:, at * HD : (at + 1) * HD],
                    buf.at[base + k * tok : base + (k + 1) * tok],
                    window_sems.at[which, k],
                )
            )
    for copy in window_copies:
        copy.start()
    depth = k_buf.shape[0]
    loose = base + (hops + 1) * tok
    if use_window and depth > loose:
        for buf in (k_buf, v_buf):
            buf[loose:depth, :] = jnp.zeros((depth - loose, HD), BF16)

    def score(offsets, biases):
        for h in range(heads):
            rows = slice(h * tok, (h + 1) * tok)
            best = best_buf[rows, :]
            for offset, bias in zip(offsets, biases):
                span = pl.ds(offset, KEY_BLOCK)
                scores = mm_nt(q_ref[:, h * HD : (h + 1) * HD], k_buf[span, :])
                scores = scores * LOG2_SCALE + bias
                s_buf[rows, span] = scores
                best = jnp.maximum(best, fold_lanes(scores, jnp.maximum))
            best_buf[rows, :] = best

    def mix(offsets):
        for h in range(heads):
            rows = slice(h * tok, (h + 1) * tok)
            best = best_buf[rows, :]
            total = total_buf[rows, :]
            acc = acc_buf[rows, :]
            for offset in offsets:
                probs = jnp.concatenate(
                    [
                        jnp.exp2(s_buf[rows, pl.ds(offset + k, 128)] - best)
                        for k in range(0, KEY_BLOCK, 128)
                    ],
                    axis=1,
                )
                total = total + fold_lanes(probs, jnp.add)
                acc = acc + mm(probs.astype(BF16), v_buf[pl.ds(offset, KEY_BLOCK), :])
            total_buf[rows, :] = total
            acc_buf[rows, :] = acc

    def sweep(visit):
        if not use_cache:
            return
        done = 0
        for size in GROUPS:
            if size > cache_total:
                continue
            count = (cache_blocks - done) // size

            def some(j, unused, size=size, done=done):
                visit([block_of(done + j * size + k) for k in range(size)])
                return 0

            lax.fori_loop(0, count, some, 0)
            done = done + count * size

    def place_of(block):
        return pl.multiple_of(block * KEY_BLOCK, KEY_BLOCK)

    def cache_score(blocks):
        offsets, biases = [], []
        for block in blocks:
            block_copy(0, keys_near, block).wait()
            offset = place_of(block)
            age = newest - (offset + lane)
            age = jnp.where(age < 0, age + slots, age)
            offsets.append(offset)
            biases.append(jnp.where(age < held, 0.0, NEG))
        score(offsets, biases)

    def cache_mix(blocks):
        for block in blocks:
            block_copy(1, values_near, block).wait()
        mix([place_of(block) for block in blocks])

    double = 2 * KEY_BLOCK
    window_pairs = (place * tok + tok + double - 1) // double

    def window_bias(at):
        if isinstance(at, int) and at * KEY_BLOCK < tok:
            later = (
                lax.broadcasted_iota(jnp.int32, (tok, KEY_BLOCK), 0)
                - lax.broadcasted_iota(jnp.int32, (tok, KEY_BLOCK), 1)
            )
            allowed = (later >= 0) | ((lane >= tok) & (lane < tok * (place + 1)))
        else:
            allowed = lane + at * KEY_BLOCK < tok * (place + 1)
        return jnp.where(allowed, 0.0, NEG)

    def window_offsets(j):
        return [pl.multiple_of(base + (2 * j + k) * KEY_BLOCK, KEY_BLOCK) for k in range(2)]

    if carry_in:
        best_buf[...] = jnp.broadcast_to(state_in[:, 0:1], best_buf.shape)
    else:
        best_buf[...] = jnp.full_like(best_buf, NEG)
    sweep(cache_score)
    if use_window:
        for copy in window_copies[: hops + 1]:
            copy.wait()
        score([base, base + KEY_BLOCK], [window_bias(0), window_bias(1)])

        def more_scores(j, unused):
            score(window_offsets(j), [window_bias(2 * j), window_bias(2 * j + 1)])
            return 0

        if depth > base + double:
            lax.fori_loop(1, window_pairs, more_scores, 0)
    best_buf[...] = jnp.broadcast_to(
        jnp.max(best_buf[...], axis=-1, keepdims=True), best_buf.shape
    )
    if carry_in:
        factor = jnp.exp2(jnp.broadcast_to(state_in[:, 0:1], best_buf.shape) - best_buf[...])
        first = lax.broadcasted_iota(jnp.int32, (1, 128), 1) == 127
        acc_buf[...] = factor * acc_in[...]
        total_buf[...] = jnp.where(first, factor * state_in[...], 0.0)
    else:
        acc_buf[...] = jnp.zeros_like(acc_buf)
        total_buf[...] = jnp.zeros_like(total_buf)
    sweep(cache_mix)
    if use_window:
        for copy in window_copies[hops + 1 :]:
            copy.wait()
        mix([base, base + KEY_BLOCK])

        def more_mix(j, unused):
            mix(window_offsets(j))
            return 0

        if depth > base + double:
            lax.fori_loop(1, window_pairs, more_mix, 0)
    for h in range(heads):
        rows = slice(h * tok, (h + 1) * tok)
        total = jnp.sum(total_buf[rows, :], axis=-1, keepdims=True)
        if final:
            outs[0][:, h * HD : (h + 1) * HD] = (acc_buf[rows, :] / total).astype(BF16)
        else:
            outs[0][rows, :] = acc_buf[rows, :]
            last = lax.broadcasted_iota(jnp.int32, (1, 128), 1) == 127
            outs[1][rows, :] = jnp.where(last, total, best_buf[rows, :])


def attend(scalars, queries, head, heads, kv_count, slots, cache=None, window=None, carry=None,
           into=None, final=True):
    tok = queries.shape[0]
    kv_head = head // (AH // KVH)
    hops = len(window) - 1 if window is not None else 0
    rows = heads * tok
    depth = slots if cache is not None else 0
    if window is not None:
        depth += -(-((hops + 1) * tok) // (2 * KEY_BLOCK)) * (2 * KEY_BLOCK)
    anywhere = pl.BlockSpec(memory_space=pl.ANY)
    part = pl.BlockSpec((tok, heads * HD), lambda k, s: (0, head // heads))
    whole = pl.BlockSpec((rows, 128), lambda k, s: (0, 0))
    operands, in_specs = [scalars, queries], [part]
    for group in (cache, window):
        if group is not None:
            operands += list(group)
            in_specs += [anywhere] * len(group)
    if carry is not None:
        operands += list(carry)
        in_specs += [whole] * 2
    aliases = {}
    if into is not None:
        aliases = {len(operands): 0}
        operands.append(into)
        in_specs.append(anywhere)
    if final:
        out_specs, out_shape = part, jax.ShapeDtypeStruct(queries.shape, BF16)
    else:
        out_specs, out_shape = [whole] * 2, [jax.ShapeDtypeStruct((rows, 128), F32)] * 2
    return pl.pallas_call(
        functools.partial(
            attend_kernel, kv_head=kv_head, kv_count=kv_count, heads=heads, hops=hops,
            slots=slots, use_cache=cache is not None, use_window=window is not None,
            carry_in=carry is not None, final=final, alias=len(aliases),
        ),
        grid_spec=pltpu.PrefetchScalarGridSpec(
            num_scalar_prefetch=1,
            grid=(1,),
            in_specs=in_specs,
            out_specs=out_specs,
            scratch_shapes=[
                pltpu.VMEM((depth, HD), BF16),
                pltpu.VMEM((depth, HD), BF16),
                pltpu.VMEM((rows, depth), F32),
                pltpu.VMEM((rows, 128), F32),
                pltpu.VMEM((rows, 128), F32),
                pltpu.VMEM((rows, 128), F32),
                pltpu.SemaphoreType.DMA((2, slots // KEY_BLOCK)),
                pltpu.SemaphoreType.DMA((2, hops + 1)),
            ],
        ),
        out_shape=out_shape,
        input_output_aliases=aliases,
        compiler_params=pltpu.CompilerParams(vmem_limit_bytes=VMEM_LIMIT),
        cost_estimate=pl.CostEstimate(
            flops=16 * rows * depth * HD, bytes_accessed=4 * depth * HD,
            transcendentals=rows * depth,
        ),
        name="attend",
    )(*operands)


def tie(*values):
    return lax.optimization_barrier(values)


def local(x_in, z_gate, b_in, c_in, dt_raw, dt_bias, a_log, d_skip, norm_weight, ssm_init, queries,
          keys, values, cache_keys, cache_values, window_start, prefix_len):
    tok, lanes = x_in.shape
    head_count = dt_raw.shape[1]
    per_group = MH // NG
    places = lax.axis_size("seq")
    place = lax.axis_index("seq")
    dp = lax.axis_index("dp")
    q_count = queries.shape[1] // HD
    kv_here = keys.shape[1] // HD
    kv_count = max(1, q_count * KVH // AH)
    width = min(lanes, STATE_WIDTH * kv_count * HD)
    chunks = lanes // width
    column = (dp * q_count) // (AH // KVH)
    slots = 2 * cache_keys.shape[0]

    ring = [(k, (k + 1) % places) for k in range(places)]
    swap = [(0, 1), (1, 0)]
    far_keys = lax.ppermute(cache_keys, "dp", swap)
    far_values = lax.ppermute(cache_values, "dp", swap)

    own_rows = jnp.concatenate(
        [
            lax.dynamic_slice_in_dim(array, column * HD, kv_count * HD, axis=1)
            for array in (keys, values)
        ],
        axis=1,
    )

    newest = jnp.mod(window_start[0] - 1, slots)
    held = prefix_len[0]
    oldest = jnp.mod(newest - held + 1, slots)
    first_block = oldest // KEY_BLOCK
    cache_blocks = jnp.minimum(
        slots // KEY_BLOCK, (oldest % KEY_BLOCK + held + KEY_BLOCK - 1) // KEY_BLOCK
    )
    first_head = dp * head_count
    scalars = jnp.stack(
        [place, dp, first_block, cache_blocks, newest, held, column, first_head]
    ).astype(jnp.int32)

    received = []
    send = own_rows
    arrived = lax.ppermute(send, "seq", ring)
    x_tied, send = tie(x_in, send)
    span = max(width, min(lanes, per_group * MP))
    states, rows, logt, dtt = ssm_states(
        scalars, x_tied, b_in, dt_raw, dt_bias, a_log, d_skip, ssm_init, width, span
    )
    received.append(arrived)

    cache = (cache_keys, far_keys, cache_values, far_values)
    heads = min(HEADS_IN_CALL, q_count)
    parts = list(range(0, q_count, heads))
    last_step = places - 1 + chunks - 1
    result = inner = opened = None
    slots_here = slots

    def attend_next(queries_now, into):
        window = [own_rows] + received[: places - 1]
        head, carry = parts.pop(0)
        return attend(
            scalars, queries_now, head, heads, kv_count, slots_here,
            cache=None if carry else cache, window=window, carry=carry, into=into,
        )

    parts = [(head, None) for head in parts]
    for step in range(1, last_step + 1):
        incoming = received[-1]
        if step == 1:
            incoming, states = tie(incoming, states)
        elif result is not None:
            incoming, result = tie(incoming, result)
        elif opened is not None:
            incoming, *opened = tie(incoming, *opened)
        else:
            incoming, inner = tie(incoming, inner)
        send = hop(place, incoming, states, rows, step)
        arrived = lax.ppermute(send, "seq", ring)
        if step == 1:
            x_tied, send = tie(x_in, send)
            inner = ssm_inner(scalars, x_tied, b_in, c_in, logt, dtt, rows, width)
        elif step == OPEN_STEP and len(parts) > 1:
            queries_now, send = tie(queries, send)
            head = parts.pop(0)[0]
            opened = attend(
                scalars, queries_now, head, heads, kv_count, slots_here, cache=cache, final=False
            )
            parts.append((head, opened))
        elif step >= places - 1 and parts:
            queries_now, send = tie(queries, send)
            if opened is not None and parts[0][1] is not None:
                parts[0] = (parts[0][0], opened)
            result = attend_next(queries_now, result)
        received.append(arrived)
    while parts:
        result = attend_next(queries, result)
    mamba_out = ssm_outputs(
        scalars, inner, z_gate, c_in, logt, norm_weight, ssm_init, received[1:], width
    )
    return (mamba_out, result)


def solution(mesh):
    rows = P(("groups", "seq"), ("tp", "dp"))
    shared = P(("groups", "seq"), "tp")
    heads = P(("tp", "dp"))
    cached = P(("groups", "dp"), "tp")
    return jax.shard_map(
        local,
        mesh=mesh,
        in_specs=(
            rows, rows, shared, shared, rows, heads, heads, heads, heads,
            P(("groups", "tp", "dp"), None, None), rows, shared, shared, cached, cached,
            P("groups"), P("groups"),
        ),
        out_specs=(rows, rows),
        check_vma=False,
    )
```

```python
import functools
import math

import jax
import jax.numpy as jnp
from jax import lax
from jax.experimental import pallas as pl
from jax.experimental.pallas import tpu as pltpu
from jax.sharding import PartitionSpec as P

MH = 128
MP = 64
N_STATE = 256
NG = 8
AH = 64
KVH = 8
HD = 128
BLOCK = 128
KEY_BLOCK = 512
GROUPS = (2, 1)
STATE_WIDTH = 4
HEADS_IN_CALL = 8
OPEN_STEP = 2
LOG2_SCALE = math.log2(math.e) / math.sqrt(HD)
NEG = -1e30
F32 = jnp.float32
BF16 = jnp.bfloat16
VMEM_LIMIT = 56 << 20


def mm(a, b):
    return jnp.dot(a, b, preferred_element_type=F32)


def mm_nt(a, b):
    return lax.dot_general(a, b, (((1,), (1,)), ((), ())), preferred_element_type=F32)


def pieces_of(value):
    first = value.astype(BF16)
    rest = value - first.astype(F32)
    second = rest.astype(BF16)
    third = (rest - second.astype(F32)).astype(BF16)
    return first, second, third


def head_table(heads, width):
    row = lax.broadcasted_iota(jnp.int32, (heads, width), 0)
    lane = lax.broadcasted_iota(jnp.int32, (heads, width), 1)
    table = jnp.where(lane // MP == row, 1.0, 0.0).astype(BF16)
    return jnp.concatenate([table] * 3, axis=0)


def expand(value, table):
    stacked = jnp.concatenate(pieces_of(value), axis=0)
    return lax.dot_general(stacked, table, (((0,), (0,)), ((), ())), preferred_element_type=F32)


def fold_lanes(value, op):
    parts = [value[:, k : k + 128] for k in range(0, value.shape[1], 128)]
    while len(parts) > 1:
        parts = [
            op(parts[k], parts[k + 1]) if k + 1 < len(parts) else parts[k]
            for k in range(0, len(parts), 2)
        ]
    return parts[0]


def ssm_states_kernel(
    scalars, x_ref, b_ref, dt_ref, bias_ref, alog_ref, dskip_ref, init_ref,
    state_ref, rows_ref, logt_ref, dtt_ref, dt_all, log_all, skip_all,
):
    span = pl.program_id(0)
    tok, lanes = x_ref.shape
    heads = lanes // MP
    spans = dt_ref.shape[0] // heads
    parts = state_ref.shape[0]
    width = lanes // parts

    @pl.when(span == 0)
    def _():
        column = lambda ref: jnp.broadcast_to(ref[...], (8, ref.shape[1])).T[:, 0:1]
        dt = jax.nn.softplus(dt_ref[...] + column(bias_ref))
        decay = -jnp.exp(column(alog_ref)) * dt
        row = lax.broadcasted_iota(jnp.int32, (BLOCK, BLOCK), 0)
        col = lax.broadcasted_iota(jnp.int32, (BLOCK, BLOCK), 1)
        upper = jnp.where(row <= col, 1.0, 0.0).astype(BF16)
        logs = []
        for blk in range(tok // BLOCK):
            first, second, third = pieces_of(decay[:, blk * BLOCK : (blk + 1) * BLOCK])
            logs.append(mm(first, upper) + mm(second, upper) + mm(third, upper))
        logs = jnp.concatenate(logs, axis=1)
        skip = jnp.broadcast_to(column(dskip_ref), (dt_ref.shape[0], 128))
        for k in range(spans):
            dt_all[k] = dt[k * heads : (k + 1) * heads]
            log_all[k] = logs[k * heads : (k + 1) * heads]
            skip_all[k] = skip[k * heads : (k + 1) * heads]

    dt = dt_all[span]
    logs = log_all[span]
    few = heads // parts
    for k in range(parts):
        logt_ref[k] = logs[k * few : (k + 1) * few]
        dtt_ref[k] = dt[k * few : (k + 1) * few]
    table = head_table(heads, lanes)
    state = None
    total = jnp.zeros((heads, 1), F32)
    for blk in range(tok // BLOCK):
        part = slice(blk * BLOCK, (blk + 1) * BLOCK)
        end = logs[:, (blk + 1) * BLOCK - 1 : (blk + 1) * BLOCK]
        tail = jnp.exp(end - logs[:, part]) * dt[:, part]
        weighted = (expand(tail, table) * x_ref[part, :].astype(F32)).astype(BF16)
        update = mm(b_ref[part, :].T, weighted)
        if state is None:
            state = update
        else:
            state = expand(jnp.broadcast_to(jnp.exp(end), (heads, 8)), table)[0:1] * state + update
        total = total + end
    place = scalars[0]
    lane = lax.broadcasted_iota(jnp.int32, (heads, 8), 1)
    rows = expand(jnp.where(lane == 0, jnp.exp(total), skip_all[span][:, 0:8]), table)
    for k in range(parts):
        state_ref[k] = state[:, k * width : (k + 1) * width]
        rows_ref[k] = rows[:, k * width : (k + 1) * width]

    @pl.when(place == 0)
    def _():
        for k in range(parts):
            first = init_ref[k * few : (k + 1) * few].reshape(width, N_STATE).T
            state_ref[k] = state_ref[k] + rows_ref[k, 0:1, :] * first
            rows_ref[k, 0:1, :] = jnp.zeros((1, width), F32)


def ssm_states(scalars, x_in, b_in, dt_raw, dt_bias, a_log, d_skip, ssm_init, width, span):
    tok, lanes = x_in.shape
    chunks = lanes // width
    head_count = dt_raw.shape[1]
    heads = span // MP
    few = width // MP
    parts = span // width
    per_group = MH // NG
    flat = lambda c, s: (0, 0)
    major = lambda c, s: (c, 0, 0)
    return pl.pallas_call(
        ssm_states_kernel,
        grid_spec=pltpu.PrefetchScalarGridSpec(
            num_scalar_prefetch=1,
            grid=(lanes // span,),
            in_specs=[
                pl.BlockSpec((tok, span), lambda c, s: (0, c)),
                pl.BlockSpec((tok, N_STATE), lambda c, s: (0, (s[7] + c * heads) // per_group)),
                pl.BlockSpec((head_count, tok), flat),
                pl.BlockSpec((1, head_count), flat),
                pl.BlockSpec((1, head_count), flat),
                pl.BlockSpec((1, head_count), flat),
                pl.BlockSpec((heads, MP, N_STATE), major),
            ],
            out_specs=[
                pl.BlockSpec((parts, N_STATE, width), major),
                pl.BlockSpec((parts, 8, width), major),
                pl.BlockSpec((parts, few, tok), major),
                pl.BlockSpec((parts, few, tok), major),
            ],
            scratch_shapes=[
                pltpu.VMEM((lanes // span, heads, tok), F32),
                pltpu.VMEM((lanes // span, heads, tok), F32),
                pltpu.VMEM((lanes // span, heads, 128), F32),
            ],
        ),
        out_shape=[
            jax.ShapeDtypeStruct((chunks, N_STATE, width), F32),
            jax.ShapeDtypeStruct((chunks, 8, width), F32),
            jax.ShapeDtypeStruct((chunks, few, tok), F32),
            jax.ShapeDtypeStruct((chunks, few, tok), F32),
        ],
        compiler_params=pltpu.CompilerParams(vmem_limit_bytes=VMEM_LIMIT),
        cost_estimate=pl.CostEstimate(
            flops=2 * tok * lanes * N_STATE * 4, bytes_accessed=6 << 20, transcendentals=1 << 16
        ),
        name="ssm_states",
    )(
        scalars, x_in, b_in, dt_raw.T, dt_bias[None, :], a_log[None, :], d_skip[None, :], ssm_init
    )


def hop(place, received, states, rows, step):
    chunks, unused, width = states.shape
    if received.shape[1] < width:
        received = jnp.pad(received, ((0, 0), (0, width - received.shape[1])))
    chunk = jnp.clip(step - 1 - place, 0, chunks - 1)
    state = lax.dynamic_index_in_dim(states, chunk, 0, keepdims=False)
    decay = lax.dynamic_index_in_dim(rows, chunk, 0, keepdims=False)[0:1, :]
    combined = (decay * received.astype(F32) + state).astype(BF16)
    return jnp.where(step <= place, received, combined)


def ssm_inner_kernel(scalars, x_ref, b_ref, c_ref, logt_ref, dtt_ref, rows_ref, out_ref):
    tok, width = x_ref.shape
    heads = width // MP
    row = lax.broadcasted_iota(jnp.int32, (BLOCK, BLOCK), 0)
    col = lax.broadcasted_iota(jnp.int32, (BLOCK, BLOCK), 1)
    lower = row >= col
    low_half = col < MP
    table = head_table(heads, width)
    logt = logt_ref[0]
    dtt = dtt_ref[0]
    logs = logt.T
    skip = rows_ref[0, 1:2, :]
    state = None
    pairs = heads // 2
    for blk in range(tok // BLOCK):
        part = slice(blk * BLOCK, (blk + 1) * BLOCK)
        c_blk = c_ref[part, :]
        b_blk = b_ref[part, :]
        x_blk = x_ref[part, :]
        products = mm_nt(c_blk, b_blk)
        log_blk = logs[part]
        kernels = []
        for h in range(heads):
            spread = log_blk[:, h : h + 1] - logt[h : h + 1, part]
            decay = jnp.exp(jnp.where(lower, spread, NEG))
            kernels.append((decay * products * dtt[h : h + 1, part]).astype(BF16))
        carried = None
        if state is not None:
            carried = expand(jnp.exp(logt[:, part]), table) * mm(c_blk, state.astype(BF16))
        if (blk + 1) * BLOCK < tok:
            end = logt[:, (blk + 1) * BLOCK - 1 : (blk + 1) * BLOCK]
            tail = jnp.exp(end - logt[:, part]) * dtt[:, part]
            weighted = (expand(tail, table) * x_blk.astype(F32)).astype(BF16)
            update = mm(b_blk.T, weighted)
            if state is None:
                state = update
            else:
                factor = expand(jnp.broadcast_to(jnp.exp(end), (heads, 8)), table)[0:1]
                state = factor * state + update
        for pair in range(pairs):
            lanes = slice(pair * 128, (pair + 1) * 128)
            x_pair = x_blk[:, lanes]
            zero = jnp.zeros_like(x_pair)
            stacked = jnp.concatenate(
                [jnp.where(low_half, x_pair, zero), jnp.where(low_half, zero, x_pair)], axis=0
            )
            inner = mm(jnp.concatenate(kernels[2 * pair : 2 * pair + 2], axis=1), stacked)
            value = inner + skip[:, lanes] * x_pair.astype(F32)
            if carried is not None:
                value = value + carried[:, lanes]
            out_ref[part, lanes] = value


def ssm_inner(scalars, x_in, b_in, c_in, logt, dtt, rows, width):
    tok, lanes = x_in.shape
    chunks = lanes // width
    heads = width // MP
    per_group = MH // NG
    per_chunk = pl.BlockSpec((tok, width), lambda c, s: (0, c))
    grouped = pl.BlockSpec((tok, N_STATE), lambda c, s: (0, (s[7] + c * heads) // per_group))
    major = lambda c, s: (c, 0, 0)
    return pl.pallas_call(
        ssm_inner_kernel,
        grid_spec=pltpu.PrefetchScalarGridSpec(
            num_scalar_prefetch=1,
            grid=(chunks,),
            in_specs=[
                per_chunk,
                grouped,
                grouped,
                pl.BlockSpec((1, heads, tok), major),
                pl.BlockSpec((1, heads, tok), major),
                pl.BlockSpec((1, 8, width), major),
            ],
            out_specs=per_chunk,
        ),
        out_shape=jax.ShapeDtypeStruct((tok, lanes), F32),
        compiler_params=pltpu.CompilerParams(vmem_limit_bytes=VMEM_LIMIT),
        cost_estimate=pl.CostEstimate(
            flops=2 * tok * lanes * N_STATE * 8, bytes_accessed=6 << 20, transcendentals=1 << 21
        ),
        name="ssm_inner",
    )(scalars, x_in, b_in, c_in, logt, dtt, rows)


def ssm_outputs_kernel(
    scalars, inner_ref, z_ref, c_ref, logt_ref, norm_ref, init_hbm, *rest, hops, chunk, alias,
):
    received = rest[:hops]
    out_ref, carry, init_buf, sem = rest[hops + alias :]
    place = scalars[0]
    tok, width = inner_ref.shape
    heads = width // MP

    for r in range(hops):
        @pl.when(place == r + 1)
        def _():
            pltpu.make_async_copy(received[r], carry, sem).start()

    @pl.when(place == 0)
    def _():
        piece = pltpu.make_async_copy(
            init_hbm.at[chunk * heads : (chunk + 1) * heads], init_buf, sem
        )
        piece.start()
        piece.wait()
        carry[...] = init_buf[...].reshape(width, N_STATE).astype(BF16).T

    row = lax.broadcasted_iota(jnp.int32, (BLOCK, BLOCK), 0)
    col = lax.broadcasted_iota(jnp.int32, (BLOCK, BLOCK), 1)
    mean_table = jnp.where(row // MP == col // MP, 1.0 / MP, 0.0).astype(BF16)
    mean_table = jnp.concatenate([mean_table, mean_table], axis=0)
    table = head_table(heads, width)
    logt = logt_ref[0]
    whole_logs = []
    before = jnp.zeros((heads, 1), F32)
    for blk in range(tok // BLOCK):
        part = slice(blk * BLOCK, (blk + 1) * BLOCK)
        whole_logs.append(jnp.exp(logt[:, part] + before))
        before = before + logt[:, (blk + 1) * BLOCK - 1 : (blk + 1) * BLOCK]
    spread = expand(jnp.concatenate(whole_logs, axis=1), table)
    z = z_ref[...].astype(F32)
    gate = z / (1.0 + jnp.exp(-z))

    @pl.when(place > 0)
    def _():
        pltpu.make_async_copy(received[0], carry, sem).wait()

    gated = (inner_ref[...] + spread * mm(c_ref[...], carry[...])) * gate
    square = gated * gated
    high = square.astype(BF16)
    low = (square - high.astype(F32)).astype(BF16)
    for at in range(0, width, 128):
        lanes = slice(at, at + 128)
        mean = mm(jnp.concatenate([high[:, lanes], low[:, lanes]], axis=1), mean_table)
        normed = gated[:, lanes] * lax.rsqrt(mean + 1e-05) * norm_ref[:, lanes]
        out_ref[:, lanes] = normed.astype(BF16)


def ssm_outputs(scalars, inner, z_gate, c_in, logt, norm_weight, ssm_init, received, width, chunk,
                into):
    tok, lanes = inner.shape
    heads = width // MP
    per_group = MH // NG
    anywhere = pl.BlockSpec(memory_space=pl.ANY)
    per_chunk = pl.BlockSpec((tok, width), lambda k, s: (0, chunk))
    operands = [scalars, inner, z_gate, c_in, logt, norm_weight[None, :], ssm_init, *received]
    in_specs = [
        per_chunk,
        per_chunk,
        pl.BlockSpec((tok, N_STATE), lambda k, s: (0, (s[7] + chunk * heads) // per_group)),
        pl.BlockSpec((1, heads, tok), lambda k, s: (chunk, 0, 0)),
        pl.BlockSpec((1, width), lambda k, s: (0, chunk)),
    ] + [anywhere] * (1 + len(received))
    aliases = {}
    if into is not None:
        aliases = {len(operands): 0}
        operands.append(into)
        in_specs.append(anywhere)
    return pl.pallas_call(
        functools.partial(
            ssm_outputs_kernel, hops=len(received), chunk=chunk, alias=len(aliases)
        ),
        grid_spec=pltpu.PrefetchScalarGridSpec(
            num_scalar_prefetch=1,
            grid=(1,),
            in_specs=in_specs,
            out_specs=per_chunk,
            scratch_shapes=[
                pltpu.VMEM((N_STATE, width), BF16),
                pltpu.VMEM((heads, MP, N_STATE), F32),
                pltpu.SemaphoreType.DMA,
            ],
        ),
        out_shape=jax.ShapeDtypeStruct((tok, lanes), BF16),
        input_output_aliases=aliases,
        compiler_params=pltpu.CompilerParams(vmem_limit_bytes=VMEM_LIMIT),
        cost_estimate=pl.CostEstimate(
            flops=2 * tok * width * N_STATE * 2, bytes_accessed=2 << 20, transcendentals=1 << 18
        ),
        name="ssm_outputs",
    )(*operands)


def attend_kernel(scalars, q_ref, *rest, kv_head, kv_count, heads, hops, slots, use_cache,
                  use_window, carry_in, final, alias):
    rest = list(rest)
    take = lambda count: [rest.pop(0) for _ in range(count)]
    keys_near, keys_far, values_near, values_far = take(4) if use_cache else [None] * 4
    window = take(hops + 1) if use_window else []
    acc_in, state_in = take(2) if carry_in else (None, None)
    take(alias)
    outs = take(1 if final else 2)
    k_buf, v_buf, s_buf, best_buf, total_buf, acc_buf, sems, window_sems = rest
    place, dp, first_block, cache_blocks, newest, held = (scalars[k] for k in range(6))
    column = scalars[6]
    tok = q_ref.shape[0]
    half = slots // 2
    cache_total = slots // KEY_BLOCK
    base = slots if use_cache else 0
    lanes = pl.ds(pl.multiple_of((column + kv_head) * HD, HD), HD)
    lane = lax.broadcasted_iota(jnp.int32, (1, KEY_BLOCK), 1)

    def block_of(j):
        return lax.rem(first_block + j, cache_total)

    def block_copy(which, source, block):
        rows = pl.ds(pl.multiple_of(lax.rem(block * KEY_BLOCK, half), KEY_BLOCK), KEY_BLOCK)
        into = pl.ds(pl.multiple_of(block * KEY_BLOCK, KEY_BLOCK), KEY_BLOCK)
        buf = (k_buf, v_buf)[which]
        return pltpu.make_async_copy(source.at[rows, lanes], buf.at[into], sems.at[which, block])

    for which, near, far in ((0, keys_near, keys_far), (1, values_near, values_far)):
        def start(j, unused, which=which, near=near, far=far):
            block = block_of(j)
            mine = block // (half // KEY_BLOCK) == dp

            @pl.when(mine)
            def _():
                block_copy(which, near, block).start()

            @pl.when(jnp.logical_not(mine))
            def _():
                block_copy(which, far, block).start()

            return 0

        if use_cache:
            lax.fori_loop(0, cache_blocks, start, 0)

    window_copies = []
    for which, buf, at in ((0, k_buf, kv_head), (1, v_buf, kv_count + kv_head)):
        for k, ref in enumerate(window):
            window_copies.append(
                pltpu.make_async_copy(
                    ref.at[:, at * HD : (at + 1) * HD],
                    buf.at[base + k * tok : base + (k + 1) * tok],
                    window_sems.at[which, k],
                )
            )
    for copy in window_copies:
        copy.start()
    depth = k_buf.shape[0]
    loose = base + (hops + 1) * tok
    if use_window and depth > loose:
        for buf in (k_buf, v_buf):
            buf[loose:depth, :] = jnp.zeros((depth - loose, HD), BF16)

    def score(offsets, biases):
        for h in range(heads):
            rows = slice(h * tok, (h + 1) * tok)
            best = best_buf[rows, :]
            for offset, bias in zip(offsets, biases):
                span = pl.ds(offset, KEY_BLOCK)
                scores = mm_nt(q_ref[:, h * HD : (h + 1) * HD], k_buf[span, :])
                scores = scores * LOG2_SCALE + bias
                s_buf[rows, span] = scores
                best = jnp.maximum(best, fold_lanes(scores, jnp.maximum))
            best_buf[rows, :] = best

    def mix(offsets):
        for h in range(heads):
            rows = slice(h * tok, (h + 1) * tok)
            best = best_buf[rows, :]
            total = total_buf[rows, :]
            acc = acc_buf[rows, :]
            for offset in offsets:
                probs = jnp.concatenate(
                    [
                        jnp.exp2(s_buf[rows, pl.ds(offset + k, 128)] - best)
                        for k in range(0, KEY_BLOCK, 128)
                    ],
                    axis=1,
                )
                total = total + fold_lanes(probs, jnp.add)
                acc = acc + mm(probs.astype(BF16), v_buf[pl.ds(offset, KEY_BLOCK), :])
            total_buf[rows, :] = total
            acc_buf[rows, :] = acc

    def sweep(visit):
        if not use_cache:
            return
        done = 0
        for size in GROUPS:
            if size > cache_total:
                continue
            count = (cache_blocks - done) // size

            def some(j, unused, size=size, done=done):
                visit([block_of(done + j * size + k) for k in range(size)])
                return 0

            lax.fori_loop(0, count, some, 0)
            done = done + count * size

    def place_of(block):
        return pl.multiple_of(block * KEY_BLOCK, KEY_BLOCK)

    def cache_score(blocks):
        offsets, biases = [], []
        for block in blocks:
            block_copy(0, keys_near, block).wait()
            offset = place_of(block)
            age = newest - (offset + lane)
            age = jnp.where(age < 0, age + slots, age)
            offsets.append(offset)
            biases.append(jnp.where(age < held, 0.0, NEG))
        score(offsets, biases)

    def cache_mix(blocks):
        for block in blocks:
            block_copy(1, values_near, block).wait()
        mix([place_of(block) for block in blocks])

    double = 2 * KEY_BLOCK
    window_pairs = (place * tok + tok + double - 1) // double

    def window_bias(at):
        if isinstance(at, int) and at * KEY_BLOCK < tok:
            later = (
                lax.broadcasted_iota(jnp.int32, (tok, KEY_BLOCK), 0)
                - lax.broadcasted_iota(jnp.int32, (tok, KEY_BLOCK), 1)
            )
            allowed = (later >= 0) | ((lane >= tok) & (lane < tok * (place + 1)))
        else:
            allowed = lane + at * KEY_BLOCK < tok * (place + 1)
        return jnp.where(allowed, 0.0, NEG)

    def window_offsets(j):
        return [pl.multiple_of(base + (2 * j + k) * KEY_BLOCK, KEY_BLOCK) for k in range(2)]

    if carry_in:
        best_buf[...] = jnp.broadcast_to(state_in[:, 0:1], best_buf.shape)
    else:
        best_buf[...] = jnp.full_like(best_buf, NEG)
    sweep(cache_score)
    if use_window:
        for copy in window_copies[: hops + 1]:
            copy.wait()
        score([base, base + KEY_BLOCK], [window_bias(0), window_bias(1)])

        def more_scores(j, unused):
            score(window_offsets(j), [window_bias(2 * j), window_bias(2 * j + 1)])
            return 0

        if depth > base + double:
            lax.fori_loop(1, window_pairs, more_scores, 0)
    best_buf[...] = jnp.broadcast_to(
        jnp.max(best_buf[...], axis=-1, keepdims=True), best_buf.shape
    )
    if carry_in:
        factor = jnp.exp2(jnp.broadcast_to(state_in[:, 0:1], best_buf.shape) - best_buf[...])
        first = lax.broadcasted_iota(jnp.int32, (1, 128), 1) == 127
        acc_buf[...] = factor * acc_in[...]
        total_buf[...] = jnp.where(first, factor * state_in[...], 0.0)
    else:
        acc_buf[...] = jnp.zeros_like(acc_buf)
        total_buf[...] = jnp.zeros_like(total_buf)
    sweep(cache_mix)
    if use_window:
        for copy in window_copies[hops + 1 :]:
            copy.wait()
        mix([base, base + KEY_BLOCK])

        def more_mix(j, unused):
            mix(window_offsets(j))
            return 0

        if depth > base + double:
            lax.fori_loop(1, window_pairs, more_mix, 0)
    for h in range(heads):
        rows = slice(h * tok, (h + 1) * tok)
        total = jnp.sum(total_buf[rows, :], axis=-1, keepdims=True)
        if final:
            outs[0][:, h * HD : (h + 1) * HD] = (acc_buf[rows, :] / total).astype(BF16)
        else:
            outs[0][rows, :] = acc_buf[rows, :]
            last = lax.broadcasted_iota(jnp.int32, (1, 128), 1) == 127
            outs[1][rows, :] = jnp.where(last, total, best_buf[rows, :])


def attend(scalars, queries, head, heads, kv_count, slots, cache=None, window=None, carry=None,
           into=None, final=True):
    tok = queries.shape[0]
    kv_head = head // (AH // KVH)
    hops = len(window) - 1 if window is not None else 0
    rows = heads * tok
    depth = slots if cache is not None else 0
    if window is not None:
        depth += -(-((hops + 1) * tok) // (2 * KEY_BLOCK)) * (2 * KEY_BLOCK)
    anywhere = pl.BlockSpec(memory_space=pl.ANY)
    part = pl.BlockSpec((tok, heads * HD), lambda k, s: (0, head // heads))
    whole = pl.BlockSpec((rows, 128), lambda k, s: (0, 0))
    operands, in_specs = [scalars, queries], [part]
    for group in (cache, window):
        if group is not None:
            operands += list(group)
            in_specs += [anywhere] * len(group)
    if carry is not None:
        operands += list(carry)
        in_specs += [whole] * 2
    aliases = {}
    if into is not None:
        aliases = {len(operands): 0}
        operands.append(into)
        in_specs.append(anywhere)
    if final:
        out_specs, out_shape = part, jax.ShapeDtypeStruct(queries.shape, BF16)
    else:
        out_specs, out_shape = [whole] * 2, [jax.ShapeDtypeStruct((rows, 128), F32)] * 2
    return pl.pallas_call(
        functools.partial(
            attend_kernel, kv_head=kv_head, kv_count=kv_count, heads=heads, hops=hops,
            slots=slots, use_cache=cache is not None, use_window=window is not None,
            carry_in=carry is not None, final=final, alias=len(aliases),
        ),
        grid_spec=pltpu.PrefetchScalarGridSpec(
            num_scalar_prefetch=1,
            grid=(1,),
            in_specs=in_specs,
            out_specs=out_specs,
            scratch_shapes=[
                pltpu.VMEM((depth, HD), BF16),
                pltpu.VMEM((depth, HD), BF16),
                pltpu.VMEM((rows, depth), F32),
                pltpu.VMEM((rows, 128), F32),
                pltpu.VMEM((rows, 128), F32),
                pltpu.VMEM((rows, 128), F32),
                pltpu.SemaphoreType.DMA((2, slots // KEY_BLOCK)),
                pltpu.SemaphoreType.DMA((2, hops + 1)),
            ],
        ),
        out_shape=out_shape,
        input_output_aliases=aliases,
        compiler_params=pltpu.CompilerParams(vmem_limit_bytes=VMEM_LIMIT),
        cost_estimate=pl.CostEstimate(
            flops=16 * rows * depth * HD, bytes_accessed=4 * depth * HD,
            transcendentals=rows * depth,
        ),
        name="attend",
    )(*operands)


def tie(*values):
    return lax.optimization_barrier(values)


def local(x_in, z_gate, b_in, c_in, dt_raw, dt_bias, a_log, d_skip, norm_weight, ssm_init, queries,
          keys, values, cache_keys, cache_values, window_start, prefix_len):
    tok, lanes = x_in.shape
    head_count = dt_raw.shape[1]
    per_group = MH // NG
    places = lax.axis_size("seq")
    place = lax.axis_index("seq")
    dp = lax.axis_index("dp")
    q_count = queries.shape[1] // HD
    kv_here = keys.shape[1] // HD
    kv_count = max(1, q_count * KVH // AH)
    width = min(lanes, STATE_WIDTH * kv_count * HD)
    chunks = lanes // width
    column = (dp * q_count) // (AH // KVH)
    slots = 2 * cache_keys.shape[0]

    ring = [(k, (k + 1) % places) for k in range(places)]
    swap = [(0, 1), (1, 0)]
    far_keys = lax.ppermute(cache_keys, "dp", swap)
    far_values = lax.ppermute(cache_values, "dp", swap)

    own_rows = jnp.concatenate(
        [
            lax.dynamic_slice_in_dim(array, column * HD, kv_count * HD, axis=1)
            for array in (keys, values)
        ],
        axis=1,
    )

    newest = jnp.mod(window_start[0] - 1, slots)
    held = prefix_len[0]
    oldest = jnp.mod(newest - held + 1, slots)
    first_block = oldest // KEY_BLOCK
    cache_blocks = jnp.minimum(
        slots // KEY_BLOCK, (oldest % KEY_BLOCK + held + KEY_BLOCK - 1) // KEY_BLOCK
    )
    first_head = dp * head_count
    scalars = jnp.stack(
        [place, dp, first_block, cache_blocks, newest, held, column, first_head]
    ).astype(jnp.int32)

    received = []
    send = own_rows
    arrived = lax.ppermute(send, "seq", ring)
    x_tied, send = tie(x_in, send)
    span = max(width, min(lanes, per_group * MP))
    states, rows, logt, dtt = ssm_states(
        scalars, x_tied, b_in, dt_raw, dt_bias, a_log, d_skip, ssm_init, width, span
    )
    received.append(arrived)

    cache = (cache_keys, far_keys, cache_values, far_values)
    heads = min(HEADS_IN_CALL, q_count)
    parts = list(range(0, q_count, heads))
    last_step = places - 1 + chunks - 1
    result = inner = opened = mamba_out = None
    outputs_done = 0

    def outputs(chunk, into):
        return ssm_outputs(
            scalars, inner, z_gate, c_in, logt, norm_weight, ssm_init,
            received[chunk + 1 : chunk + places], width, chunk, into,
        )

    slots_here = slots

    def attend_next(queries_now, into):
        window = [own_rows] + received[: places - 1]
        head, carry = parts.pop(0)
        return attend(
            scalars, queries_now, head, heads, kv_count, slots_here,
            cache=None if carry else cache, window=window, carry=carry, into=into,
        )

    parts = [(head, None) for head in parts]
    for step in range(1, last_step + 1):
        incoming = received[-1]
        if step == 1:
            incoming, states = tie(incoming, states)
        elif result is not None:
            incoming, result = tie(incoming, result)
        elif opened is not None:
            incoming, *opened = tie(incoming, *opened)
        else:
            incoming, inner = tie(incoming, inner)
        send = hop(place, incoming, states, rows, step)
        senders = range(max(0, step - chunks), places - 1)
        pairs = ring if len(senders) == places - 1 else [(k, k + 1) for k in senders]
        arrived = lax.ppermute(send, "seq", pairs)
        if step == 1:
            x_tied, send = tie(x_in, send)
            inner = ssm_inner(scalars, x_tied, b_in, c_in, logt, dtt, rows, width)
        elif step == OPEN_STEP and len(parts) > 1:
            queries_now, send = tie(queries, send)
            head = parts.pop(0)[0]
            opened = attend(
                scalars, queries_now, head, heads, kv_count, slots_here, cache=cache, final=False
            )
            parts.append((head, opened))
        elif step >= places - 1 and parts:
            queries_now, send = tie(queries, send)
            if opened is not None and parts[0][1] is not None:
                parts[0] = (parts[0][0], opened)
            result = attend_next(queries_now, result)
            if step == last_step and chunks > 1:
                logt, send = tie(logt, send)
                mamba_out = outputs(0, mamba_out)
                outputs_done = 1
        received.append(arrived)
    while parts:
        result = attend_next(queries, result)
    for chunk in range(outputs_done, chunks):
        mamba_out = outputs(chunk, mamba_out)
    return (mamba_out, result)


def solution(mesh):
    rows = P(("groups", "seq"), ("tp", "dp"))
    shared = P(("groups", "seq"), "tp")
    heads = P(("tp", "dp"))
    cached = P(("groups", "dp"), "tp")
    return jax.shard_map(
        local,
        mesh=mesh,
        in_specs=(
            rows, rows, shared, shared, rows, heads, heads, heads, heads,
            P(("groups", "tp", "dp"), None, None), rows, shared, shared, cached, cached,
            P("groups"), P("groups"),
        ),
        out_specs=(rows, rows),
        check_vma=False,
    )
```

```python
import functools
import math

import jax
import jax.numpy as jnp
from jax import lax
from jax.experimental import pallas as pl
from jax.experimental.pallas import tpu as pltpu
from jax.sharding import PartitionSpec as P

MH = 128
MP = 64
N_STATE = 256
NG = 8
AH = 64
KVH = 8
HD = 128
BLOCK = 128
KEY_BLOCK = 512
GROUPS = (2, 1)
STATE_WIDTH = 4
HEADS_IN_CALL = 8
OPEN_STEP = 2
LOG2_SCALE = math.log2(math.e) / math.sqrt(HD)
NEG = -1e30
F32 = jnp.float32
BF16 = jnp.bfloat16
VMEM_LIMIT = 56 << 20


SCALARS = pl.BlockSpec(memory_space=pltpu.SMEM)


def group_lanes(scalars, head):
    group = (scalars[7] + head) // (MH // NG)
    return pl.ds(pl.multiple_of(group * N_STATE, N_STATE), N_STATE)


def mm(a, b):
    return jnp.dot(a, b, preferred_element_type=F32)


def mm_nt(a, b):
    return lax.dot_general(a, b, (((1,), (1,)), ((), ())), preferred_element_type=F32)


def pieces_of(value):
    first = value.astype(BF16)
    rest = value - first.astype(F32)
    second = rest.astype(BF16)
    third = (rest - second.astype(F32)).astype(BF16)
    return first, second, third


def head_table(heads, width):
    row = lax.broadcasted_iota(jnp.int32, (heads, width), 0)
    lane = lax.broadcasted_iota(jnp.int32, (heads, width), 1)
    table = jnp.where(lane // MP == row, 1.0, 0.0).astype(BF16)
    return jnp.concatenate([table] * 3, axis=0)


def expand(value, table):
    stacked = jnp.concatenate(pieces_of(value), axis=0)
    return lax.dot_general(stacked, table, (((0,), (0,)), ((), ())), preferred_element_type=F32)


def fold_lanes(value, op):
    parts = [value[:, k : k + 128] for k in range(0, value.shape[1], 128)]
    while len(parts) > 1:
        parts = [
            op(parts[k], parts[k + 1]) if k + 1 < len(parts) else parts[k]
            for k in range(0, len(parts), 2)
        ]
    return parts[0]


def ssm_states_kernel(
    scalars, x_ref, b_ref, dt_ref, bias_ref, alog_ref, dskip_ref, init_ref,
    state_ref, rows_ref, logt_ref, dtt_ref, dt_all, log_all, skip_all,
):
    span = pl.program_id(0)
    tok, lanes = x_ref.shape
    heads = lanes // MP
    spans = dt_ref.shape[0] // heads
    parts = state_ref.shape[0]
    width = lanes // parts
    group = group_lanes(scalars, span * heads)

    @pl.when(span == 0)
    def _():
        column = lambda ref: jnp.broadcast_to(ref[...], (8, ref.shape[1])).T[:, 0:1]
        dt = jax.nn.softplus(dt_ref[...] + column(bias_ref))
        decay = -jnp.exp(column(alog_ref)) * dt
        row = lax.broadcasted_iota(jnp.int32, (BLOCK, BLOCK), 0)
        col = lax.broadcasted_iota(jnp.int32, (BLOCK, BLOCK), 1)
        upper = jnp.where(row <= col, 1.0, 0.0).astype(BF16)
        logs = []
        for blk in range(tok // BLOCK):
            first, second, third = pieces_of(decay[:, blk * BLOCK : (blk + 1) * BLOCK])
            logs.append(mm(first, upper) + mm(second, upper) + mm(third, upper))
        logs = jnp.concatenate(logs, axis=1)
        skip = jnp.broadcast_to(column(dskip_ref), (dt_ref.shape[0], 128))
        for k in range(spans):
            dt_all[k] = dt[k * heads : (k + 1) * heads]
            log_all[k] = logs[k * heads : (k + 1) * heads]
            skip_all[k] = skip[k * heads : (k + 1) * heads]

    dt = dt_all[span]
    logs = log_all[span]
    few = heads // parts
    for k in range(parts):
        logt_ref[k] = logs[k * few : (k + 1) * few]
        dtt_ref[k] = dt[k * few : (k + 1) * few]
    table = head_table(heads, lanes)
    state = None
    total = jnp.zeros((heads, 1), F32)
    for blk in range(tok // BLOCK):
        part = slice(blk * BLOCK, (blk + 1) * BLOCK)
        end = logs[:, (blk + 1) * BLOCK - 1 : (blk + 1) * BLOCK]
        tail = jnp.exp(end - logs[:, part]) * dt[:, part]
        weighted = (expand(tail, table) * x_ref[part, :].astype(F32)).astype(BF16)
        update = mm(b_ref[part, group].T, weighted)
        if state is None:
            state = update
        else:
            state = expand(jnp.broadcast_to(jnp.exp(end), (heads, 8)), table)[0:1] * state + update
        total = total + end
    place = scalars[0]
    lane = lax.broadcasted_iota(jnp.int32, (heads, 8), 1)
    rows = expand(jnp.where(lane == 0, jnp.exp(total), skip_all[span][:, 0:8]), table)
    for k in range(parts):
        state_ref[k] = state[:, k * width : (k + 1) * width]
        rows_ref[k] = rows[:, k * width : (k + 1) * width]

    @pl.when(place == 0)
    def _():
        for k in range(parts):
            first = init_ref[k * few : (k + 1) * few].reshape(width, N_STATE).T
            state_ref[k] = state_ref[k] + rows_ref[k, 0:1, :] * first
            rows_ref[k, 0:1, :] = jnp.zeros((1, width), F32)


def ssm_states(scalars, x_in, b_in, dt_raw, dt_bias, a_log, d_skip, ssm_init, width, span):
    tok, lanes = x_in.shape
    chunks = lanes // width
    head_count = dt_raw.shape[1]
    heads = span // MP
    few = width // MP
    parts = span // width
    flat = lambda c: (0, 0)
    major = lambda c: (c, 0, 0)
    return pl.pallas_call(
        ssm_states_kernel,
        grid_spec=pl.GridSpec(
            grid=(lanes // span,),
            in_specs=[
                SCALARS,
                pl.BlockSpec((tok, span), lambda c: (0, c)),
                pl.BlockSpec(b_in.shape, flat),
                pl.BlockSpec((head_count, tok), flat),
                pl.BlockSpec((1, head_count), flat),
                pl.BlockSpec((1, head_count), flat),
                pl.BlockSpec((1, head_count), flat),
                pl.BlockSpec((heads, MP, N_STATE), major),
            ],
            out_specs=[
                pl.BlockSpec((parts, N_STATE, width), major),
                pl.BlockSpec((parts, 8, width), major),
                pl.BlockSpec((parts, few, tok), major),
                pl.BlockSpec((parts, few, tok), major),
            ],
            scratch_shapes=[
                pltpu.VMEM((lanes // span, heads, tok), F32),
                pltpu.VMEM((lanes // span, heads, tok), F32),
                pltpu.VMEM((lanes // span, heads, 128), F32),
            ],
        ),
        out_shape=[
            jax.ShapeDtypeStruct((chunks, N_STATE, width), F32),
            jax.ShapeDtypeStruct((chunks, 8, width), F32),
            jax.ShapeDtypeStruct((chunks, few, tok), F32),
            jax.ShapeDtypeStruct((chunks, few, tok), F32),
        ],
        compiler_params=pltpu.CompilerParams(vmem_limit_bytes=VMEM_LIMIT),
        cost_estimate=pl.CostEstimate(
            flops=2 * tok * lanes * N_STATE * 4, bytes_accessed=6 << 20, transcendentals=1 << 16
        ),
        name="ssm_states",
    )(
        scalars, x_in, b_in, dt_raw.T, dt_bias[None, :], a_log[None, :], d_skip[None, :], ssm_init
    )


def hop(place, received, states, rows, step):
    chunks, unused, width = states.shape
    if received.shape[1] < width:
        received = jnp.pad(received, ((0, 0), (0, width - received.shape[1])))
    chunk = jnp.clip(step - 1 - place, 0, chunks - 1)
    state = lax.dynamic_index_in_dim(states, chunk, 0, keepdims=False)
    decay = lax.dynamic_index_in_dim(rows, chunk, 0, keepdims=False)[0:1, :]
    combined = (decay * received.astype(F32) + state).astype(BF16)
    return jnp.where(step <= place, received, combined)


def ssm_inner_kernel(scalars, x_ref, b_ref, c_ref, logt_ref, dtt_ref, rows_ref, out_ref):
    tok, width = x_ref.shape
    heads = width // MP
    row = lax.broadcasted_iota(jnp.int32, (BLOCK, BLOCK), 0)
    col = lax.broadcasted_iota(jnp.int32, (BLOCK, BLOCK), 1)
    lower = row >= col
    low_half = col < MP
    table = head_table(heads, width)
    logt = logt_ref[0]
    dtt = dtt_ref[0]
    logs = logt.T
    skip = rows_ref[0, 1:2, :]
    state = None
    pairs = heads // 2
    group = group_lanes(scalars, pl.program_id(0) * heads)
    for blk in range(tok // BLOCK):
        part = slice(blk * BLOCK, (blk + 1) * BLOCK)
        c_blk = c_ref[part, group]
        b_blk = b_ref[part, group]
        x_blk = x_ref[part, :]
        products = mm_nt(c_blk, b_blk)
        log_blk = logs[part]
        kernels = []
        for h in range(heads):
            spread = log_blk[:, h : h + 1] - logt[h : h + 1, part]
            decay = jnp.exp(jnp.where(lower, spread, NEG))
            kernels.append((decay * products * dtt[h : h + 1, part]).astype(BF16))
        carried = None
        if state is not None:
            carried = expand(jnp.exp(logt[:, part]), table) * mm(c_blk, state.astype(BF16))
        if (blk + 1) * BLOCK < tok:
            end = logt[:, (blk + 1) * BLOCK - 1 : (blk + 1) * BLOCK]
            tail = jnp.exp(end - logt[:, part]) * dtt[:, part]
            weighted = (expand(tail, table) * x_blk.astype(F32)).astype(BF16)
            update = mm(b_blk.T, weighted)
            if state is None:
                state = update
            else:
                factor = expand(jnp.broadcast_to(jnp.exp(end), (heads, 8)), table)[0:1]
                state = factor * state + update
        for pair in range(pairs):
            lanes = slice(pair * 128, (pair + 1) * 128)
            x_pair = x_blk[:, lanes]
            zero = jnp.zeros_like(x_pair)
            stacked = jnp.concatenate(
                [jnp.where(low_half, x_pair, zero), jnp.where(low_half, zero, x_pair)], axis=0
            )
            inner = mm(jnp.concatenate(kernels[2 * pair : 2 * pair + 2], axis=1), stacked)
            value = inner + skip[:, lanes] * x_pair.astype(F32)
            if carried is not None:
                value = value + carried[:, lanes]
            out_ref[part, lanes] = value


def ssm_inner(scalars, x_in, b_in, c_in, logt, dtt, rows, width):
    tok, lanes = x_in.shape
    chunks = lanes // width
    heads = width // MP
    per_chunk = pl.BlockSpec((tok, width), lambda c: (0, c))
    grouped = pl.BlockSpec(b_in.shape, lambda c: (0, 0))
    major = lambda c: (c, 0, 0)
    return pl.pallas_call(
        ssm_inner_kernel,
        grid_spec=pl.GridSpec(
            grid=(chunks,),
            in_specs=[
                SCALARS,
                per_chunk,
                grouped,
                grouped,
                pl.BlockSpec((1, heads, tok), major),
                pl.BlockSpec((1, heads, tok), major),
                pl.BlockSpec((1, 8, width), major),
            ],
            out_specs=per_chunk,
        ),
        out_shape=jax.ShapeDtypeStruct((tok, lanes), F32),
        compiler_params=pltpu.CompilerParams(vmem_limit_bytes=VMEM_LIMIT),
        cost_estimate=pl.CostEstimate(
            flops=2 * tok * lanes * N_STATE * 8, bytes_accessed=6 << 20, transcendentals=1 << 21
        ),
        name="ssm_inner",
    )(scalars, x_in, b_in, c_in, logt, dtt, rows)


def ssm_outputs_kernel(
    scalars, inner_ref, z_ref, c_ref, logt_ref, norm_ref, init_hbm, *rest, hops, chunk, alias,
):
    received = rest[:hops]
    out_ref, carry, init_buf, sem = rest[hops + alias :]
    place = scalars[0]
    tok, width = inner_ref.shape
    heads = width // MP

    for r in range(hops):
        @pl.when(place == r + 1)
        def _():
            pltpu.make_async_copy(received[r], carry, sem).start()

    initial = pltpu.make_async_copy(
        init_hbm.at[chunk * heads : (chunk + 1) * heads], init_buf, sem
    )

    @pl.when(place == 0)
    def _():
        initial.start()

    row = lax.broadcasted_iota(jnp.int32, (BLOCK, BLOCK), 0)
    col = lax.broadcasted_iota(jnp.int32, (BLOCK, BLOCK), 1)
    mean_table = jnp.where(row // MP == col // MP, 1.0 / MP, 0.0).astype(BF16)
    mean_table = jnp.concatenate([mean_table, mean_table], axis=0)
    table = head_table(heads, width)
    logt = logt_ref[0]
    whole_logs = []
    before = jnp.zeros((heads, 1), F32)
    for blk in range(tok // BLOCK):
        part = slice(blk * BLOCK, (blk + 1) * BLOCK)
        whole_logs.append(jnp.exp(logt[:, part] + before))
        before = before + logt[:, (blk + 1) * BLOCK - 1 : (blk + 1) * BLOCK]
    spread = expand(jnp.concatenate(whole_logs, axis=1), table)
    z = z_ref[...].astype(F32)
    gate = z / (1.0 + jnp.exp(-z))

    @pl.when(place > 0)
    def _():
        pltpu.make_async_copy(received[0], carry, sem).wait()

    @pl.when(place == 0)
    def _():
        initial.wait()
        carry[...] = init_buf[...].reshape(width, N_STATE).astype(BF16).T

    gated = (inner_ref[...] + spread * mm(c_ref[:, group_lanes(scalars, chunk * heads)], carry[...])) * gate
    square = gated * gated
    high = square.astype(BF16)
    low = (square - high.astype(F32)).astype(BF16)
    for at in range(0, width, 128):
        lanes = slice(at, at + 128)
        mean = mm(jnp.concatenate([high[:, lanes], low[:, lanes]], axis=1), mean_table)
        normed = gated[:, lanes] * lax.rsqrt(mean + 1e-05) * norm_ref[:, lanes]
        out_ref[:, lanes] = normed.astype(BF16)


def ssm_outputs(scalars, inner, z_gate, c_in, logt, norm_weight, ssm_init, received, width, chunk,
                into):
    tok, lanes = inner.shape
    heads = width // MP
    anywhere = pl.BlockSpec(memory_space=pl.ANY)
    per_chunk = pl.BlockSpec((tok, width), lambda k: (0, chunk))
    operands = [scalars, inner, z_gate, c_in, logt, norm_weight[None, :], ssm_init, *received]
    in_specs = [
        SCALARS,
        per_chunk,
        per_chunk,
        pl.BlockSpec(c_in.shape, lambda k: (0, 0)),
        pl.BlockSpec((1, heads, tok), lambda k: (chunk, 0, 0)),
        pl.BlockSpec((1, width), lambda k: (0, chunk)),
    ] + [anywhere] * (1 + len(received))
    aliases = {}
    if into is not None:
        aliases = {len(operands): 0}
        operands.append(into)
        in_specs.append(anywhere)
    return pl.pallas_call(
        functools.partial(
            ssm_outputs_kernel, hops=len(received), chunk=chunk, alias=len(aliases)
        ),
        grid_spec=pl.GridSpec(
            grid=(1,),
            in_specs=in_specs,
            out_specs=per_chunk,
            scratch_shapes=[
                pltpu.VMEM((N_STATE, width), BF16),
                pltpu.VMEM((heads, MP, N_STATE), F32),
                pltpu.SemaphoreType.DMA,
            ],
        ),
        out_shape=jax.ShapeDtypeStruct((tok, lanes), BF16),
        input_output_aliases=aliases,
        compiler_params=pltpu.CompilerParams(vmem_limit_bytes=VMEM_LIMIT),
        cost_estimate=pl.CostEstimate(
            flops=2 * tok * width * N_STATE * 2, bytes_accessed=2 << 20, transcendentals=1 << 18
        ),
        name="ssm_outputs",
    )(*operands)


def attend_kernel(scalars, q_ref, *rest, kv_head, kv_count, heads, hops, slots, use_cache,
                  use_window, carry_in, final, alias):
    rest = list(rest)
    take = lambda count: [rest.pop(0) for _ in range(count)]
    keys_near, keys_far, values_near, values_far = take(4) if use_cache else [None] * 4
    window = take(hops + 1) if use_window else []
    acc_in, state_in = take(2) if carry_in else (None, None)
    take(alias)
    outs = take(1 if final else 2)
    k_buf, v_buf, s_buf, best_buf, total_buf, acc_buf, sems, window_sems = rest
    place, dp, first_block, cache_blocks, newest, held = (scalars[k] for k in range(6))
    column = scalars[6]
    tok = q_ref.shape[0]
    half = slots // 2
    cache_total = slots // KEY_BLOCK
    base = slots if use_cache else 0
    lanes = pl.ds(pl.multiple_of((column + kv_head) * HD, HD), HD)
    lane = lax.broadcasted_iota(jnp.int32, (1, KEY_BLOCK), 1)

    def block_of(j):
        return lax.rem(first_block + j, cache_total)

    def block_copy(which, source, block):
        rows = pl.ds(pl.multiple_of(lax.rem(block * KEY_BLOCK, half), KEY_BLOCK), KEY_BLOCK)
        into = pl.ds(pl.multiple_of(block * KEY_BLOCK, KEY_BLOCK), KEY_BLOCK)
        buf = (k_buf, v_buf)[which]
        return pltpu.make_async_copy(source.at[rows, lanes], buf.at[into], sems.at[which, block])

    for which, near, far in ((0, keys_near, keys_far), (1, values_near, values_far)):
        def start(j, unused, which=which, near=near, far=far):
            block = block_of(j)
            mine = block // (half // KEY_BLOCK) == dp

            @pl.when(mine)
            def _():
                block_copy(which, near, block).start()

            @pl.when(jnp.logical_not(mine))
            def _():
                block_copy(which, far, block).start()

            return 0

        if use_cache:
            lax.fori_loop(0, cache_blocks, start, 0)

    window_copies = []
    for which, buf, at in ((0, k_buf, kv_head), (1, v_buf, kv_count + kv_head)):
        for k, ref in enumerate(window):
            window_copies.append(
                pltpu.make_async_copy(
                    ref.at[:, at * HD : (at + 1) * HD],
                    buf.at[base + k * tok : base + (k + 1) * tok],
                    window_sems.at[which, k],
                )
            )
    for copy in window_copies:
        copy.start()
    depth = k_buf.shape[0]
    loose = base + (hops + 1) * tok
    if use_window and depth > loose:
        for buf in (k_buf, v_buf):
            buf[loose:depth, :] = jnp.zeros((depth - loose, HD), BF16)

    def score(offsets, biases):
        for h in range(heads):
            rows = slice(h * tok, (h + 1) * tok)
            best = best_buf[rows, :]
            for offset, bias in zip(offsets, biases):
                span = pl.ds(offset, KEY_BLOCK)
                scores = mm_nt(q_ref[:, h * HD : (h + 1) * HD], k_buf[span, :])
                scores = scores * LOG2_SCALE + bias
                s_buf[rows, span] = scores
                best = jnp.maximum(best, fold_lanes(scores, jnp.maximum))
            best_buf[rows, :] = best

    def mix(offsets):
        for h in range(heads):
            rows = slice(h * tok, (h + 1) * tok)
            best = best_buf[rows, :]
            total = total_buf[rows, :]
            acc = acc_buf[rows, :]
            for offset in offsets:
                probs = jnp.concatenate(
                    [
                        jnp.exp2(s_buf[rows, pl.ds(offset + k, 128)] - best)
                        for k in range(0, KEY_BLOCK, 128)
                    ],
                    axis=1,
                )
                total = total + fold_lanes(probs, jnp.add)
                acc = acc + mm(probs.astype(BF16), v_buf[pl.ds(offset, KEY_BLOCK), :])
            total_buf[rows, :] = total
            acc_buf[rows, :] = acc

    def sweep(visit):
        if not use_cache:
            return
        done = 0
        for size in GROUPS:
            if size > cache_total:
                continue
            count = (cache_blocks - done) // size

            def some(j, unused, size=size, done=done):
                visit([block_of(done + j * size + k) for k in range(size)])
                return 0

            lax.fori_loop(0, count, some, 0)
            done = done + count * size

    def place_of(block):
        return pl.multiple_of(block * KEY_BLOCK, KEY_BLOCK)

    def cache_score(blocks):
        offsets, biases = [], []
        for block in blocks:
            block_copy(0, keys_near, block).wait()
            offset = place_of(block)
            age = newest - (offset + lane)
            age = jnp.where(age < 0, age + slots, age)
            offsets.append(offset)
            biases.append(jnp.where(age < held, 0.0, NEG))
        score(offsets, biases)

    def cache_mix(blocks):
        for block in blocks:
            block_copy(1, values_near, block).wait()
        mix([place_of(block) for block in blocks])

    double = 2 * KEY_BLOCK
    window_pairs = (place * tok + tok + double - 1) // double

    def window_bias(at):
        if isinstance(at, int) and at * KEY_BLOCK < tok:
            later = (
                lax.broadcasted_iota(jnp.int32, (tok, KEY_BLOCK), 0)
                - lax.broadcasted_iota(jnp.int32, (tok, KEY_BLOCK), 1)
            )
            allowed = (later >= 0) | ((lane >= tok) & (lane < tok * (place + 1)))
        else:
            allowed = lane + at * KEY_BLOCK < tok * (place + 1)
        return jnp.where(allowed, 0.0, NEG)

    def window_offsets(j):
        return [pl.multiple_of(base + (2 * j + k) * KEY_BLOCK, KEY_BLOCK) for k in range(2)]

    if carry_in:
        best_buf[...] = jnp.broadcast_to(state_in[:, 0:1], best_buf.shape)
    else:
        best_buf[...] = jnp.full_like(best_buf, NEG)
    sweep(cache_score)
    if use_window:
        for copy in window_copies[: hops + 1]:
            copy.wait()
        score([base, base + KEY_BLOCK], [window_bias(0), window_bias(1)])

        def more_scores(j, unused):
            score(window_offsets(j), [window_bias(2 * j), window_bias(2 * j + 1)])
            return 0

        if depth > base + double:
            lax.fori_loop(1, window_pairs, more_scores, 0)
    best_buf[...] = jnp.broadcast_to(
        jnp.max(best_buf[...], axis=-1, keepdims=True), best_buf.shape
    )
    if carry_in:
        factor = jnp.exp2(jnp.broadcast_to(state_in[:, 0:1], best_buf.shape) - best_buf[...])
        first = lax.broadcasted_iota(jnp.int32, (1, 128), 1) == 127
        acc_buf[...] = factor * acc_in[...]
        total_buf[...] = jnp.where(first, factor * state_in[...], 0.0)
    else:
        acc_buf[...] = jnp.zeros_like(acc_buf)
        total_buf[...] = jnp.zeros_like(total_buf)
    sweep(cache_mix)
    if use_window:
        for copy in window_copies[hops + 1 :]:
            copy.wait()
        mix([base, base + KEY_BLOCK])

        def more_mix(j, unused):
            mix(window_offsets(j))
            return 0

        if depth > base + double:
            lax.fori_loop(1, window_pairs, more_mix, 0)
    for h in range(heads):
        rows = slice(h * tok, (h + 1) * tok)
        total = jnp.sum(total_buf[rows, :], axis=-1, keepdims=True)
        if final:
            outs[0][:, h * HD : (h + 1) * HD] = (acc_buf[rows, :] / total).astype(BF16)
        else:
            outs[0][rows, :] = acc_buf[rows, :]
            last = lax.broadcasted_iota(jnp.int32, (1, 128), 1) == 127
            outs[1][rows, :] = jnp.where(last, total, best_buf[rows, :])


def attend(scalars, queries, head, heads, kv_count, slots, cache=None, window=None, carry=None,
           into=None, final=True):
    tok = queries.shape[0]
    kv_head = head // (AH // KVH)
    hops = len(window) - 1 if window is not None else 0
    rows = heads * tok
    depth = slots if cache is not None else 0
    if window is not None:
        depth += -(-((hops + 1) * tok) // (2 * KEY_BLOCK)) * (2 * KEY_BLOCK)
    anywhere = pl.BlockSpec(memory_space=pl.ANY)
    part = pl.BlockSpec((tok, heads * HD), lambda k: (0, head // heads))
    whole = pl.BlockSpec((rows, 128), lambda k: (0, 0))
    operands, in_specs = [scalars, queries], [SCALARS, part]
    for group in (cache, window):
        if group is not None:
            operands += list(group)
            in_specs += [anywhere] * len(group)
    if carry is not None:
        operands += list(carry)
        in_specs += [whole] * 2
    aliases = {}
    if into is not None:
        aliases = {len(operands): 0}
        operands.append(into)
        in_specs.append(anywhere)
    if final:
        out_specs, out_shape = part, jax.ShapeDtypeStruct(queries.shape, BF16)
    else:
        out_specs, out_shape = [whole] * 2, [jax.ShapeDtypeStruct((rows, 128), F32)] * 2
    return pl.pallas_call(
        functools.partial(
            attend_kernel, kv_head=kv_head, kv_count=kv_count, heads=heads, hops=hops,
            slots=slots, use_cache=cache is not None, use_window=window is not None,
            carry_in=carry is not None, final=final, alias=len(aliases),
        ),
        grid_spec=pl.GridSpec(
            grid=(1,),
            in_specs=in_specs,
            out_specs=out_specs,
            scratch_shapes=[
                pltpu.VMEM((depth, HD), BF16),
                pltpu.VMEM((depth, HD), BF16),
                pltpu.VMEM((rows, depth), F32),
                pltpu.VMEM((rows, 128), F32),
                pltpu.VMEM((rows, 128), F32),
                pltpu.VMEM((rows, 128), F32),
                pltpu.SemaphoreType.DMA((2, slots // KEY_BLOCK)),
                pltpu.SemaphoreType.DMA((2, hops + 1)),
            ],
        ),
        out_shape=out_shape,
        input_output_aliases=aliases,
        compiler_params=pltpu.CompilerParams(vmem_limit_bytes=VMEM_LIMIT),
        cost_estimate=pl.CostEstimate(
            flops=16 * rows * depth * HD, bytes_accessed=4 * depth * HD,
            transcendentals=rows * depth,
        ),
        name="attend",
    )(*operands)


def tie(*values):
    return lax.optimization_barrier(values)


def local(x_in, z_gate, b_in, c_in, dt_raw, dt_bias, a_log, d_skip, norm_weight, ssm_init, queries,
          keys, values, cache_keys, cache_values, window_start, prefix_len):
    tok, lanes = x_in.shape
    head_count = dt_raw.shape[1]
    per_group = MH // NG
    places = lax.axis_size("seq")
    place = lax.axis_index("seq")
    dp = lax.axis_index("dp")
    q_count = queries.shape[1] // HD
    kv_here = keys.shape[1] // HD
    kv_count = max(1, q_count * KVH // AH)
    width = min(lanes, STATE_WIDTH * kv_count * HD)
    chunks = lanes // width
    column = (dp * q_count) // (AH // KVH)
    slots = 2 * cache_keys.shape[0]

    ring = [(k, (k + 1) % places) for k in range(places)]
    swap = [(0, 1), (1, 0)]
    far_keys = lax.ppermute(cache_keys, "dp", swap)
    far_values = lax.ppermute(cache_values, "dp", swap)

    own_rows = jnp.concatenate(
        [
            lax.dynamic_slice_in_dim(array, column * HD, kv_count * HD, axis=1)
            for array in (keys, values)
        ],
        axis=1,
    )

    newest = jnp.mod(window_start[0] - 1, slots)
    held = prefix_len[0]
    oldest = jnp.mod(newest - held + 1, slots)
    first_block = oldest // KEY_BLOCK
    cache_blocks = jnp.minimum(
        slots // KEY_BLOCK, (oldest % KEY_BLOCK + held + KEY_BLOCK - 1) // KEY_BLOCK
    )
    first_head = dp * head_count
    scalars = jnp.stack(
        [place, dp, first_block, cache_blocks, newest, held, column, first_head]
    ).astype(jnp.int32)

    received = []
    send = own_rows
    arrived = lax.ppermute(send, "seq", ring)
    x_tied, send = tie(x_in, send)
    span = max(width, min(lanes, per_group * MP))
    states, rows, logt, dtt = ssm_states(
        scalars, x_tied, b_in, dt_raw, dt_bias, a_log, d_skip, ssm_init, width, span
    )
    received.append(arrived)

    cache = (cache_keys, far_keys, cache_values, far_values)
    heads = min(HEADS_IN_CALL, q_count)
    parts = list(range(0, q_count, heads))
    last_step = places - 1 + chunks - 1
    result = inner = opened = mamba_out = None
    outputs_done = 0

    def outputs(chunk, into):
        return ssm_outputs(
            scalars, inner, z_gate, c_in, logt, norm_weight, ssm_init,
            received[chunk + 1 : chunk + places], width, chunk, into,
        )

    slots_here = slots

    def attend_next(queries_now, into):
        window = [own_rows] + received[: places - 1]
        head, carry = parts.pop(0)
        return attend(
            scalars, queries_now, head, heads, kv_count, slots_here,
            cache=None if carry else cache, window=window, carry=carry, into=into,
        )

    parts = [(head, None) for head in parts]
    for step in range(1, last_step + 1):
        incoming = received[-1]
        if step == 1:
            incoming, states = tie(incoming, states)
        elif result is not None:
            incoming, result = tie(incoming, result)
        elif opened is not None:
            incoming, *opened = tie(incoming, *opened)
        else:
            incoming, inner = tie(incoming, inner)
        send = hop(place, incoming, states, rows, step)
        senders = range(max(0, step - chunks), places - 1)
        pairs = ring if len(senders) == places - 1 else [(k, k + 1) for k in senders]
        arrived = lax.ppermute(send, "seq", pairs)
        if step == 1:
            x_tied, send = tie(x_in, send)
            inner = ssm_inner(scalars, x_tied, b_in, c_in, logt, dtt, rows, width)
        elif step == OPEN_STEP and len(parts) > 1:
            queries_now, send = tie(queries, send)
            head = parts.pop(0)[0]
            opened = attend(
                scalars, queries_now, head, heads, kv_count, slots_here, cache=cache, final=False
            )
            parts.append((head, opened))
        elif step >= places - 1 and parts:
            queries_now, send = tie(queries, send)
            if opened is not None and parts[0][1] is not None:
                parts[0] = (parts[0][0], opened)
            result = attend_next(queries_now, result)
            if step == last_step and chunks > 1:
                logt, send = tie(logt, send)
                mamba_out = outputs(0, mamba_out)
                outputs_done = 1
        received.append(arrived)
    while parts:
        result = attend_next(queries, result)
    for chunk in range(outputs_done, chunks):
        mamba_out = outputs(chunk, mamba_out)
    return (mamba_out, result)


def solution(mesh):
    rows = P(("groups", "seq"), ("tp", "dp"))
    shared = P(("groups", "seq"), "tp")
    heads = P(("tp", "dp"))
    cached = P(("groups", "dp"), "tp")
    return jax.shard_map(
        local,
        mesh=mesh,
        in_specs=(
            rows, rows, shared, shared, rows, heads, heads, heads, heads,
            P(("groups", "tp", "dp"), None, None), rows, shared, shared, cached, cached,
            P("groups"), P("groups"),
        ),
        out_specs=(rows, rows),
        check_vma=False,
    )
```

```python
import functools
import math

import jax
import jax.numpy as jnp
from jax import lax
from jax.experimental import pallas as pl
from jax.experimental.pallas import tpu as pltpu
from jax.sharding import PartitionSpec as P

MH = 128
MP = 64
N_STATE = 256
NG = 8
AH = 64
KVH = 8
HD = 128
BLOCK = 128
KEY_BLOCK = 512
GROUPS = (4, 2, 1)
STATE_WIDTH = 4
HEADS_IN_CALL = 8
OPEN_STEP = 2
LOG2_SCALE = math.log2(math.e) / math.sqrt(HD)
NEG = -1e30
F32 = jnp.float32
BF16 = jnp.bfloat16
VMEM_LIMIT = 56 << 20


SCALARS = pl.BlockSpec(memory_space=pltpu.SMEM)


def group_lanes(scalars, head):
    group = (scalars[7] + head) // (MH // NG)
    return pl.ds(pl.multiple_of(group * N_STATE, N_STATE), N_STATE)


def mm(a, b):
    return jnp.dot(a, b, preferred_element_type=F32)


def mm_nt(a, b):
    return lax.dot_general(a, b, (((1,), (1,)), ((), ())), preferred_element_type=F32)


def pieces_of(value):
    first = value.astype(BF16)
    rest = value - first.astype(F32)
    second = rest.astype(BF16)
    third = (rest - second.astype(F32)).astype(BF16)
    return first, second, third


def head_table(heads, width):
    row = lax.broadcasted_iota(jnp.int32, (heads, width), 0)
    lane = lax.broadcasted_iota(jnp.int32, (heads, width), 1)
    table = jnp.where(lane // MP == row, 1.0, 0.0).astype(BF16)
    return jnp.concatenate([table] * 3, axis=0)


def expand(value, table):
    stacked = jnp.concatenate(pieces_of(value), axis=0)
    return lax.dot_general(stacked, table, (((0,), (0,)), ((), ())), preferred_element_type=F32)


def fold_lanes(value, op):
    parts = [value[:, k : k + 128] for k in range(0, value.shape[1], 128)]
    while len(parts) > 1:
        parts = [
            op(parts[k], parts[k + 1]) if k + 1 < len(parts) else parts[k]
            for k in range(0, len(parts), 2)
        ]
    return parts[0]


def ssm_states_kernel(
    scalars, x_ref, b_ref, dt_ref, bias_ref, alog_ref, dskip_ref, init_ref,
    state_ref, rows_ref, logt_ref, dtt_ref, first_ref, dt_all, log_all, skip_all,
):
    span = pl.program_id(0)
    tok, lanes = x_ref.shape
    heads = lanes // MP
    spans = dt_ref.shape[0] // heads
    parts = state_ref.shape[0]
    width = lanes // parts
    group = group_lanes(scalars, span * heads)

    @pl.when(span == 0)
    def _():
        column = lambda ref: jnp.broadcast_to(ref[...], (8, ref.shape[1])).T[:, 0:1]
        dt = jax.nn.softplus(dt_ref[...] + column(bias_ref))
        decay = -jnp.exp(column(alog_ref)) * dt
        row = lax.broadcasted_iota(jnp.int32, (BLOCK, BLOCK), 0)
        col = lax.broadcasted_iota(jnp.int32, (BLOCK, BLOCK), 1)
        upper = jnp.where(row <= col, 1.0, 0.0).astype(BF16)
        logs = []
        for blk in range(tok // BLOCK):
            first, second, third = pieces_of(decay[:, blk * BLOCK : (blk + 1) * BLOCK])
            logs.append(mm(first, upper) + mm(second, upper) + mm(third, upper))
        logs = jnp.concatenate(logs, axis=1)
        skip = jnp.broadcast_to(column(dskip_ref), (dt_ref.shape[0], 128))
        for k in range(spans):
            dt_all[k] = dt[k * heads : (k + 1) * heads]
            log_all[k] = logs[k * heads : (k + 1) * heads]
            skip_all[k] = skip[k * heads : (k + 1) * heads]

    dt = dt_all[span]
    logs = log_all[span]
    few = heads // parts
    for k in range(parts):
        logt_ref[k] = logs[k * few : (k + 1) * few]
        dtt_ref[k] = dt[k * few : (k + 1) * few]
    table = head_table(heads, lanes)
    state = None
    total = jnp.zeros((heads, 1), F32)
    for blk in range(tok // BLOCK):
        part = slice(blk * BLOCK, (blk + 1) * BLOCK)
        end = logs[:, (blk + 1) * BLOCK - 1 : (blk + 1) * BLOCK]
        tail = jnp.exp(end - logs[:, part]) * dt[:, part]
        weighted = (expand(tail, table) * x_ref[part, :].astype(F32)).astype(BF16)
        update = mm(b_ref[part, group].T, weighted)
        if state is None:
            state = update
        else:
            state = expand(jnp.broadcast_to(jnp.exp(end), (heads, 8)), table)[0:1] * state + update
        total = total + end
    place = scalars[0]
    lane = lax.broadcasted_iota(jnp.int32, (heads, 8), 1)
    rows = expand(jnp.where(lane == 0, jnp.exp(total), skip_all[span][:, 0:8]), table)
    for k in range(parts):
        state_ref[k] = state[:, k * width : (k + 1) * width]
        rows_ref[k] = rows[:, k * width : (k + 1) * width]

    @pl.when(place == 0)
    def _():
        for k in range(parts):
            first = init_ref[k * few : (k + 1) * few].reshape(width, N_STATE).T
            state_ref[k] = state_ref[k] + rows_ref[k, 0:1, :] * first
            rows_ref[k, 0:1, :] = jnp.zeros((1, width), F32)

    @pl.when(span == 0)
    def _():
        first_ref[...] = state_ref[0].astype(BF16)


def ssm_states(scalars, x_in, b_in, dt_raw, dt_bias, a_log, d_skip, ssm_init, width, span):
    tok, lanes = x_in.shape
    chunks = lanes // width
    head_count = dt_raw.shape[1]
    heads = span // MP
    few = width // MP
    parts = span // width
    flat = lambda c: (0, 0)
    major = lambda c: (c, 0, 0)
    return pl.pallas_call(
        ssm_states_kernel,
        grid_spec=pl.GridSpec(
            grid=(lanes // span,),
            in_specs=[
                SCALARS,
                pl.BlockSpec((tok, span), lambda c: (0, c)),
                pl.BlockSpec(b_in.shape, flat),
                pl.BlockSpec((head_count, tok), flat),
                pl.BlockSpec((1, head_count), flat),
                pl.BlockSpec((1, head_count), flat),
                pl.BlockSpec((1, head_count), flat),
                pl.BlockSpec((heads, MP, N_STATE), major),
            ],
            out_specs=[
                pl.BlockSpec((parts, N_STATE, width), major),
                pl.BlockSpec((parts, 8, width), major),
                pl.BlockSpec((parts, few, tok), major),
                pl.BlockSpec((parts, few, tok), major),
                pl.BlockSpec((N_STATE, width), flat),
            ],
            scratch_shapes=[
                pltpu.VMEM((lanes // span, heads, tok), F32),
                pltpu.VMEM((lanes // span, heads, tok), F32),
                pltpu.VMEM((lanes // span, heads, 128), F32),
            ],
        ),
        out_shape=[
            jax.ShapeDtypeStruct((chunks, N_STATE, width), F32),
            jax.ShapeDtypeStruct((chunks, 8, width), F32),
            jax.ShapeDtypeStruct((chunks, few, tok), F32),
            jax.ShapeDtypeStruct((chunks, few, tok), F32),
            jax.ShapeDtypeStruct((N_STATE, width), BF16),
        ],
        compiler_params=pltpu.CompilerParams(vmem_limit_bytes=VMEM_LIMIT),
        cost_estimate=pl.CostEstimate(
            flops=2 * tok * lanes * N_STATE * 4, bytes_accessed=6 << 20, transcendentals=1 << 16
        ),
        name="ssm_states",
    )(
        scalars, x_in, b_in, dt_raw.T, dt_bias[None, :], a_log[None, :], d_skip[None, :], ssm_init
    )


def hop(place, received, states, rows, step):
    chunks = states.shape[0]
    chunk = jnp.clip(step - 1 - place, 0, chunks - 1)
    state = lax.dynamic_index_in_dim(states, chunk, 0, keepdims=False)
    decay = lax.dynamic_index_in_dim(rows, chunk, 0, keepdims=False)[0:1, :]
    combined = (decay * received.astype(F32) + state).astype(BF16)
    return jnp.where(step <= place, received, combined)


def ssm_inner_kernel(scalars, x_ref, b_ref, c_ref, logt_ref, dtt_ref, rows_ref, out_ref):
    tok, width = x_ref.shape
    heads = width // MP
    row = lax.broadcasted_iota(jnp.int32, (BLOCK, BLOCK), 0)
    col = lax.broadcasted_iota(jnp.int32, (BLOCK, BLOCK), 1)
    lower = row >= col
    low_half = col < MP
    table = head_table(heads, width)
    logt = logt_ref[0]
    dtt = dtt_ref[0]
    logs = logt.T
    skip = rows_ref[0, 1:2, :]
    state = None
    pairs = heads // 2
    group = group_lanes(scalars, pl.program_id(0) * heads)
    for blk in range(tok // BLOCK):
        part = slice(blk * BLOCK, (blk + 1) * BLOCK)
        c_blk = c_ref[part, group]
        b_blk = b_ref[part, group]
        x_blk = x_ref[part, :]
        products = mm_nt(c_blk, b_blk)
        log_blk = logs[part]
        kernels = []
        for h in range(heads):
            spread = log_blk[:, h : h + 1] - logt[h : h + 1, part]
            decay = jnp.exp(jnp.where(lower, spread, NEG))
            kernels.append((decay * products * dtt[h : h + 1, part]).astype(BF16))
        carried = None
        if state is not None:
            carried = expand(jnp.exp(logt[:, part]), table) * mm(c_blk, state.astype(BF16))
        if (blk + 1) * BLOCK < tok:
            end = logt[:, (blk + 1) * BLOCK - 1 : (blk + 1) * BLOCK]
            tail = jnp.exp(end - logt[:, part]) * dtt[:, part]
            weighted = (expand(tail, table) * x_blk.astype(F32)).astype(BF16)
            update = mm(b_blk.T, weighted)
            if state is None:
                state = update
            else:
                factor = expand(jnp.broadcast_to(jnp.exp(end), (heads, 8)), table)[0:1]
                state = factor * state + update
        for pair in range(pairs):
            lanes = slice(pair * 128, (pair + 1) * 128)
            x_pair = x_blk[:, lanes]
            zero = jnp.zeros_like(x_pair)
            stacked = jnp.concatenate(
                [jnp.where(low_half, x_pair, zero), jnp.where(low_half, zero, x_pair)], axis=0
            )
            inner = mm(jnp.concatenate(kernels[2 * pair : 2 * pair + 2], axis=1), stacked)
            value = inner + skip[:, lanes] * x_pair.astype(F32)
            if carried is not None:
                value = value + carried[:, lanes]
            out_ref[part, lanes] = value


def ssm_inner(scalars, x_in, b_in, c_in, logt, dtt, rows, width):
    tok, lanes = x_in.shape
    chunks = lanes // width
    heads = width // MP
    per_chunk = pl.BlockSpec((tok, width), lambda c: (0, c))
    grouped = pl.BlockSpec(b_in.shape, lambda c: (0, 0))
    major = lambda c: (c, 0, 0)
    return pl.pallas_call(
        ssm_inner_kernel,
        grid_spec=pl.GridSpec(
            grid=(chunks,),
            in_specs=[
                SCALARS,
                per_chunk,
                grouped,
                grouped,
                pl.BlockSpec((1, heads, tok), major),
                pl.BlockSpec((1, heads, tok), major),
                pl.BlockSpec((1, 8, width), major),
            ],
            out_specs=per_chunk,
        ),
        out_shape=jax.ShapeDtypeStruct((tok, lanes), F32),
        compiler_params=pltpu.CompilerParams(vmem_limit_bytes=VMEM_LIMIT),
        cost_estimate=pl.CostEstimate(
            flops=2 * tok * lanes * N_STATE * 8, bytes_accessed=6 << 20, transcendentals=1 << 21
        ),
        name="ssm_inner",
    )(scalars, x_in, b_in, c_in, logt, dtt, rows)


def ssm_outputs_kernel(
    scalars, inner_ref, z_ref, c_ref, logt_ref, norm_ref, init_hbm, *rest, hops, chunk, alias,
):
    received = rest[:hops]
    out_ref, carry, init_buf, sem = rest[hops + alias :]
    place = scalars[0]
    tok, width = inner_ref.shape
    heads = width // MP

    for r in range(hops):
        @pl.when(place == r + 1)
        def _():
            pltpu.make_async_copy(received[r], carry, sem).start()

    initial = pltpu.make_async_copy(
        init_hbm.at[chunk * heads : (chunk + 1) * heads], init_buf, sem
    )

    @pl.when(place == 0)
    def _():
        initial.start()

    row = lax.broadcasted_iota(jnp.int32, (BLOCK, BLOCK), 0)
    col = lax.broadcasted_iota(jnp.int32, (BLOCK, BLOCK), 1)
    mean_table = jnp.where(row // MP == col // MP, 1.0 / MP, 0.0).astype(BF16)
    mean_table = jnp.concatenate([mean_table, mean_table], axis=0)
    table = head_table(heads, width)
    logt = logt_ref[0]
    whole_logs = []
    before = jnp.zeros((heads, 1), F32)
    for blk in range(tok // BLOCK):
        part = slice(blk * BLOCK, (blk + 1) * BLOCK)
        whole_logs.append(jnp.exp(logt[:, part] + before))
        before = before + logt[:, (blk + 1) * BLOCK - 1 : (blk + 1) * BLOCK]
    spread = expand(jnp.concatenate(whole_logs, axis=1), table)
    z = z_ref[...].astype(F32)
    gate = z / (1.0 + jnp.exp(-z))

    @pl.when(place > 0)
    def _():
        pltpu.make_async_copy(received[0], carry, sem).wait()

    @pl.when(place == 0)
    def _():
        initial.wait()
        carry[...] = init_buf[...].reshape(width, N_STATE).astype(BF16).T

    gated = (inner_ref[...] + spread * mm(c_ref[:, group_lanes(scalars, chunk * heads)], carry[...])) * gate
    square = gated * gated
    high = square.astype(BF16)
    low = (square - high.astype(F32)).astype(BF16)
    for at in range(0, width, 128):
        lanes = slice(at, at + 128)
        mean = mm(jnp.concatenate([high[:, lanes], low[:, lanes]], axis=1), mean_table)
        normed = gated[:, lanes] * lax.rsqrt(mean + 1e-05) * norm_ref[:, lanes]
        out_ref[:, lanes] = normed.astype(BF16)


def ssm_outputs(scalars, inner, z_gate, c_in, logt, norm_weight, ssm_init, received, width, chunk,
                into):
    tok, lanes = inner.shape
    heads = width // MP
    anywhere = pl.BlockSpec(memory_space=pl.ANY)
    per_chunk = pl.BlockSpec((tok, width), lambda k: (0, chunk))
    operands = [scalars, inner, z_gate, c_in, logt, norm_weight[None, :], ssm_init, *received]
    in_specs = [
        SCALARS,
        per_chunk,
        per_chunk,
        pl.BlockSpec(c_in.shape, lambda k: (0, 0)),
        pl.BlockSpec((1, heads, tok), lambda k: (chunk, 0, 0)),
        pl.BlockSpec((1, width), lambda k: (0, chunk)),
    ] + [anywhere] * (1 + len(received))
    aliases = {}
    if into is not None:
        aliases = {len(operands): 0}
        operands.append(into)
        in_specs.append(anywhere)
    return pl.pallas_call(
        functools.partial(
            ssm_outputs_kernel, hops=len(received), chunk=chunk, alias=len(aliases)
        ),
        grid_spec=pl.GridSpec(
            grid=(1,),
            in_specs=in_specs,
            out_specs=per_chunk,
            scratch_shapes=[
                pltpu.VMEM((N_STATE, width), BF16),
                pltpu.VMEM((heads, MP, N_STATE), F32),
                pltpu.SemaphoreType.DMA,
            ],
        ),
        out_shape=jax.ShapeDtypeStruct((tok, lanes), BF16),
        input_output_aliases=aliases,
        compiler_params=pltpu.CompilerParams(vmem_limit_bytes=VMEM_LIMIT),
        cost_estimate=pl.CostEstimate(
            flops=2 * tok * width * N_STATE * 2, bytes_accessed=2 << 20, transcendentals=1 << 18
        ),
        name="ssm_outputs",
    )(*operands)


def attend_kernel(scalars, q_ref, *rest, kv_head, kv_count, heads, hops, slots, use_cache,
                  use_window, carry_in, final, alias):
    rest = list(rest)
    take = lambda count: [rest.pop(0) for _ in range(count)]
    keys_near, keys_far, values_near, values_far = take(4) if use_cache else [None] * 4
    window = take(hops + 1) if use_window else []
    acc_in, state_in = take(2) if carry_in else (None, None)
    take(alias)
    outs = take(1 if final else 2)
    k_buf, v_buf, s_buf, best_buf, total_buf, acc_buf, sems, window_sems = rest
    place, dp, first_block, cache_blocks, newest, held = (scalars[k] for k in range(6))
    column = scalars[6]
    tok = q_ref.shape[0]
    half = slots // 2
    cache_total = slots // KEY_BLOCK
    base = slots if use_cache else 0
    lanes = pl.ds(pl.multiple_of((column + kv_head) * HD, HD), HD)
    lane = lax.broadcasted_iota(jnp.int32, (1, KEY_BLOCK), 1)

    def block_of(j):
        return lax.rem(first_block + j, cache_total)

    def block_copy(which, source, block):
        rows = pl.ds(pl.multiple_of(lax.rem(block * KEY_BLOCK, half), KEY_BLOCK), KEY_BLOCK)
        into = pl.ds(pl.multiple_of(block * KEY_BLOCK, KEY_BLOCK), KEY_BLOCK)
        buf = (k_buf, v_buf)[which]
        return pltpu.make_async_copy(source.at[rows, lanes], buf.at[into], sems.at[which, block])

    for which, near, far in ((0, keys_near, keys_far), (1, values_near, values_far)):
        def start(j, unused, which=which, near=near, far=far):
            block = block_of(j)
            mine = block // (half // KEY_BLOCK) == dp

            @pl.when(mine)
            def _():
                block_copy(which, near, block).start()

            @pl.when(jnp.logical_not(mine))
            def _():
                block_copy(which, far, block).start()

            return 0

        if use_cache:
            lax.fori_loop(0, cache_blocks, start, 0)

    window_copies = []
    for which, buf, at in ((0, k_buf, kv_head), (1, v_buf, kv_count + kv_head)):
        for k, ref in enumerate(window):
            window_copies.append(
                pltpu.make_async_copy(
                    ref.at[:, at * HD : (at + 1) * HD],
                    buf.at[base + k * tok : base + (k + 1) * tok],
                    window_sems.at[which, k],
                )
            )
    for copy in window_copies:
        copy.start()
    depth = k_buf.shape[0]
    loose = base + (hops + 1) * tok
    if use_window and depth > loose:
        for buf in (k_buf, v_buf):
            buf[loose:depth, :] = jnp.zeros((depth - loose, HD), BF16)

    def score(offsets, biases):
        for h in range(heads):
            rows = slice(h * tok, (h + 1) * tok)
            best = best_buf[rows, :]
            for offset, bias in zip(offsets, biases):
                span = pl.ds(offset, KEY_BLOCK)
                scores = mm_nt(q_ref[:, h * HD : (h + 1) * HD], k_buf[span, :])
                scores = scores * LOG2_SCALE + bias
                s_buf[rows, span] = scores
                best = jnp.maximum(best, fold_lanes(scores, jnp.maximum))
            best_buf[rows, :] = best

    def mix(offsets):
        for h in range(heads):
            rows = slice(h * tok, (h + 1) * tok)
            best = best_buf[rows, :]
            total = total_buf[rows, :]
            acc = acc_buf[rows, :]
            for offset in offsets:
                probs = jnp.concatenate(
                    [
                        jnp.exp2(s_buf[rows, pl.ds(offset + k, 128)] - best)
                        for k in range(0, KEY_BLOCK, 128)
                    ],
                    axis=1,
                )
                total = total + fold_lanes(probs, jnp.add)
                acc = acc + mm(probs.astype(BF16), v_buf[pl.ds(offset, KEY_BLOCK), :])
            total_buf[rows, :] = total
            acc_buf[rows, :] = acc

    def sweep(visit):
        if not use_cache:
            return
        done = 0
        for size in GROUPS:
            if size > cache_total:
                continue
            count = (cache_blocks - done) // size

            def some(j, unused, size=size, done=done):
                visit([block_of(done + j * size + k) for k in range(size)])
                return 0

            lax.fori_loop(0, count, some, 0)
            done = done + count * size

    def place_of(block):
        return pl.multiple_of(block * KEY_BLOCK, KEY_BLOCK)

    def cache_score(blocks):
        offsets, biases = [], []
        for block in blocks:
            block_copy(0, keys_near, block).wait()
            offset = place_of(block)
            age = newest - (offset + lane)
            age = jnp.where(age < 0, age + slots, age)
            offsets.append(offset)
            biases.append(jnp.where(age < held, 0.0, NEG))
        score(offsets, biases)

    def cache_mix(blocks):
        for block in blocks:
            block_copy(1, values_near, block).wait()
        mix([place_of(block) for block in blocks])

    double = 2 * KEY_BLOCK
    window_pairs = (place * tok + tok + double - 1) // double

    def window_bias(at):
        if isinstance(at, int) and at * KEY_BLOCK < tok:
            later = (
                lax.broadcasted_iota(jnp.int32, (tok, KEY_BLOCK), 0)
                - lax.broadcasted_iota(jnp.int32, (tok, KEY_BLOCK), 1)
            )
            allowed = (later >= 0) | ((lane >= tok) & (lane < tok * (place + 1)))
        else:
            allowed = lane + at * KEY_BLOCK < tok * (place + 1)
        return jnp.where(allowed, 0.0, NEG)

    def window_offsets(j):
        return [pl.multiple_of(base + (2 * j + k) * KEY_BLOCK, KEY_BLOCK) for k in range(2)]

    if carry_in:
        best_buf[...] = jnp.broadcast_to(state_in[:, 0:1], best_buf.shape)
    else:
        best_buf[...] = jnp.full_like(best_buf, NEG)
    sweep(cache_score)
    if use_window:
        for copy in window_copies[: hops + 1]:
            copy.wait()
        score([base, base + KEY_BLOCK], [window_bias(0), window_bias(1)])

        def more_scores(j, unused):
            score(window_offsets(j), [window_bias(2 * j), window_bias(2 * j + 1)])
            return 0

        if depth > base + double:
            lax.fori_loop(1, window_pairs, more_scores, 0)
    best_buf[...] = jnp.broadcast_to(
        jnp.max(best_buf[...], axis=-1, keepdims=True), best_buf.shape
    )
    if carry_in:
        factor = jnp.exp2(jnp.broadcast_to(state_in[:, 0:1], best_buf.shape) - best_buf[...])
        first = lax.broadcasted_iota(jnp.int32, (1, 128), 1) == 127
        acc_buf[...] = factor * acc_in[...]
        total_buf[...] = jnp.where(first, factor * state_in[...], 0.0)
    else:
        acc_buf[...] = jnp.zeros_like(acc_buf)
        total_buf[...] = jnp.zeros_like(total_buf)
    sweep(cache_mix)
    if use_window:
        for copy in window_copies[hops + 1 :]:
            copy.wait()
        mix([base, base + KEY_BLOCK])

        def more_mix(j, unused):
            mix(window_offsets(j))
            return 0

        if depth > base + double:
            lax.fori_loop(1, window_pairs, more_mix, 0)
    for h in range(heads):
        rows = slice(h * tok, (h + 1) * tok)
        total = jnp.sum(total_buf[rows, :], axis=-1, keepdims=True)
        if final:
            outs[0][:, h * HD : (h + 1) * HD] = (acc_buf[rows, :] / total).astype(BF16)
        else:
            outs[0][rows, :] = acc_buf[rows, :]
            last = lax.broadcasted_iota(jnp.int32, (1, 128), 1) == 127
            outs[1][rows, :] = jnp.where(last, total, best_buf[rows, :])


def attend(scalars, queries, head, heads, kv_count, slots, cache=None, window=None, carry=None,
           into=None, final=True):
    tok = queries.shape[0]
    kv_head = head // (AH // KVH)
    hops = len(window) - 1 if window is not None else 0
    rows = heads * tok
    depth = slots if cache is not None else 0
    if window is not None:
        depth += -(-((hops + 1) * tok) // (2 * KEY_BLOCK)) * (2 * KEY_BLOCK)
    anywhere = pl.BlockSpec(memory_space=pl.ANY)
    part = pl.BlockSpec((tok, heads * HD), lambda k: (0, head // heads))
    whole = pl.BlockSpec((rows, 128), lambda k: (0, 0))
    operands, in_specs = [scalars, queries], [SCALARS, part]
    for group in (cache, window):
        if group is not None:
            operands += list(group)
            in_specs += [anywhere] * len(group)
    if carry is not None:
        operands += list(carry)
        in_specs += [whole] * 2
    aliases = {}
    if into is not None:
        aliases = {len(operands): 0}
        operands.append(into)
        in_specs.append(anywhere)
    if final:
        out_specs, out_shape = part, jax.ShapeDtypeStruct(queries.shape, BF16)
    else:
        out_specs, out_shape = [whole] * 2, [jax.ShapeDtypeStruct((rows, 128), F32)] * 2
    return pl.pallas_call(
        functools.partial(
            attend_kernel, kv_head=kv_head, kv_count=kv_count, heads=heads, hops=hops,
            slots=slots, use_cache=cache is not None, use_window=window is not None,
            carry_in=carry is not None, final=final, alias=len(aliases),
        ),
        grid_spec=pl.GridSpec(
            grid=(1,),
            in_specs=in_specs,
            out_specs=out_specs,
            scratch_shapes=[
                pltpu.VMEM((depth, HD), BF16),
                pltpu.VMEM((depth, HD), BF16),
                pltpu.VMEM((rows, depth), F32),
                pltpu.VMEM((rows, 128), F32),
                pltpu.VMEM((rows, 128), F32),
                pltpu.VMEM((rows, 128), F32),
                pltpu.SemaphoreType.DMA((2, slots // KEY_BLOCK)),
                pltpu.SemaphoreType.DMA((2, hops + 1)),
            ],
        ),
        out_shape=out_shape,
        input_output_aliases=aliases,
        compiler_params=pltpu.CompilerParams(vmem_limit_bytes=VMEM_LIMIT),
        cost_estimate=pl.CostEstimate(
            flops=16 * rows * depth * HD, bytes_accessed=4 * depth * HD,
            transcendentals=rows * depth,
        ),
        name="attend",
    )(*operands)


def tie(*values):
    return lax.optimization_barrier(values)


def local(x_in, z_gate, b_in, c_in, dt_raw, dt_bias, a_log, d_skip, norm_weight, ssm_init, queries,
          keys, values, cache_keys, cache_values, window_start, prefix_len):
    tok, lanes = x_in.shape
    head_count = dt_raw.shape[1]
    per_group = MH // NG
    places = lax.axis_size("seq")
    place = lax.axis_index("seq")
    dp = lax.axis_index("dp")
    q_count = queries.shape[1] // HD
    kv_here = keys.shape[1] // HD
    kv_count = max(1, q_count * KVH // AH)
    width = min(lanes, STATE_WIDTH * kv_count * HD)
    chunks = lanes // width
    column = (dp * q_count) // (AH // KVH)
    slots = 2 * cache_keys.shape[0]

    ring = [(k, (k + 1) % places) for k in range(places)]
    swap = [(0, 1), (1, 0)]
    far_keys = lax.ppermute(cache_keys, "dp", swap)
    far_values = lax.ppermute(cache_values, "dp", swap)

    own_rows = jnp.concatenate(
        [
            lax.dynamic_slice_in_dim(array, column * HD, kv_count * HD, axis=1)
            for array in (keys, values)
        ],
        axis=1,
    )

    newest = jnp.mod(window_start[0] - 1, slots)
    held = prefix_len[0]
    oldest = jnp.mod(newest - held + 1, slots)
    first_block = oldest // KEY_BLOCK
    cache_blocks = jnp.minimum(
        slots // KEY_BLOCK, (oldest % KEY_BLOCK + held + KEY_BLOCK - 1) // KEY_BLOCK
    )
    first_head = dp * head_count
    scalars = jnp.stack(
        [place, dp, first_block, cache_blocks, newest, held, column, first_head]
    ).astype(jnp.int32)

    received = []
    send = own_rows
    arrived = lax.ppermute(send, "seq", ring)
    x_tied, send = tie(x_in, send)
    span = max(width, min(lanes, per_group * MP))
    states, rows, logt, dtt, first_chunk = ssm_states(
        scalars, x_tied, b_in, dt_raw, dt_bias, a_log, d_skip, ssm_init, width, span
    )
    received.append(arrived)

    cache = (cache_keys, far_keys, cache_values, far_values)
    heads = min(HEADS_IN_CALL, q_count)
    parts = list(range(0, q_count, heads))
    last_step = places - 1 + chunks - 1
    result = inner = opened = mamba_out = None
    outputs_done = 0

    def outputs(chunk, into):
        return ssm_outputs(
            scalars, inner, z_gate, c_in, logt, norm_weight, ssm_init,
            received[chunk + 1 : chunk + places], width, chunk, into,
        )

    slots_here = slots

    def attend_next(queries_now, into):
        window = [own_rows] + received[: places - 1]
        head, carry = parts.pop(0)
        return attend(
            scalars, queries_now, head, heads, kv_count, slots_here,
            cache=None if carry else cache, window=window, carry=carry, into=into,
        )

    parts = [(head, None) for head in parts]
    for step in range(1, last_step + 1):
        incoming = received[-1]
        if step == 1:
            incoming, states = tie(incoming, states)
        elif result is not None:
            incoming, result = tie(incoming, result)
        elif opened is not None:
            incoming, *opened = tie(incoming, *opened)
        else:
            incoming, inner = tie(incoming, inner)
        if step == 1:
            padding = ((0, 0), (0, width - incoming.shape[1]))
            send = jnp.where(place > 0, jnp.pad(incoming, padding), first_chunk)
        else:
            send = hop(place, incoming, states, rows, step)
        senders = range(max(0, step - chunks), places - 1)
        pairs = ring if len(senders) == places - 1 else [(k, k + 1) for k in senders]
        arrived = lax.ppermute(send, "seq", pairs)
        if step == 1:
            x_tied, send = tie(x_in, send)
            inner = ssm_inner(scalars, x_tied, b_in, c_in, logt, dtt, rows, width)
        elif step == OPEN_STEP and len(parts) > 1:
            queries_now, send = tie(queries, send)
            head = parts.pop(0)[0]
            opened = attend(
                scalars, queries_now, head, heads, kv_count, slots_here, cache=cache, final=False
            )
            parts.append((head, opened))
        elif step >= places - 1 and parts:
            queries_now, send = tie(queries, send)
            if opened is not None and parts[0][1] is not None:
                parts[0] = (parts[0][0], opened)
            result = attend_next(queries_now, result)
            if step == last_step and chunks > 1:
                logt, send = tie(logt, send)
                mamba_out = outputs(0, mamba_out)
                outputs_done = 1
        received.append(arrived)
    while parts:
        result = attend_next(queries, result)
    for chunk in range(outputs_done, chunks):
        mamba_out = outputs(chunk, mamba_out)
    return (mamba_out, result)


def solution(mesh):
    rows = P(("groups", "seq"), ("tp", "dp"))
    shared = P(("groups", "seq"), "tp")
    heads = P(("tp", "dp"))
    cached = P(("groups", "dp"), "tp")
    return jax.shard_map(
        local,
        mesh=mesh,
        in_specs=(
            rows, rows, shared, shared, rows, heads, heads, heads, heads,
            P(("groups", "tp", "dp"), None, None), rows, shared, shared, cached, cached,
            P("groups"), P("groups"),
        ),
        out_specs=(rows, rows),
        check_vma=False,
    )
```

```python
import functools
import math

import jax
import jax.numpy as jnp
from jax import lax
from jax.experimental import pallas as pl
from jax.experimental.pallas import tpu as pltpu
from jax.sharding import PartitionSpec as P

MH = 128
MP = 64
N_STATE = 256
NG = 8
AH = 64
KVH = 8
HD = 128
BLOCK = 128
KEY_BLOCK = 512
GROUPS = (4, 2, 1)
STATE_WIDTH = 4
HEADS_IN_CALL = 8
OPEN_STEP = 2
LOG2_SCALE = math.log2(math.e) / math.sqrt(HD)
NEG = -1e30
F32 = jnp.float32
BF16 = jnp.bfloat16
VMEM_LIMIT = 56 << 20


SCALARS = pl.BlockSpec(memory_space=pltpu.SMEM)


def group_lanes(scalars, head):
    group = (scalars[7] + head) // (MH // NG)
    return pl.ds(pl.multiple_of(group * N_STATE, N_STATE), N_STATE)


def mm(a, b):
    return jnp.dot(a, b, preferred_element_type=F32)


def mm_nt(a, b):
    return lax.dot_general(a, b, (((1,), (1,)), ((), ())), preferred_element_type=F32)


def pieces_of(value):
    first = value.astype(BF16)
    rest = value - first.astype(F32)
    second = rest.astype(BF16)
    third = (rest - second.astype(F32)).astype(BF16)
    return first, second, third


def head_table(heads, width):
    row = lax.broadcasted_iota(jnp.int32, (heads, width), 0)
    lane = lax.broadcasted_iota(jnp.int32, (heads, width), 1)
    table = jnp.where(lane // MP == row, 1.0, 0.0).astype(BF16)
    return jnp.concatenate([table] * 3, axis=0)


def expand(value, table):
    stacked = jnp.concatenate(pieces_of(value), axis=0)
    return lax.dot_general(stacked, table, (((0,), (0,)), ((), ())), preferred_element_type=F32)


def fold_lanes(value, op):
    parts = [value[:, k : k + 128] for k in range(0, value.shape[1], 128)]
    while len(parts) > 1:
        parts = [
            op(parts[k], parts[k + 1]) if k + 1 < len(parts) else parts[k]
            for k in range(0, len(parts), 2)
        ]
    return parts[0]


def ssm_states_kernel(
    scalars, x_ref, b_ref, dt_ref, bias_ref, alog_ref, dskip_ref, init_ref,
    state_ref, rows_ref, logt_ref, dtt_ref, first_ref, dt_all, log_all, skip_all,
):
    span = pl.program_id(0)
    tok, lanes = x_ref.shape
    heads = lanes // MP
    spans = dt_ref.shape[0] // heads
    parts = state_ref.shape[0]
    width = lanes // parts
    group = group_lanes(scalars, span * heads)

    @pl.when(span == 0)
    def _():
        column = lambda ref: jnp.broadcast_to(ref[...], (8, ref.shape[1])).T[:, 0:1]
        dt = jax.nn.softplus(dt_ref[...] + column(bias_ref))
        decay = -jnp.exp(column(alog_ref)) * dt
        row = lax.broadcasted_iota(jnp.int32, (BLOCK, BLOCK), 0)
        col = lax.broadcasted_iota(jnp.int32, (BLOCK, BLOCK), 1)
        upper = jnp.where(row <= col, 1.0, 0.0).astype(BF16)
        logs = []
        for blk in range(tok // BLOCK):
            first, second, third = pieces_of(decay[:, blk * BLOCK : (blk + 1) * BLOCK])
            logs.append(mm(first, upper) + mm(second, upper) + mm(third, upper))
        logs = jnp.concatenate(logs, axis=1)
        skip = jnp.broadcast_to(column(dskip_ref), (dt_ref.shape[0], 128))
        for k in range(spans):
            dt_all[k] = dt[k * heads : (k + 1) * heads]
            log_all[k] = logs[k * heads : (k + 1) * heads]
            skip_all[k] = skip[k * heads : (k + 1) * heads]

    dt = dt_all[span]
    logs = log_all[span]
    few = heads // parts
    for k in range(parts):
        logt_ref[k] = logs[k * few : (k + 1) * few]
        dtt_ref[k] = dt[k * few : (k + 1) * few]
    table = head_table(heads, lanes)
    state = None
    total = jnp.zeros((heads, 1), F32)
    for blk in range(tok // BLOCK):
        part = slice(blk * BLOCK, (blk + 1) * BLOCK)
        end = logs[:, (blk + 1) * BLOCK - 1 : (blk + 1) * BLOCK]
        tail = jnp.exp(end - logs[:, part]) * dt[:, part]
        weighted = (expand(tail, table) * x_ref[part, :].astype(F32)).astype(BF16)
        update = mm(b_ref[part, group].T, weighted)
        if state is None:
            state = update
        else:
            state = expand(jnp.broadcast_to(jnp.exp(end), (heads, 8)), table)[0:1] * state + update
        total = total + end
    place = scalars[0]
    lane = lax.broadcasted_iota(jnp.int32, (heads, 8), 1)
    rows = expand(jnp.where(lane == 0, jnp.exp(total), skip_all[span][:, 0:8]), table)
    for k in range(parts):
        state_ref[k] = state[:, k * width : (k + 1) * width]
        rows_ref[k] = rows[:, k * width : (k + 1) * width]

    @pl.when(place == 0)
    def _():
        for k in range(parts):
            first = init_ref[k * few : (k + 1) * few].reshape(width, N_STATE).T
            state_ref[k] = state_ref[k] + rows_ref[k, 0:1, :] * first
            rows_ref[k, 0:1, :] = jnp.zeros((1, width), F32)

    @pl.when(span == 0)
    def _():
        first_ref[...] = state_ref[0].astype(BF16)


def ssm_states(scalars, x_in, b_in, dt_raw, dt_bias, a_log, d_skip, ssm_init, width, span):
    tok, lanes = x_in.shape
    chunks = lanes // width
    head_count = dt_raw.shape[1]
    heads = span // MP
    few = width // MP
    parts = span // width
    flat = lambda c: (0, 0)
    major = lambda c: (c, 0, 0)
    return pl.pallas_call(
        ssm_states_kernel,
        grid_spec=pl.GridSpec(
            grid=(lanes // span,),
            in_specs=[
                SCALARS,
                pl.BlockSpec((tok, span), lambda c: (0, c)),
                pl.BlockSpec(b_in.shape, flat),
                pl.BlockSpec((head_count, tok), flat),
                pl.BlockSpec((1, head_count), flat),
                pl.BlockSpec((1, head_count), flat),
                pl.BlockSpec((1, head_count), flat),
                pl.BlockSpec((heads, MP, N_STATE), major),
            ],
            out_specs=[
                pl.BlockSpec((parts, N_STATE, width), major),
                pl.BlockSpec((parts, 8, width), major),
                pl.BlockSpec((parts, few, tok), major),
                pl.BlockSpec((parts, few, tok), major),
                pl.BlockSpec((N_STATE, width), flat),
            ],
            scratch_shapes=[
                pltpu.VMEM((lanes // span, heads, tok), F32),
                pltpu.VMEM((lanes // span, heads, tok), F32),
                pltpu.VMEM((lanes // span, heads, 128), F32),
            ],
        ),
        out_shape=[
            jax.ShapeDtypeStruct((chunks, N_STATE, width), F32),
            jax.ShapeDtypeStruct((chunks, 8, width), F32),
            jax.ShapeDtypeStruct((chunks, few, tok), F32),
            jax.ShapeDtypeStruct((chunks, few, tok), F32),
            jax.ShapeDtypeStruct((N_STATE, width), BF16),
        ],
        compiler_params=pltpu.CompilerParams(vmem_limit_bytes=VMEM_LIMIT),
        cost_estimate=pl.CostEstimate(
            flops=2 * tok * lanes * N_STATE * 4, bytes_accessed=6 << 20, transcendentals=1 << 16
        ),
        name="ssm_states",
    )(
        scalars, x_in, b_in, dt_raw.T, dt_bias[None, :], a_log[None, :], d_skip[None, :], ssm_init
    )


def hop(place, received, states, rows, step):
    chunks = states.shape[0]
    chunk = jnp.clip(step - 1 - place, 0, chunks - 1)
    state = lax.dynamic_index_in_dim(states, chunk, 0, keepdims=False)
    decay = lax.dynamic_index_in_dim(rows, chunk, 0, keepdims=False)[0:1, :]
    combined = (decay * received.astype(F32) + state).astype(BF16)
    return jnp.where(step <= place, received, combined)


def ssm_inner_kernel(scalars, x_ref, b_ref, c_ref, logt_ref, dtt_ref, rows_ref, out_ref):
    tok, width = x_ref.shape
    heads = width // MP
    row = lax.broadcasted_iota(jnp.int32, (BLOCK, BLOCK), 0)
    col = lax.broadcasted_iota(jnp.int32, (BLOCK, BLOCK), 1)
    lower = row >= col
    low_half = col < MP
    table = head_table(heads, width)
    logt = logt_ref[0]
    dtt = dtt_ref[0]
    logs = logt.T
    skip = rows_ref[0, 1:2, :]
    state = None
    pairs = heads // 2
    group = group_lanes(scalars, pl.program_id(0) * heads)
    for blk in range(tok // BLOCK):
        part = slice(blk * BLOCK, (blk + 1) * BLOCK)
        c_blk = c_ref[part, group]
        b_blk = b_ref[part, group]
        x_blk = x_ref[part, :]
        products = mm_nt(c_blk, b_blk)
        log_blk = logs[part]
        kernels = []
        for h in range(heads):
            spread = log_blk[:, h : h + 1] - logt[h : h + 1, part]
            decay = jnp.exp(jnp.where(lower, spread, NEG))
            kernels.append((decay * products * dtt[h : h + 1, part]).astype(BF16))
        carried = None
        if state is not None:
            carried = expand(jnp.exp(logt[:, part]), table) * mm(c_blk, state.astype(BF16))
        if (blk + 1) * BLOCK < tok:
            end = logt[:, (blk + 1) * BLOCK - 1 : (blk + 1) * BLOCK]
            tail = jnp.exp(end - logt[:, part]) * dtt[:, part]
            weighted = (expand(tail, table) * x_blk.astype(F32)).astype(BF16)
            update = mm(b_blk.T, weighted)
            if state is None:
                state = update
            else:
                factor = expand(jnp.broadcast_to(jnp.exp(end), (heads, 8)), table)[0:1]
                state = factor * state + update
        for pair in range(pairs):
            lanes = slice(pair * 128, (pair + 1) * 128)
            x_pair = x_blk[:, lanes]
            zero = jnp.zeros_like(x_pair)
            stacked = jnp.concatenate(
                [jnp.where(low_half, x_pair, zero), jnp.where(low_half, zero, x_pair)], axis=0
            )
            inner = mm(jnp.concatenate(kernels[2 * pair : 2 * pair + 2], axis=1), stacked)
            value = inner + skip[:, lanes] * x_pair.astype(F32)
            if carried is not None:
                value = value + carried[:, lanes]
            out_ref[part, lanes] = value


def ssm_inner(scalars, x_in, b_in, c_in, logt, dtt, rows, width):
    tok, lanes = x_in.shape
    chunks = lanes // width
    heads = width // MP
    per_chunk = pl.BlockSpec((tok, width), lambda c: (0, c))
    grouped = pl.BlockSpec(b_in.shape, lambda c: (0, 0))
    major = lambda c: (c, 0, 0)
    return pl.pallas_call(
        ssm_inner_kernel,
        grid_spec=pl.GridSpec(
            grid=(chunks,),
            in_specs=[
                SCALARS,
                per_chunk,
                grouped,
                grouped,
                pl.BlockSpec((1, heads, tok), major),
                pl.BlockSpec((1, heads, tok), major),
                pl.BlockSpec((1, 8, width), major),
            ],
            out_specs=per_chunk,
        ),
        out_shape=jax.ShapeDtypeStruct((tok, lanes), F32),
        compiler_params=pltpu.CompilerParams(vmem_limit_bytes=VMEM_LIMIT),
        cost_estimate=pl.CostEstimate(
            flops=2 * tok * lanes * N_STATE * 8, bytes_accessed=6 << 20, transcendentals=1 << 21
        ),
        name="ssm_inner",
    )(scalars, x_in, b_in, c_in, logt, dtt, rows)


def ssm_outputs_kernel(
    scalars, inner_ref, z_ref, c_ref, logt_ref, norm_ref, init_hbm, *rest, hops, chunk, alias,
):
    received = rest[:hops]
    out_ref, carry, init_buf, sem = rest[hops + alias :]
    place = scalars[0]
    tok, width = inner_ref.shape
    heads = width // MP

    for r in range(hops):
        @pl.when(place == r + 1)
        def _():
            pltpu.make_async_copy(received[r], carry, sem).start()

    initial = pltpu.make_async_copy(
        init_hbm.at[chunk * heads : (chunk + 1) * heads], init_buf, sem
    )

    @pl.when(place == 0)
    def _():
        initial.start()

    row = lax.broadcasted_iota(jnp.int32, (BLOCK, BLOCK), 0)
    col = lax.broadcasted_iota(jnp.int32, (BLOCK, BLOCK), 1)
    mean_table = jnp.where(row // MP == col // MP, 1.0 / MP, 0.0).astype(BF16)
    mean_table = jnp.concatenate([mean_table, mean_table], axis=0)
    table = head_table(heads, width)
    logt = logt_ref[0]
    whole_logs = []
    before = jnp.zeros((heads, 1), F32)
    for blk in range(tok // BLOCK):
        part = slice(blk * BLOCK, (blk + 1) * BLOCK)
        whole_logs.append(jnp.exp(logt[:, part] + before))
        before = before + logt[:, (blk + 1) * BLOCK - 1 : (blk + 1) * BLOCK]
    spread = expand(jnp.concatenate(whole_logs, axis=1), table)
    z = z_ref[...].astype(F32)
    gate = z / (1.0 + jnp.exp(-z))

    @pl.when(place > 0)
    def _():
        pltpu.make_async_copy(received[0], carry, sem).wait()

    @pl.when(place == 0)
    def _():
        initial.wait()
        carry[...] = init_buf[...].reshape(width, N_STATE).astype(BF16).T

    gated = (inner_ref[...] + spread * mm(c_ref[:, group_lanes(scalars, chunk * heads)], carry[...])) * gate
    square = gated * gated
    high = square.astype(BF16)
    low = (square - high.astype(F32)).astype(BF16)
    for at in range(0, width, 128):
        lanes = slice(at, at + 128)
        mean = mm(jnp.concatenate([high[:, lanes], low[:, lanes]], axis=1), mean_table)
        normed = gated[:, lanes] * lax.rsqrt(mean + 1e-05) * norm_ref[:, lanes]
        out_ref[:, lanes] = normed.astype(BF16)


def ssm_outputs(scalars, inner, z_gate, c_in, logt, norm_weight, ssm_init, received, width, chunk,
                into):
    tok, lanes = inner.shape
    heads = width // MP
    anywhere = pl.BlockSpec(memory_space=pl.ANY)
    per_chunk = pl.BlockSpec((tok, width), lambda k: (0, chunk))
    operands = [scalars, inner, z_gate, c_in, logt, norm_weight[None, :], ssm_init, *received]
    in_specs = [
        SCALARS,
        per_chunk,
        per_chunk,
        pl.BlockSpec(c_in.shape, lambda k: (0, 0)),
        pl.BlockSpec((1, heads, tok), lambda k: (chunk, 0, 0)),
        pl.BlockSpec((1, width), lambda k: (0, chunk)),
    ] + [anywhere] * (1 + len(received))
    aliases = {}
    if into is not None:
        aliases = {len(operands): 0}
        operands.append(into)
        in_specs.append(anywhere)
    return pl.pallas_call(
        functools.partial(
            ssm_outputs_kernel, hops=len(received), chunk=chunk, alias=len(aliases)
        ),
        grid_spec=pl.GridSpec(
            grid=(1,),
            in_specs=in_specs,
            out_specs=per_chunk,
            scratch_shapes=[
                pltpu.VMEM((N_STATE, width), BF16),
                pltpu.VMEM((heads, MP, N_STATE), F32),
                pltpu.SemaphoreType.DMA,
            ],
        ),
        out_shape=jax.ShapeDtypeStruct((tok, lanes), BF16),
        input_output_aliases=aliases,
        compiler_params=pltpu.CompilerParams(vmem_limit_bytes=VMEM_LIMIT),
        cost_estimate=pl.CostEstimate(
            flops=2 * tok * width * N_STATE * 2, bytes_accessed=2 << 20, transcendentals=1 << 18
        ),
        name="ssm_outputs",
    )(*operands)


def attend_kernel(scalars, q_ref, *rest, kv_head, kv_count, heads, hops, slots, use_cache,
                  use_window, carry_in, final, alias):
    rest = list(rest)
    take = lambda count: [rest.pop(0) for _ in range(count)]
    keys_near, keys_far, values_near, values_far = take(4) if use_cache else [None] * 4
    window = take(hops + 1) if use_window else []
    acc_in, state_in = take(2) if carry_in else (None, None)
    take(alias)
    outs = take(1 if final else 2)
    k_buf, v_buf, s_buf, best_buf, total_buf, acc_buf, sems, window_sems = rest
    place, dp, first_block, cache_blocks, newest, held = (scalars[k] for k in range(6))
    column = scalars[6]
    tok = q_ref.shape[0]
    half = slots // 2
    cache_total = slots // KEY_BLOCK
    base = slots if use_cache else 0
    lanes = pl.ds(pl.multiple_of((column + kv_head) * HD, HD), HD)
    lane = lax.broadcasted_iota(jnp.int32, (1, KEY_BLOCK), 1)

    def block_of(j):
        return lax.rem(first_block + j, cache_total)

    def block_copy(which, source, block):
        rows = pl.ds(pl.multiple_of(lax.rem(block * KEY_BLOCK, half), KEY_BLOCK), KEY_BLOCK)
        into = pl.ds(pl.multiple_of(block * KEY_BLOCK, KEY_BLOCK), KEY_BLOCK)
        buf = (k_buf, v_buf)[which]
        return pltpu.make_async_copy(source.at[rows, lanes], buf.at[into], sems.at[which, block])

    for which, near, far in ((0, keys_near, keys_far), (1, values_near, values_far)):
        def start(j, unused, which=which, near=near, far=far):
            block = block_of(j)
            mine = block // (half // KEY_BLOCK) == dp

            @pl.when(mine)
            def _():
                block_copy(which, near, block).start()

            @pl.when(jnp.logical_not(mine))
            def _():
                block_copy(which, far, block).start()

            return 0

        if use_cache:
            lax.fori_loop(0, cache_blocks, start, 0)

    window_copies = []
    for which, buf, at in ((0, k_buf, kv_head), (1, v_buf, kv_count + kv_head)):
        for k, ref in enumerate(window):
            window_copies.append(
                pltpu.make_async_copy(
                    ref.at[:, at * HD : (at + 1) * HD],
                    buf.at[base + k * tok : base + (k + 1) * tok],
                    window_sems.at[which, k],
                )
            )
    for copy in window_copies:
        copy.start()
    depth = k_buf.shape[0]
    loose = base + (hops + 1) * tok
    if use_window and depth > loose:
        for buf in (k_buf, v_buf):
            buf[loose:depth, :] = jnp.zeros((depth - loose, HD), BF16)

    def score(offsets, biases):
        for h in range(heads):
            rows = slice(h * tok, (h + 1) * tok)
            best = best_buf[rows, :]
            for offset, bias in zip(offsets, biases):
                span = pl.ds(offset, KEY_BLOCK)
                scores = mm_nt(q_ref[:, h * HD : (h + 1) * HD], k_buf[span, :])
                scores = scores * LOG2_SCALE + bias
                s_buf[rows, span] = scores
                best = jnp.maximum(best, fold_lanes(scores, jnp.maximum))
            best_buf[rows, :] = best

    def mix(offsets):
        for h in range(heads):
            rows = slice(h * tok, (h + 1) * tok)
            best = best_buf[rows, :]
            total = total_buf[rows, :]
            acc = acc_buf[rows, :]
            for offset in offsets:
                probs = jnp.concatenate(
                    [
                        jnp.exp2(s_buf[rows, pl.ds(offset + k, 128)] - best)
                        for k in range(0, KEY_BLOCK, 128)
                    ],
                    axis=1,
                )
                total = total + fold_lanes(probs, jnp.add)
                acc = acc + mm(probs.astype(BF16), v_buf[pl.ds(offset, KEY_BLOCK), :])
            total_buf[rows, :] = total
            acc_buf[rows, :] = acc

    def sweep(visit):
        if not use_cache:
            return
        done = 0
        for size in GROUPS:
            if size > cache_total:
                continue
            count = (cache_blocks - done) // size

            def some(j, unused, size=size, done=done):
                visit([block_of(done + j * size + k) for k in range(size)])
                return 0

            lax.fori_loop(0, count, some, 0)
            done = done + count * size

    def place_of(block):
        return pl.multiple_of(block * KEY_BLOCK, KEY_BLOCK)

    def cache_score(blocks):
        offsets, biases = [], []
        for block in blocks:
            block_copy(0, keys_near, block).wait()
            offset = place_of(block)
            age = newest - (offset + lane)
            age = jnp.where(age < 0, age + slots, age)
            offsets.append(offset)
            biases.append(jnp.where(age < held, 0.0, NEG))
        score(offsets, biases)

    def cache_mix(blocks):
        for block in blocks:
            block_copy(1, values_near, block).wait()
        mix([place_of(block) for block in blocks])

    double = 2 * KEY_BLOCK
    window_pairs = (place * tok + tok + double - 1) // double

    def window_bias(at):
        if isinstance(at, int) and at * KEY_BLOCK < tok:
            later = (
                lax.broadcasted_iota(jnp.int32, (tok, KEY_BLOCK), 0)
                - lax.broadcasted_iota(jnp.int32, (tok, KEY_BLOCK), 1)
            )
            allowed = (later >= 0) | ((lane >= tok) & (lane < tok * (place + 1)))
        else:
            allowed = lane + at * KEY_BLOCK < tok * (place + 1)
        return jnp.where(allowed, 0.0, NEG)

    def window_offsets(j):
        return [pl.multiple_of(base + (2 * j + k) * KEY_BLOCK, KEY_BLOCK) for k in range(2)]

    if carry_in:
        best_buf[...] = jnp.broadcast_to(state_in[:, 0:1], best_buf.shape)
    else:
        best_buf[...] = jnp.full_like(best_buf, NEG)
    sweep(cache_score)
    if use_window:
        for copy in window_copies[: hops + 1]:
            copy.wait()
        score([base, base + KEY_BLOCK], [window_bias(0), window_bias(1)])

        def more_scores(j, unused):
            score(window_offsets(j), [window_bias(2 * j), window_bias(2 * j + 1)])
            return 0

        if depth > base + double:
            lax.fori_loop(1, window_pairs, more_scores, 0)
    best_buf[...] = jnp.broadcast_to(
        jnp.max(best_buf[...], axis=-1, keepdims=True), best_buf.shape
    )
    if carry_in:
        factor = jnp.exp2(jnp.broadcast_to(state_in[:, 0:1], best_buf.shape) - best_buf[...])
        first = lax.broadcasted_iota(jnp.int32, (1, 128), 1) == 127
        acc_buf[...] = factor * acc_in[...]
        total_buf[...] = jnp.where(first, factor * state_in[...], 0.0)
    else:
        acc_buf[...] = jnp.zeros_like(acc_buf)
        total_buf[...] = jnp.zeros_like(total_buf)
    sweep(cache_mix)
    if use_window:
        for copy in window_copies[hops + 1 :]:
            copy.wait()
        mix([base, base + KEY_BLOCK])

        def more_mix(j, unused):
            mix(window_offsets(j))
            return 0

        if depth > base + double:
            lax.fori_loop(1, window_pairs, more_mix, 0)
    for h in range(heads):
        rows = slice(h * tok, (h + 1) * tok)
        total = jnp.sum(total_buf[rows, :], axis=-1, keepdims=True)
        if final:
            outs[0][:, h * HD : (h + 1) * HD] = (acc_buf[rows, :] / total).astype(BF16)
        else:
            outs[0][rows, :] = acc_buf[rows, :]
            last = lax.broadcasted_iota(jnp.int32, (1, 128), 1) == 127
            outs[1][rows, :] = jnp.where(last, total, best_buf[rows, :])


def attend(scalars, queries, head, heads, kv_count, slots, cache=None, window=None, carry=None,
           into=None, final=True):
    tok = queries.shape[0]
    kv_head = head // (AH // KVH)
    hops = len(window) - 1 if window is not None else 0
    rows = heads * tok
    depth = slots if cache is not None else 0
    if window is not None:
        depth += -(-((hops + 1) * tok) // (2 * KEY_BLOCK)) * (2 * KEY_BLOCK)
    anywhere = pl.BlockSpec(memory_space=pl.ANY)
    part = pl.BlockSpec((tok, heads * HD), lambda k: (0, head // heads))
    whole = pl.BlockSpec((rows, 128), lambda k: (0, 0))
    operands, in_specs = [scalars, queries], [SCALARS, part]
    for group in (cache, window):
        if group is not None:
            operands += list(group)
            in_specs += [anywhere] * len(group)
    if carry is not None:
        operands += list(carry)
        in_specs += [whole] * 2
    aliases = {}
    if into is not None:
        aliases = {len(operands): 0}
        operands.append(into)
        in_specs.append(anywhere)
    if final:
        out_specs, out_shape = part, jax.ShapeDtypeStruct(queries.shape, BF16)
    else:
        out_specs, out_shape = [whole] * 2, [jax.ShapeDtypeStruct((rows, 128), F32)] * 2
    return pl.pallas_call(
        functools.partial(
            attend_kernel, kv_head=kv_head, kv_count=kv_count, heads=heads, hops=hops,
            slots=slots, use_cache=cache is not None, use_window=window is not None,
            carry_in=carry is not None, final=final, alias=len(aliases),
        ),
        grid_spec=pl.GridSpec(
            grid=(1,),
            in_specs=in_specs,
            out_specs=out_specs,
            scratch_shapes=[
                pltpu.VMEM((depth, HD), BF16),
                pltpu.VMEM((depth, HD), BF16),
                pltpu.VMEM((rows, depth), F32),
                pltpu.VMEM((rows, 128), F32),
                pltpu.VMEM((rows, 128), F32),
                pltpu.VMEM((rows, 128), F32),
                pltpu.SemaphoreType.DMA((2, slots // KEY_BLOCK)),
                pltpu.SemaphoreType.DMA((2, hops + 1)),
            ],
        ),
        out_shape=out_shape,
        input_output_aliases=aliases,
        compiler_params=pltpu.CompilerParams(vmem_limit_bytes=VMEM_LIMIT),
        cost_estimate=pl.CostEstimate(
            flops=16 * rows * depth * HD, bytes_accessed=4 * depth * HD,
            transcendentals=rows * depth,
        ),
        name="attend",
    )(*operands)


def tie(*values):
    return lax.optimization_barrier(values)


def local(x_in, z_gate, b_in, c_in, dt_raw, dt_bias, a_log, d_skip, norm_weight, ssm_init, queries,
          keys, values, cache_keys, cache_values, window_start, prefix_len):
    tok, lanes = x_in.shape
    head_count = dt_raw.shape[1]
    per_group = MH // NG
    places = lax.axis_size("seq")
    place = lax.axis_index("seq")
    dp = lax.axis_index("dp")
    q_count = queries.shape[1] // HD
    kv_here = keys.shape[1] // HD
    kv_count = max(1, q_count * KVH // AH)
    width = min(lanes, STATE_WIDTH * kv_count * HD)
    chunks = lanes // width
    column = (dp * q_count) // (AH // KVH)
    slots = 2 * cache_keys.shape[0]

    ring = [(k, (k + 1) % places) for k in range(places)]
    swap = [(0, 1), (1, 0)]
    own_rows = jnp.concatenate(
        [
            lax.dynamic_slice_in_dim(array, column * HD, kv_count * HD, axis=1)
            for array in (keys, values)
        ],
        axis=1,
    )

    newest = jnp.mod(window_start[0] - 1, slots)
    held = prefix_len[0]
    oldest = jnp.mod(newest - held + 1, slots)
    first_block = oldest // KEY_BLOCK
    cache_blocks = jnp.minimum(
        slots // KEY_BLOCK, (oldest % KEY_BLOCK + held + KEY_BLOCK - 1) // KEY_BLOCK
    )
    first_head = dp * head_count
    scalars = jnp.stack(
        [place, dp, first_block, cache_blocks, newest, held, column, first_head]
    ).astype(jnp.int32)

    received = []
    send = own_rows
    arrived = lax.ppermute(send, "seq", ring)
    x_tied, send = tie(x_in, send)
    span = max(width, min(lanes, per_group * MP))
    states, rows, logt, dtt, first_chunk = ssm_states(
        scalars, x_tied, b_in, dt_raw, dt_bias, a_log, d_skip, ssm_init, width, span
    )
    received.append(arrived)

    heads = min(HEADS_IN_CALL, q_count)
    parts = list(range(0, q_count, heads))
    last_step = places - 1 + chunks - 1
    result = inner = opened = mamba_out = None
    outputs_done = 0

    def outputs(chunk, into):
        return ssm_outputs(
            scalars, inner, z_gate, c_in, logt, norm_weight, ssm_init,
            received[chunk + 1 : chunk + places], width, chunk, into,
        )

    slots_here = slots

    def attend_next(queries_now, into):
        window = [own_rows] + received[: places - 1]
        head, carry = parts.pop(0)
        return attend(
            scalars, queries_now, head, heads, kv_count, slots_here,
            cache=None if carry else cache, window=window, carry=carry, into=into,
        )

    parts = [(head, None) for head in parts]
    for step in range(1, last_step + 1):
        incoming = received[-1]
        if step == 1:
            incoming, states = tie(incoming, states)
        elif result is not None:
            incoming, result = tie(incoming, result)
        elif opened is not None:
            incoming, *opened = tie(incoming, *opened)
        else:
            incoming, inner = tie(incoming, inner)
        if step == 1:
            padding = ((0, 0), (0, width - incoming.shape[1]))
            send = jnp.where(place > 0, jnp.pad(incoming, padding), first_chunk)
        else:
            send = hop(place, incoming, states, rows, step)
        senders = range(max(0, step - chunks), places - 1)
        pairs = ring if len(senders) == places - 1 else [(k, k + 1) for k in senders]
        arrived = lax.ppermute(send, "seq", pairs)
        if step == 1:
            x_tied, keys_tied, values_tied, send = tie(x_in, cache_keys, cache_values, send)
            far_keys = lax.ppermute(keys_tied, "dp", swap)
            far_values = lax.ppermute(values_tied, "dp", swap)
            cache = (cache_keys, far_keys, cache_values, far_values)
            inner = ssm_inner(scalars, x_tied, b_in, c_in, logt, dtt, rows, width)
        elif step == OPEN_STEP and len(parts) > 1:
            queries_now, send = tie(queries, send)
            head = parts.pop(0)[0]
            opened = attend(
                scalars, queries_now, head, heads, kv_count, slots_here, cache=cache, final=False
            )
            parts.append((head, opened))
        elif step >= places - 1 and parts:
            queries_now, send = tie(queries, send)
            if opened is not None and parts[0][1] is not None:
                parts[0] = (parts[0][0], opened)
            result = attend_next(queries_now, result)
            if step == last_step and chunks > 1:
                logt, send = tie(logt, send)
                mamba_out = outputs(0, mamba_out)
                outputs_done = 1
        received.append(arrived)
    while parts:
        result = attend_next(queries, result)
    for chunk in range(outputs_done, chunks):
        mamba_out = outputs(chunk, mamba_out)
    return (mamba_out, result)


def solution(mesh):
    rows = P(("groups", "seq"), ("tp", "dp"))
    shared = P(("groups", "seq"), "tp")
    heads = P(("tp", "dp"))
    cached = P(("groups", "dp"), "tp")
    return jax.shard_map(
        local,
        mesh=mesh,
        in_specs=(
            rows, rows, shared, shared, rows, heads, heads, heads, heads,
            P(("groups", "tp", "dp"), None, None), rows, shared, shared, cached, cached,
            P("groups"), P("groups"),
        ),
        out_specs=(rows, rows),
        check_vma=False,
    )
```
